32 devices in a mesh: dp: 4 (over z), ctx: 8 (over y, x, core).
Axes of the slice: x: 2, y: 2, z: 4, core: 2. Of those that a mesh axis runs over, the one named last changes fastest.
Arguments:
- hidden: bfloat16 [8192, 1536], P(('dp', 'ctx')), may hold values from -6 to 6
- gain_attn: bfloat16 [1536], P(('dp', 'ctx')), may hold values from 0.5 to 1.5
- w_query: bfloat16 [1536, 1536], P(('dp', 'ctx')), may hold values from -0.625 to 0.625
- w_key: bfloat16 [1536, 512], P(('dp', 'ctx')), may hold values from -0.625 to 0.625
- w_value: bfloat16 [1536, 512], P(('dp', 'ctx')), may hold values from -0.15625 to 0.15625
- w_out: bfloat16 [1536, 1536], P(('dp', 'ctx')), may hold values from -4 to 4
- gain_ffn: bfloat16 [1536], P(('dp', 'ctx')), may hold values from 0.5 to 1.5
- router: bfloat16 [1536, 16], P(('dp', 'ctx')), may hold values from -0.078125 to 0.078125
- routes: int32 [8192, 8], P(('dp', 'ctx')), may hold values from 0 to 15, all different within a row; in each aligned block of 256 rows (0 to 255, 256 to 511, ...) at most 160 rows name the same one
- slot_order: int32 [32, 256], P(('dp', 'ctx')), may hold values from 0 to 255, each once within a row
- w_gate: bfloat16 [16, 1536, 512], P('ctx', 'dp'), may hold values from -0.15625 to 0.15625
- w_up: bfloat16 [16, 1536, 512], P('ctx', 'dp'), may hold values from -0.15625 to 0.15625
- w_down: bfloat16 [16, 1536, 512], P('ctx', 'dp'), may hold values from -6 to 6
- grad_out: bfloat16 [8192, 1536], P(('dp', 'ctx')), may hold values from -6 to 6
Outputs:
- output: bfloat16 [8192, 1536], P(('dp', 'ctx'))
- grad_hidden: float32 [8192, 1536], P(('dp', 'ctx'))
- grad_gain_attn: float32 [1536], P(('dp', 'ctx'))
- grad_query: float32 [1536, 1536], P(('dp', 'ctx'))
- grad_key: float32 [1536, 512], P(('dp', 'ctx'))
- grad_value: float32 [1536, 512], P(('dp', 'ctx'))
- grad_out_proj: float32 [1536, 1536], P(('dp', 'ctx'))
- grad_gain_ffn: float32 [1536], P(('dp', 'ctx'))
- grad_router: float32 [1536, 16], P(('dp', 'ctx'))
- grad_gate: float32 [16, 1536, 512], P('ctx', 'dp')
- grad_up: float32 [16, 1536, 512], P('ctx', 'dp')
- grad_down: float32 [16, 1536, 512], P('ctx', 'dp')
The draws below stay inside these ranges and needn't reach their ends.
Inputs may be any that keep to these rules, and one draw needn't show every extreme that they name: `routes`: each row names 8 different experts. Among the 256 rows of one device (aligned blocks) no expert is named by more than 160 rows, a bound that some block reaches. `slot_order`: each row is a permutation of 0 to 255.
All inputs are finite; a program needn't handle non-finite values.
Results may differ from the reference program's by a relative error of at most 0.025.
Values may be sent and summed in bfloat16 or wider, within the bound.
No kernel may reach another device: no remote copies, remote signals or barrier semaphores. Data moves between devices by JAX's collectives and lax.ppermute only.
A program may use at most 192 MiB of HBM per device.

```python
import math
import jax
import jax.numpy as jnp
import numpy as np
from jax import lax

D = 1536
H = 24
KV = 8
HD = 64
FF = 512
TOP = 8
TOK_DEV = 256
TOKENS = 8192
EXPERTS = 16
CAP = 1024
MOST = 160
N_DP = 4
N_CTX = 8


def raised(values, key, source, target, blocks, factor):
    def block_of(dim):
        return (jnp.arange(values.shape[dim]) // (values.shape[dim] // blocks)).reshape((-1,) + (1,) * (values.ndim - 1 - dim))

    one_side = jax.random.permutation(key, blocks)[block_of(target)]
    second = (block_of(target) + blocks // 2) % blocks
    return jnp.where((block_of(source) == one_side) | (block_of(source) == second), factor * values, values)


def block_scale(rng, dims, cuts, low, largest):
    def one(axis_at, shards_of):
        heights = jax.random.uniform(jax.random.fold_in(jax.random.fold_in(rng, 6), axis_at), (shards_of,), jnp.float32, low / len(cuts), largest / len(cuts))
        return jnp.repeat(jnp.exp(heights), dims[axis_at] // shards_of).reshape((-1,) + (1,) * (len(dims) - axis_at - 1))

    factor_of = one(*cuts[0])
    for cut in cuts[1:]:
        factor_of = factor_of * one(*cut)
    return factor_of


def deal_out(stream_key, own, number, rows, count, top, bound, skew):
    sequence = jax.random.permutation(stream_key, count)
    packed, common = portions_of(count, rows * top, bound, skew, True), portions_of(count, rows * top, bound, skew, False)
    places = jnp.arange(count)

    def named(lengths, offset_by):
        used = int((lengths > 0).sum())
        fixed = max(1, used // 4)
        passed = fixed + (places - fixed + offset_by * (used - fixed)) % max(1, count - fixed)
        return jnp.zeros((count,), jnp.int32).at[sequence[jnp.where(places < fixed, places, passed)]].set(jnp.asarray(lengths, jnp.int32))

    lengths = jnp.where(number % 4 == 0, named(packed, number // 4), named(common, number - number // 4 - 1))
    mixed = jax.random.permutation(jax.random.fold_in(own, 3), count)
    source_of, sink = mixed[0:count // 2 * 2:2], mixed[1:count // 2 * 2:2]
    slack = jnp.minimum(lengths[source_of] - 1, bound - lengths[sink]) // 2
    slack = jnp.where((source_of == sequence[0]) | (sink == sequence[0]) | (lengths[sink] == 0), 0, jnp.maximum(slack, 0))
    passed = jax.random.randint(jax.random.fold_in(own, 4), (count // 2,), 0, 1 << 20) % (slack + 1)
    lengths = lengths.at[source_of].add(-passed).at[sink].add(passed)
    labels = jnp.searchsorted(jnp.cumsum(lengths), jnp.arange(rows * top), side="right").astype(jnp.int32)
    grid = labels.reshape(top, rows).T
    grid = grid[jax.random.permutation(jax.random.fold_in(own, 1), rows)]
    offset_by = jax.random.randint(jax.random.fold_in(own, 2), (rows, 1), 0, top)
    return jnp.take_along_axis(grid, (jnp.arange(top)[None, :] + offset_by) % top, axis=1)


def portions_of(number_of, total, most, slope, full):
    loads = [(1 << 20) // math.isqrt(grade ** slope) + 1 for grade in range(1, number_of + 1)]
    largest = most if full else min(most, max(-(-total // number_of), total * loads[0] // sum(loads)))
    least = 1 if total - largest >= number_of - 1 else 0
    given, spare = [largest] + [least] * (number_of - 1), total - largest - least * (number_of - 1)
    while spare > 0:
        candidates = [i for i in range(1, number_of) if given[i] < largest] or [i for i in range(1, number_of) if given[i] < most]
        whole, remaining = sum([loads[i] for i in candidates]), spare
        for i in candidates:
            more = min(most - given[i], max(1, remaining * loads[i] // whole), spare)
            given[i] = given[i] + more
            spare = spare - more
    return np.array(given)


def noise(stream_key, shape, spread, bound, cuts=(), kind=jnp.bfloat16):
    level = block_scale(stream_key, shape, cuts, -0.22, 0.18) if cuts else 1.0
    values = jax.random.normal(stream_key, shape, jnp.float32) * spread * level
    return jnp.minimum(jnp.maximum(values, -bound), bound).astype(kind)


def heavy_noise(rng, dims, scale, most, cuts, heavy, kind=jnp.bfloat16):
    values = scale * jax.random.normal(rng, dims, jnp.float32)
    if cuts:
        values = values * block_scale(rng, dims, cuts, -0.22, 0.18)
    return jnp.clip(raised(values, jax.random.fold_in(rng, 3), *heavy), -most, most).astype(kind)


def setup_inputs(seed: int = 0) -> dict:
    arg_keys = jax.random.split(jax.random.key(seed), 15)
    hidden = heavy_noise(arg_keys[0], (TOKENS, D), 1.0, 6.0, ((0, 32),), (0, 1, 32, 2.75))
    gain_attn = jnp.clip(1.0 + 0.1 * jax.random.normal(arg_keys[1], (D,), jnp.float32), 0.5, 1.5).astype(jnp.bfloat16)
    w_query = noise(arg_keys[2], (D, H * HD), (D // 16) ** -0.5, 0.625, ((0, 32),))
    w_key = noise(arg_keys[3], (D, KV * HD), (D // 16) ** -0.5, 0.625, ((0, 32),))
    w_value = noise(arg_keys[4], (D, KV * HD), D ** -0.5, 0.15625, ((0, 32),))
    w_out = noise(arg_keys[5], (H * HD, D), (max(1, H * HD // 640)) ** -0.5, 4.0, ((0, 32),))
    gain_ffn = jnp.clip(1.0 + 0.1 * jax.random.normal(arg_keys[6], (D,), jnp.float32), 0.5, 1.5).astype(jnp.bfloat16)
    router = noise(arg_keys[7], (D, EXPERTS), (4 * D) ** -0.5, 0.078125, ((0, 32),))
    routes_keys = jax.random.split(jax.random.fold_in(arg_keys[8], 1), TOKENS // TOK_DEV)
    routes_turns = jax.random.permutation(jax.random.fold_in(arg_keys[8], 3), TOKENS // TOK_DEV)
    routes = jax.vmap(lambda own, number: deal_out(jax.random.fold_in(arg_keys[8], 2), own, number, TOK_DEV, EXPERTS, TOP, MOST, 2))(routes_keys, routes_turns).reshape((TOKENS, TOP))
    slot_order = jax.vmap(lambda own: jax.random.permutation(own, TOK_DEV))(jax.random.split(arg_keys[9], (TOKENS // TOK_DEV))).reshape((TOKENS // TOK_DEV, TOK_DEV)).astype(jnp.int32)
    w_gate = noise(arg_keys[10], (EXPERTS, D, FF), D ** -0.5, 0.15625, ((0, 8), (1, 4)))
    w_up = noise(arg_keys[11], (EXPERTS, D, FF), D ** -0.5, 0.15625, ((0, 8), (1, 4)))
    w_down = noise(arg_keys[12], (EXPERTS, D, FF), (max(1, FF // 320)) ** -0.5, 6.0, ((0, 8), (1, 4)))
    grad_out = noise(arg_keys[13], (TOKENS, D), 1.0, 6.0, ((0, 32),))
    return {"hidden": hidden, "gain_attn": gain_attn, "w_query": w_query, "w_key": w_key, "w_value": w_value, "w_out": w_out, "gain_ffn": gain_ffn, "router": router, "routes": routes, "slot_order": slot_order, "w_gate": w_gate, "w_up": w_up, "w_down": w_down, "grad_out": grad_out}


EPS = 1e-06
NEG_FILL = -1e+30
SCORE_SCALE = 0.015625
RESIDUAL_SCALE = 0.22
HIGH = lax.Precision.HIGHEST

@jax.custom_vjp
def low(v):
    return lax.optimization_barrier(v.astype(jnp.bfloat16)).astype(jnp.float32)

@jax.custom_vjp
def low_back(v):
    return v

def low_keep(v):
    return (low(v), None)

def low_pass(kept, grad):
    return (grad,)

def back_keep(v):
    return (v, None)

def back_low(kept, grad):
    return (low(grad),)
low.defvjp(low_keep, low_pass)
low_back.defvjp(back_keep, back_low)

def matmul_high(left, right):
    return jnp.dot(left, right, precision=HIGH)

def rope_tables(positions, head_dim):
    half_dim = head_dim // 2
    exponents = jnp.arange(half_dim, dtype=jnp.float32) * (2.0 / head_dim)
    inverse = jnp.power(10000.0, -exponents)
    angles = positions.astype(jnp.float32)[:, None] * inverse[None, :]
    return (jnp.cos(angles), jnp.sin(angles))

def rotate(values_in, cos_table, sin_table):
    row_total = values_in.shape[0]
    split = values_in.reshape(row_total, -1, 2, cos_table.shape[1])
    first_half = split[:, :, 0, :]
    second_half = split[:, :, 1, :]
    cos_wide = cos_table[:, None, :]
    sin_wide = sin_table[:, None, :]
    turned = jnp.stack([first_half * cos_wide - second_half * sin_wide, second_half * cos_wide + first_half * sin_wide], axis=2)
    return turned.reshape(row_total, -1)

def slot_plan(route_seq, order_seq):
    seq_len = route_seq.shape[0]
    block_of = jnp.arange(seq_len, dtype=jnp.int32) // TOK_DEV
    priority = block_of * TOK_DEV + order_seq.reshape(-1).astype(jnp.int32)
    by_priority = jnp.argsort(priority)
    chosen = (route_seq[:, :, None] == jnp.arange(EXPERTS, dtype=jnp.int32)[None, None, :]).astype(jnp.int32)
    per_token = lax.optimization_barrier(jnp.sum(chosen, axis=1))
    ordered = per_token[by_priority]
    ahead = jnp.cumsum(ordered, axis=0) - ordered
    slot_all = jnp.zeros_like(per_token).at[by_priority].set(ahead)
    slot_seq = lax.optimization_barrier(jnp.sum(chosen * slot_all[:, None, :], axis=-1))
    kept_mask = slot_seq < CAP
    dest = jnp.where(kept_mask, route_seq * CAP + slot_seq, EXPERTS * CAP).reshape(-1).astype(jnp.int32)
    pair_ids = jnp.arange(seq_len * TOP, dtype=jnp.int32)
    slot_pair = jnp.zeros((EXPERTS * CAP,), jnp.int32).at[dest].set(pair_ids, mode='drop')
    slot_used = jnp.zeros((EXPERTS * CAP,), jnp.float32).at[dest].set(1.0, mode='drop')
    gather_index = jnp.minimum(dest, EXPERTS * CAP - 1).reshape(seq_len, TOP)
    return (slot_pair // TOP, slot_used, gather_index, kept_mask.astype(jnp.float32))

def layer(params, hidden_seq, route_seq, order_seq):
    gain_attn, w_query, w_key, w_value, w_out, gain_ffn, router, w_gate, w_up, w_down = params
    seq_len = hidden_seq.shape[0]
    group_size = H // KV
    normed_a = hidden_seq * lax.rsqrt(lax.optimization_barrier(jnp.mean(hidden_seq * hidden_seq, axis=-1, keepdims=True)) + EPS)
    attn_in = low(normed_a * gain_attn)
    positions = jnp.arange(seq_len, dtype=jnp.int32)
    cos_table, sin_table = rope_tables(positions, HD)
    queries = low(rotate(low_back(matmul_high(attn_in, w_query)), cos_table, sin_table))
    keys_all = low(rotate(low_back(matmul_high(attn_in, w_key)), cos_table, sin_table))
    values_all = low(low_back(matmul_high(attn_in, w_value)))
    block_rows = min(512, seq_len)
    block_count = seq_len // block_rows
    query_blocks = queries.reshape(block_count, block_rows, KV, group_size, HD)
    block_starts = jnp.arange(block_count, dtype=jnp.int32) * block_rows
    key_heads = keys_all.reshape(seq_len, KV, HD)
    value_heads = values_all.reshape(seq_len, KV, HD)

    def one_block(block_inputs):
        query_block, first_row = block_inputs
        scores = jnp.einsum('qcgd,kcd->cgqk', query_block, key_heads, precision=HIGH)
        scores = low_back(scores * SCORE_SCALE)
        query_pos = first_row + jnp.arange(block_rows, dtype=jnp.int32)
        allowed = jnp.arange(seq_len, dtype=jnp.int32)[None, :] <= query_pos[:, None]
        scores = jnp.where(allowed, scores, NEG_FILL)
        probs = low(jax.nn.softmax(scores, axis=-1))
        return jnp.einsum('cgqk,kcd->qcgd', probs, value_heads, precision=HIGH)
    attended = lax.map(jax.checkpoint(one_block), (query_blocks, block_starts))
    attn = low(low_back(attended.reshape(seq_len, H * HD)))
    resid = hidden_seq + RESIDUAL_SCALE * low_back(matmul_high(attn, w_out))
    normed_f = resid * lax.rsqrt(lax.optimization_barrier(jnp.mean(resid * resid, axis=-1, keepdims=True)) + EPS)
    moe_in = low(normed_f * gain_ffn)
    logits = low_back(matmul_high(moe_in, router))
    route_logit = jnp.take_along_axis(logits, route_seq, axis=1)
    gates = jax.nn.softmax(route_logit, axis=-1)
    slot_token, slot_used, gather_index, kept = slot_plan(route_seq, order_seq)
    expert_in = low_back(moe_in[slot_token] * slot_used[:, None]).reshape(EXPERTS, CAP, D)
    gate_pre = low_back(jnp.einsum('ecd,edf->ecf', expert_in, w_gate, precision=HIGH))
    up_pre = low_back(jnp.einsum('ecd,edf->ecf', expert_in, w_up, precision=HIGH))
    inner = low(jax.nn.silu(gate_pre) * up_pre)
    expert_out = low(low_back(jnp.einsum('ecf,edf->ecd', inner, w_down, precision=HIGH)))
    routed = expert_out.reshape(EXPERTS * CAP, D)[gather_index]
    mixed = lax.optimization_barrier(jnp.sum((kept * gates)[:, :, None] * routed, axis=1))
    return resid + RESIDUAL_SCALE * mixed

def add_up(first_tree, second_tree):
    return jax.tree.map(lambda first_leaf, second_leaf: first_leaf + second_leaf, first_tree, second_tree)

def reference(hidden, gain_attn, w_query, w_key, w_value, w_out, gain_ffn, router, routes, slot_order, w_gate, w_up, w_down, grad_out):
    params = tuple((member.astype(jnp.float32) for member in (gain_attn, w_query, w_key, w_value, w_out, gain_ffn, router, w_gate, w_up, w_down)))
    seq_len = TOK_DEV * N_CTX
    hidden_seqs = hidden.astype(jnp.float32).reshape(N_DP, seq_len, D)
    route_seqs = routes.reshape(N_DP, seq_len, TOP)
    order_seqs = slot_order.reshape(N_DP, N_CTX, TOK_DEV)
    cotangents = grad_out.astype(jnp.float32).reshape(N_DP, seq_len, D)

    def one_sequence(totals, seq_inputs):
        hidden_seq, route_seq, order_seq, cotangent = seq_inputs

        def forward(param_tuple, hidden_in):
            return layer(param_tuple, hidden_in, route_seq, order_seq)
        result, pullback = jax.vjp(forward, params, hidden_seq)
        param_grads, hidden_grad = pullback(cotangent)
        return (add_up(totals, param_grads), (result.astype(jnp.bfloat16), hidden_grad))
    start_totals = jax.tree.map(jnp.zeros_like, params)
    totals, (results, hidden_grads) = lax.scan(one_sequence, start_totals, (hidden_seqs, route_seqs, order_seqs, cotangents))
    return (results.reshape(N_DP * seq_len, D), hidden_grads.reshape(N_DP * seq_len, D), totals[0], totals[1], totals[2], totals[3], totals[4], totals[5], totals[6], totals[7], totals[8], totals[9])
```

```python
import functools

import jax
import jax.numpy as jnp
from jax import lax
from jax.experimental import pallas as pl
from jax.experimental.pallas import tpu as pltpu
from jax.sharding import PartitionSpec as P

H = 24
KV = 8
HD = 64
TOP = 8
CAP = 1024

EPS = 1e-06
NEG_FILL = -1e30
SCORE_SCALE = 0.015625
RESIDUAL_SCALE = 0.22

GROUP = H // KV
HALF = HD // 2
QW = GROUP * HD
QKV = QW + 2 * HD
LOW = 64
EXTRA = 128

f32 = jnp.float32
bf16 = jnp.bfloat16
i32 = jnp.int32
VMEM_LIMIT = 58 * 1024 * 1024


def dot_nn(a, b):
    return lax.dot_general(a, b, (((1,), (0,)), ((), ())), preferred_element_type=f32)


def dot_nt(a, b):
    return lax.dot_general(a, b, (((1,), (1,)), ((), ())), preferred_element_type=f32)


def dot_tn(a, b):
    return lax.dot_general(a, b, (((0,), (0,)), ((), ())), preferred_element_type=f32)


def params(limit=VMEM_LIMIT):
    return pltpu.CompilerParams(dimension_semantics=("arbitrary",), vmem_limit_bytes=limit)


def lane_orders(count):
    bits = []
    bit = 2
    while bit < count:
        bits.append(bit)
        bit *= 2
    return (bits[::-1] + [1], bits + [1])


def slots_of(order):
    slots = [0]
    for bit in order:
        slots = slots + [s ^ bit for s in slots]
    return slots


def swap(value, bit, count):
    return lax.ppermute(value, "ctx", [(i, i ^ bit) for i in range(count)])


def plane_gather(first, second, count):
    order_a, order_b = lane_orders(count)
    a, b = (first[None], second[None])
    for bit_a, bit_b in zip(order_a, order_b):
        got_a, got_b = (swap(a, bit_a, count), swap(b, bit_b, count))
        a = jnp.concatenate([a, got_a], axis=0)
        b = jnp.concatenate([b, got_b], axis=0)
    return a, b


def plane_scatter(a, b, count):
    order_a, order_b = lane_orders(count)
    for bit_a, bit_b in zip(order_a[::-1], order_b[::-1]):
        half = a.shape[0] // 2
        got_a, got_b = (swap(a[half:], bit_a, count), swap(b[half:], bit_b, count))
        a = a[:half].astype(f32) + got_a.astype(f32)
        b = b[:half].astype(f32) + got_b.astype(f32)
        if half > 1:
            a, b = (a.astype(bf16), b.astype(bf16))
    return a[0], b[0]


def qkv_kernel(slot_ref, xa, xb, gain, wt, cos, sin, ain_o, qt_o, k_o, kt_o, v_o, vt_o):
    x = jnp.concatenate([xa[0], xb[0]], axis=0).astype(f32)
    inv = lax.rsqrt(jnp.mean(x * x, axis=-1, keepdims=True) + EPS)
    a = (x * inv * gain[...]).astype(bf16)
    ain_o[0] = a
    y = dot_nt(wt[...], a)
    c, s = (cos[0], sin[0])

    def turn(rows):
        lo, hi = (rows[:HALF], rows[HALF:])
        return jnp.concatenate([lo * c - hi * s, hi * c + lo * s], axis=0)

    for h in range(GROUP):
        q = turn(y[h * HD : (h + 1) * HD]).astype(bf16).astype(f32) * SCORE_SCALE
        qt_o[0, h * HD : (h + 1) * HD, :] = q.astype(bf16)
    k = turn(y[QW : QW + HD])
    kt_o[0] = k.astype(bf16)
    k_o[0] = k.T.astype(bf16)
    v = y[QW + HD :]
    vt_o[0] = v.astype(bf16)
    v_o[0] = v.T.astype(bf16)


def heads_wide(rows):
    return jnp.concatenate([rows[h * HD : (h + 1) * HD] for h in range(GROUP)], axis=1)


def causal(shape, width):
    key = lax.broadcasted_iota(i32, shape, 0)
    query = lax.broadcasted_iota(i32, shape, 1)
    for _ in range(GROUP - 1):
        query = jnp.where(query >= width, query - width, query)
    return key <= query


def attn_fwd_kernel(qt, k, vt, of_o, ob_o, lse_o):
    a = pl.program_id(0)
    tok = qt.shape[2]
    q = heads_wide(qt[0])
    s = dot_nn(k[a], q)
    s = jnp.where(causal(s.shape, tok), s, NEG_FILL)
    m = jnp.max(s, axis=0, keepdims=True)
    p = jnp.exp(s - m)
    l = jnp.sum(p, axis=0, keepdims=True)
    o = dot_nn(vt[a], p.astype(bf16))

    def step(b, carry):
        m, l, o = carry
        s = dot_nn(k[b], q)
        new = jnp.maximum(m, jnp.max(s, axis=0, keepdims=True))
        p = jnp.exp(s - new)
        back = jnp.exp(m - new)
        l = l * back + jnp.sum(p, axis=0, keepdims=True)
        o = o * back + dot_nn(vt[b], p.astype(bf16))
        return (new, l, o)

    m, l, o = lax.fori_loop(0, a, step, (m, l, o))
    o = o / l
    lse_o[0] = m + jnp.log(l)
    for h in range(GROUP):
        part = o[:, h * tok : (h + 1) * tok]
        of_o[0, h * HD : (h + 1) * HD, :] = part
        ob_o[0, h * HD : (h + 1) * HD, :] = part.astype(bf16)


def attn_bwd_kernel(qt, dot_, of, lse, k, kt, v, cos, sin, dq_o, dk_o, dv_o, dk_s, dv_s):
    a = pl.program_id(0)
    tok = qt.shape[2]
    count = k.shape[0]
    q = heads_wide(qt[0])
    do = heads_wide(dot_[0])
    delta = jnp.sum(do.astype(f32) * heads_wide(of[0]), axis=0, keepdims=True)
    total = lse[0]

    def pair(b, mask):
        s = dot_nn(k[b], q)
        p = jnp.exp(s - total)
        if mask:
            p = jnp.where(causal(s.shape, tok), p, 0.0)
        dp = dot_nn(v[b], do)
        ds = (p * (dp - delta)).astype(bf16)
        return dot_nt(ds, q), dot_nt(p.astype(bf16), do), dot_nn(kt[b], ds)

    dk, dv, dq = pair(a, True)
    dk_s[a] = dk
    dv_s[a] = dv

    def step(b, dq):
        dk, dv, more = pair(b, False)
        dk_s[b] += dk
        dv_s[b] += dv
        return dq + more

    dq = lax.fori_loop(0, a, step, dq) * SCORE_SCALE

    def back(rows, c, s):
        lo, hi = (rows[:HALF], rows[HALF:])
        return jnp.concatenate([lo * c + hi * s, hi * c - lo * s], axis=0)

    for h in range(GROUP):
        dq_o[0, h * HD : (h + 1) * HD, :] = back(
            dq[:, h * tok : (h + 1) * tok], cos[a], sin[a]
        ).astype(bf16)

    @pl.when(a == count - 1)
    def _():
        @pl.loop(0, count)
        def _(b):
            dk_o[b] = back(dk_s[b].T, cos[b], sin[b]).astype(bf16)
            dv_o[b] = dv_s[b].T.astype(bf16)


def qkv_bwd_kernel(share, slot_ref, dq, dk, dv, ain, xa, xb, wt, da_o, db_o, gw_o, gg_o, acc, gacc):
    a = pl.program_id(0)
    d = jnp.concatenate([dq[0], dk[0], dv[0]], axis=0)
    part = dot_tn(d, wt[...]) * share
    x = jnp.concatenate([xa[0], xb[0]], axis=0).astype(f32)
    inv = lax.rsqrt(jnp.mean(x * x, axis=-1, keepdims=True) + EPS)
    half = xa.shape[1]
    da_o[0] = part[:half].astype(bf16)
    db_o[0] = part[half:].astype(bf16)

    @pl.when(a == 0)
    def _():
        acc[...] = jnp.zeros_like(acc)
        gacc[...] = jnp.zeros_like(gacc)

    acc[...] += dot_nn(d, ain[0])
    gacc[...] += jnp.sum(part * (x * inv), axis=0, keepdims=True)

    @pl.when(a == pl.num_programs(0) - 1)
    def _():
        width = gw_o.shape[2]
        for z in range(gw_o.shape[0]):
            gw_o[z] = acc[:, z * width : (z + 1) * width].astype(bf16)
        gg_o[...] = gacc[...]


def moe_kernel(second, which, *refs):
    xa, xb, ya, yb, router, code, weights = refs[:7]
    refs = refs[7:]
    if second:
        din_pa, din_pb, out_pa, out_pb = refs[:4]
        refs = refs[4:]
    din_a, din_b, out_a, out_b, grad_o, acc_g, acc_u, acc_d = refs
    i = pl.program_id(0)
    expert = which[0]
    x = jnp.concatenate([xa[0], xb[0]], axis=0)
    y = jnp.concatenate([ya[0], yb[0]], axis=0)
    shards, _, depth, ff = weights.shape
    width = shards * depth
    w_gate = weights[:, 0].reshape(width, ff)
    w_up = weights[:, 1].reshape(width, ff)
    w_down = weights[:, 2].reshape(width, ff)

    logits = dot_nt(x, router[...])
    named = code[0] > 0.5
    logits = jnp.where(named, logits, NEG_FILL)
    top = jnp.max(logits, axis=-1, keepdims=True)
    raised = jnp.where(named, jnp.exp(logits - top), 0.0)
    gates = raised / jnp.sum(raised, axis=-1, keepdims=True)
    mine = (lax.broadcasted_iota(i32, gates.shape, 1) == expert) & (code[0] > 1.5)
    weight = RESIDUAL_SCALE * jnp.sum(jnp.where(mine, gates, 0.0), axis=-1, keepdims=True)
    kept = RESIDUAL_SCALE * jnp.sum(jnp.where(mine, 1.0, 0.0), axis=-1, keepdims=True)

    gate_pre = dot_nn(x, w_gate)
    up_pre = dot_nn(x, w_up)
    back = dot_nn(y, w_down)
    sig = jax.nn.sigmoid(gate_pre)
    act = gate_pre * sig
    inner = act * up_pre
    gate_grad = kept * jnp.sum(inner * back, axis=-1, keepdims=True)
    inner_w = (inner * weight).astype(bf16)
    d_inner = back * weight
    d_gate = (d_inner * up_pre * sig * (1.0 + gate_pre * (1.0 - sig))).astype(bf16)
    d_up = (d_inner * act).astype(bf16)

    out = dot_nt(inner_w, w_down)
    din = dot_nt(d_gate, w_gate) + dot_nt(d_up, w_up)
    high = gate_grad.astype(bf16)
    low = (gate_grad - high.astype(f32)).astype(bf16)
    lane = lax.broadcasted_iota(i32, (x.shape[0], EXTRA), 1)
    side = jnp.where(lane == expert, high.astype(f32), 0.0) + jnp.where(
        lane == expert + LOW, low.astype(f32), 0.0
    )
    half = xa.shape[1]
    for part, din_o, out_o in ((slice(0, half), din_a, out_a), (slice(half, None), din_b, out_b)):
        d, o, s = (din[part], out[part], side[part])
        if second:
            din_p, out_p = (din_pa, out_pa) if din_o is din_a else (din_pb, out_pb)
            d = d + din_p[0, :, :width].astype(f32)
            s = s + din_p[0, :, width:].astype(f32)
            o = o + out_p[0].astype(f32)
        din_o[0, :, :width] = d.astype(bf16)
        din_o[0, :, width:] = s.astype(bf16)
        out_o[0] = o.astype(bf16)

    @pl.when(i == 0)
    def _():
        acc_g[...] = jnp.zeros_like(acc_g)
        acc_u[...] = jnp.zeros_like(acc_u)
        acc_d[...] = jnp.zeros_like(acc_d)

    acc_g[...] += dot_tn(x, d_gate)
    acc_u[...] += dot_tn(x, d_up)
    acc_d[...] += dot_tn(y, inner_w)

    @pl.when(i == pl.num_programs(0) - 1)
    def _():
        for z in range(shards):
            rows = slice(z * depth, (z + 1) * depth)
            grad_o[z, 0] = acc_g[rows, :].astype(bf16)
            grad_o[z, 1] = acc_u[rows, :].astype(bf16)
            grad_o[z, 2] = acc_d[rows, :].astype(bf16)


def place_kernel(slot_ref, a, b, out):
    half = a.shape[1]
    for z in range(half):
        out[z, 0] = a[0, z]
        out[half + z, 0] = b[0, z]


def whole(shape):
    zeros = (0,) * len(shape)
    return pl.BlockSpec(shape, lambda i, *refs: zeros)


def at_step(shape):
    zeros = (0,) * (len(shape) - 1)
    return pl.BlockSpec(shape, lambda i, *refs: (i,) + zeros)


def at_slot(shape, lane):
    zeros = (0,) * (len(shape) - 1)
    return pl.BlockSpec(shape, lambda i, slots: (slots[lane, i],) + zeros)


def shape_of(*dims, dtype=bf16):
    return jax.ShapeDtypeStruct(dims, dtype)


def shards(
    hidden,
    gain_attn,
    w_query,
    w_key,
    w_value,
    w_out,
    gain_ffn,
    router,
    routes,
    slot_order,
    w_gate,
    w_up,
    w_down,
    grad_out,
):
    tok, width = hidden.shape
    n = lax.axis_size("ctx")
    dp = lax.axis_size("dp")
    me = lax.axis_index("ctx")
    copies = n // KV
    rp = w_query.shape[0]
    slab = rp * n
    experts = router.shape[1]
    half = tok // 2
    ff = w_gate.shape[2]
    depth = w_gate.shape[1]
    order_a, order_b = lane_orders(n)
    slots_a, slots_b = (slots_of(order_a), slots_of(order_b))
    absolute = jnp.arange(n, dtype=i32)
    inverse_a = jnp.zeros((n,), i32).at[jnp.array(slots_a)].set(absolute)
    inverse_b = jnp.zeros((n,), i32).at[jnp.array(slots_b)].set(absolute)
    slot_at = jnp.stack([inverse_a[absolute ^ me], inverse_b[absolute ^ me]])
    block_a = jnp.array(slots_a, i32) ^ me
    block_b = jnp.array(slots_b, i32) ^ me

    by_head = jnp.concatenate(
        [
            w_query.reshape(rp, KV, QW),
            w_key.reshape(rp, KV, HD),
            w_value.reshape(rp, KV, HD),
        ],
        axis=2,
    ).transpose(1, 0, 2)
    extras = jnp.concatenate([gain_attn[:, None], gain_ffn[:, None], router], axis=1)
    send = jnp.concatenate(
        [
            jnp.repeat(by_head, copies, axis=0),
            jnp.broadcast_to(extras[None], (n,) + extras.shape),
        ],
        axis=2,
    )
    took = lax.all_to_all(send, "ctx", split_axis=0, concat_axis=0, tiled=True)
    side = took.shape[2]
    pad = -(side + rp * dp) % 16
    pack = jnp.concatenate(
        [took.reshape(slab, side).T, w_out.reshape(rp * dp, slab)], axis=0
    )
    packs = lax.all_gather(pack, "dp", axis=0)
    wt = packs[:, :QKV].transpose(1, 0, 2).reshape(QKV, width)
    gains = packs[:, QKV : QKV + 2].transpose(1, 0, 2).reshape(2, width).astype(f32)
    router_t = packs[:, QKV + 2 : side].transpose(1, 0, 2).reshape(experts, width)
    gain_a, gain_f = (gains[0:1], gains[1:2])
    out_rows = packs[:, side:].reshape(dp, rp, width)

    expert_w = [
        lax.all_gather(jnp.stack([w_gate[e], w_up[e], w_down[e]]), "dp", axis=0)
        for e in range(w_gate.shape[0])
    ]

    xa, xb = plane_gather(hidden[:half], hidden[half:], n)
    ya, yb = plane_gather(grad_out[:half], grad_out[half:], n)
    oa, ob = plane_gather(out_rows[: dp // 2], out_rows[dp // 2 :], n)

    table = lax.all_gather(
        jnp.concatenate([routes, slot_order.reshape(tok, 1)], axis=1), "ctx", axis=0
    )
    names = jnp.arange(experts, dtype=i32)
    named = jnp.sum(
        (table[:, :, :TOP, None] == names).astype(f32), axis=2
    )
    ranks = table[:, :, TOP]
    before = (ranks[:, None, :] < ranks[:, :, None]).astype(bf16)
    local = jnp.einsum("btu,bue->bte", before, named.astype(bf16), preferred_element_type=f32)
    load = jnp.sum(named, axis=1)
    earlier = jnp.cumsum(load, axis=0) - load
    slot = local + earlier[:, None, :]
    code_all = named * (1.0 + (slot < CAP).astype(f32))
    code = jnp.concatenate([code_all[block_a, :half], code_all[block_b, half:]], axis=1)
    code_mine = code_all[me]

    exponents = jnp.arange(HALF, dtype=f32) * (2.0 / HD)
    inverse_freq = jnp.power(10000.0, -exponents)
    positions = jnp.arange(n * tok, dtype=f32).reshape(n, 1, tok)
    angles = positions * inverse_freq[None, :, None]
    cos, sin = (jnp.cos(angles), jnp.sin(angles))

    grid_spec = pltpu.PrefetchScalarGridSpec

    ain, qt, k, kt, v, vt = pl.pallas_call(
        qkv_kernel,
        grid_spec=grid_spec(
            num_scalar_prefetch=1,
            grid=(n,),
            in_specs=[
                at_slot((1, half, width), 0),
                at_slot((1, half, width), 1),
                whole((1, width)),
                whole((QKV, width)),
                at_step((1, HALF, tok)),
                at_step((1, HALF, tok)),
            ],
            out_specs=[
                at_step((1, tok, width)),
                at_step((1, QW, tok)),
                at_step((1, tok, HD)),
                at_step((1, HD, tok)),
                at_step((1, tok, HD)),
                at_step((1, HD, tok)),
            ],
        ),
        out_shape=[
            shape_of(n, tok, width),
            shape_of(n, QW, tok),
            shape_of(n, tok, HD),
            shape_of(n, HD, tok),
            shape_of(n, tok, HD),
            shape_of(n, HD, tok),
        ],
        compiler_params=params(32 * 1024 * 1024),
        name="qkv",
    )(slot_at, xa, xb, gain_a, wt, cos, sin)

    of, attn_t, lse = pl.pallas_call(
        attn_fwd_kernel,
        grid=(n,),
        in_specs=[at_step((1, QW, tok)), whole((n, tok, HD)), whole((n, HD, tok))],
        out_specs=[
            at_step((1, QW, tok)),
            at_step((1, QW, tok)),
            at_step((1, 1, GROUP * tok)),
        ],
        out_shape=[
            shape_of(n, QW, tok, dtype=f32),
            shape_of(n, QW, tok),
            shape_of(n, 1, GROUP * tok, dtype=f32),
        ],
        compiler_params=params(32 * 1024 * 1024),
        name="attn_fwd",
    )(qt, k, vt)

    attn_b = lax.all_to_all(attn_t, "ctx", split_axis=0, concat_axis=0, tiled=True)
    attn_b = attn_b[::copies].reshape(KV * QW, tok)

    w_out_all = pl.pallas_call(
        place_kernel,
        grid_spec=grid_spec(
            num_scalar_prefetch=1,
            grid=(n,),
            in_specs=[
                at_slot((1, dp // 2, rp, width), 0),
                at_slot((1, dp // 2, rp, width), 1),
            ],
            out_specs=pl.BlockSpec((dp, 1, rp, width), lambda i, slots: (0, i, 0, 0)),
        ),
        out_shape=shape_of(dp, n, rp, width),
        compiler_params=params(16 * 1024 * 1024),
        name="place",
    )(slot_at, oa, ob).reshape(KV * QW, width)

    hidden_f = hidden.astype(f32)
    branch = dot_tn(attn_b, w_out_all)
    resid = hidden_f + RESIDUAL_SCALE * branch
    inv_ffn = lax.rsqrt(jnp.mean(resid * resid, axis=-1, keepdims=True) + EPS)
    normed_f = resid * inv_ffn
    moe_in = (normed_f * gain_f).astype(bf16)

    ma, mb = plane_gather(moe_in[:half], moe_in[half:], n)

    side_w = width + EXTRA
    din = None
    expert_grads = []
    for e, gathered in enumerate(expert_w):
        operands = [ma, mb, ya, yb, router_t, code, gathered]
        in_specs = [at_step((1, half, width))] * 4 + [
            whole((experts, width)),
            at_step((1, tok, experts)),
            whole((dp, 3, depth, ff)),
        ]
        if din is not None:
            operands += [din[0], din[1], din[2], din[3]]
            in_specs += [at_step((1, half, side_w))] * 2 + [at_step((1, half, width))] * 2
        *din, grads = pl.pallas_call(
            functools.partial(moe_kernel, din is not None),
            grid_spec=grid_spec(
                num_scalar_prefetch=1,
                grid=(n,),
                in_specs=in_specs,
                out_specs=[at_step((1, half, side_w))] * 2
                + [at_step((1, half, width))] * 2
                + [whole((dp, 3, depth, ff))],
                scratch_shapes=[pltpu.VMEM((width, ff), f32)] * 3,
            ),
            out_shape=[shape_of(n, half, side_w)] * 2
            + [shape_of(n, half, width)] * 2
            + [shape_of(dp, 3, depth, ff)],
            compiler_params=params(),
            name="moe",
        )((me * len(expert_w) + e).reshape(1).astype(i32), *operands)
        expert_grads.append(
            lax.psum_scatter(grads, "dp", scatter_dimension=0, tiled=True)[0].astype(f32)
        )

    back_a, back_b = plane_scatter(din[0], din[1], n)
    back = jnp.concatenate([back_a, back_b], axis=0)
    mix_a, mix_b = plane_scatter(din[2], din[3], n)
    output = (resid + jnp.concatenate([mix_a, mix_b], axis=0)).astype(bf16)

    grad_f = grad_out.astype(f32)
    chosen = code_mine > 0.5
    logits = jnp.where(chosen, dot_nt(moe_in, router_t), NEG_FILL)
    gates = jnp.where(chosen, jax.nn.softmax(logits, axis=-1), 0.0)
    gate_grad = (
        back[:, width : width + experts] + back[:, width + LOW : width + LOW + experts]
    )
    logit_grad = gates * (gate_grad - jnp.sum(gates * gate_grad, axis=-1, keepdims=True))
    dlogits = logit_grad.astype(bf16)
    d_router = dot_tn(dlogits, moe_in)
    d_moe_in = back[:, :width] + dot_nn(dlogits, router_t)
    d_gain_ffn = jnp.sum(d_moe_in * normed_f, axis=0, keepdims=True)
    d_normed_f = d_moe_in * gain_f
    d_resid = grad_f + inv_ffn * (
        d_normed_f - normed_f * jnp.mean(d_normed_f * normed_f, axis=-1, keepdims=True)
    )
    d_branch = (RESIDUAL_SCALE * d_resid).astype(bf16)
    d_attn = dot_nt(w_out_all, d_branch).astype(bf16).reshape(KV, QW, tok)
    d_heads = lax.all_to_all(
        jnp.repeat(d_attn, copies, axis=0), "ctx", split_axis=0, concat_axis=0, tiled=True
    )

    d_wout = dot_nn(attn_b, d_branch).astype(bf16).reshape(dp, n, rp, width)
    wout_a, wout_b = plane_scatter(
        d_wout[: dp // 2].transpose(1, 0, 2, 3)[block_a],
        d_wout[dp // 2 :].transpose(1, 0, 2, 3)[block_b],
        n,
    )
    d_wout = jnp.concatenate([wout_a, wout_b], axis=0).astype(bf16)

    dq, dk, dv = pl.pallas_call(
        attn_bwd_kernel,
        grid=(n,),
        in_specs=[
            at_step((1, QW, tok)),
            at_step((1, QW, tok)),
            at_step((1, QW, tok)),
            at_step((1, 1, GROUP * tok)),
            whole((n, tok, HD)),
            whole((n, HD, tok)),
            whole((n, tok, HD)),
            whole((n, HALF, tok)),
            whole((n, HALF, tok)),
        ],
        out_specs=[at_step((1, QW, tok)), whole((n, HD, tok)), whole((n, HD, tok))],
        out_shape=[shape_of(n, QW, tok), shape_of(n, HD, tok), shape_of(n, HD, tok)],
        scratch_shapes=[pltpu.VMEM((n, tok, HD), f32), pltpu.VMEM((n, tok, HD), f32)],
        compiler_params=params(40 * 1024 * 1024),
        name="attn_bwd",
    )(qt, d_heads, of, lse, k, kt, v, cos, sin)

    da, db, gw, d_gain_attn = pl.pallas_call(
        functools.partial(qkv_bwd_kernel, 1.0 / copies),
        grid_spec=grid_spec(
            num_scalar_prefetch=1,
            grid=(n,),
            in_specs=[
                at_step((1, QW, tok)),
                at_step((1, HD, tok)),
                at_step((1, HD, tok)),
                at_step((1, tok, width)),
                at_slot((1, half, width), 0),
                at_slot((1, half, width), 1),
                whole((QKV, width)),
            ],
            out_specs=[
                at_slot((1, half, width), 0),
                at_slot((1, half, width), 1),
                whole((dp, QKV, slab)),
                whole((1, width)),
            ],
            scratch_shapes=[pltpu.VMEM((QKV, width), f32), pltpu.VMEM((1, width), f32)],
        ),
        out_shape=[
            shape_of(n, half, width),
            shape_of(n, half, width),
            shape_of(dp, QKV, slab),
            shape_of(1, width, dtype=f32),
        ],
        compiler_params=params(40 * 1024 * 1024),
        name="qkv_bwd",
    )(slot_at, dq, dk, dv, ain, xa, xb, wt)

    rest = jnp.concatenate([d_gain_attn, d_gain_ffn, d_router], axis=0).astype(bf16)
    grads = jnp.concatenate(
        [
            gw,
            rest.reshape(2 + experts, dp, slab).transpose(1, 0, 2),
            d_wout.reshape(dp, rp * dp, slab),
            jnp.zeros((dp, pad, slab), bf16),
        ],
        axis=1,
    )
    own = lax.psum_scatter(grads, "dp", scatter_dimension=0, tiled=True)[0]
    given = lax.all_to_all(
        own[:side].T.reshape(n, rp, side), "ctx", split_axis=0, concat_axis=0, tiled=True
    ).astype(f32)
    heads = given[::copies].transpose(1, 0, 2)
    grad_query = heads[:, :, :QW].reshape(rp, KV * QW)
    grad_key = heads[:, :, QW : QW + HD].reshape(rp, KV * HD)
    grad_value = heads[:, :, QW + HD : QKV].reshape(rp, KV * HD)
    sums = jnp.sum(given[:, :, QKV:], axis=0)
    grad_out_proj = own[side : side + rp * dp].reshape(rp, width).astype(f32)

    in_a, in_b = plane_scatter(da, db, n)
    d_attn_in = jnp.concatenate([in_a, in_b], axis=0)
    inv_attn = lax.rsqrt(jnp.mean(hidden_f * hidden_f, axis=-1, keepdims=True) + EPS)
    normed_a = hidden_f * inv_attn
    d_normed_a = d_attn_in * gain_a
    d_hidden = d_resid + inv_attn * (
        d_normed_a - normed_a * jnp.mean(d_normed_a * normed_a, axis=-1, keepdims=True)
    )
    expert_grads = jnp.stack(expert_grads)
    return (
        output,
        d_hidden,
        sums[:, 0],
        grad_query,
        grad_key,
        grad_value,
        grad_out_proj,
        sums[:, 1],
        sums[:, 2:],
        expert_grads[:, 0],
        expert_grads[:, 1],
        expert_grads[:, 2],
    )


def solution(mesh):
    rows = P(("dp", "ctx"), None)
    flat = P(("dp", "ctx"))
    expert = P("ctx", "dp", None)
    return jax.shard_map(
        shards,
        mesh=mesh,
        in_specs=(
            rows,
            flat,
            rows,
            rows,
            rows,
            rows,
            flat,
            rows,
            rows,
            rows,
            expert,
            expert,
            expert,
            rows,
        ),
        out_specs=(
            rows,
            rows,
            flat,
            rows,
            rows,
            rows,
            rows,
            flat,
            rows,
            expert,
            expert,
            expert,
        ),
        check_vma=False,
    )
```

```python
import functools

import jax
import jax.numpy as jnp
from jax import lax
from jax.experimental import pallas as pl
from jax.experimental.pallas import tpu as pltpu
from jax.sharding import PartitionSpec as P

H = 24
KV = 8
HD = 64
TOP = 8
CAP = 1024

EPS = 1e-06
NEG_FILL = -1e30
SCORE_SCALE = 0.015625
RESIDUAL_SCALE = 0.22

GROUP = H // KV
HALF = HD // 2
QW = GROUP * HD
QKV = QW + 2 * HD
LOW = 64
EXTRA = 128

f32 = jnp.float32
bf16 = jnp.bfloat16
i32 = jnp.int32
VMEM_LIMIT = 58 * 1024 * 1024


def dot_nn(a, b):
    return lax.dot_general(a, b, (((1,), (0,)), ((), ())), preferred_element_type=f32)


def dot_nt(a, b):
    return lax.dot_general(a, b, (((1,), (1,)), ((), ())), preferred_element_type=f32)


def dot_tn(a, b):
    return lax.dot_general(a, b, (((0,), (0,)), ((), ())), preferred_element_type=f32)


def params(limit=VMEM_LIMIT):
    return pltpu.CompilerParams(dimension_semantics=("arbitrary",), vmem_limit_bytes=limit)


def lane_orders(count):
    bits = []
    bit = 2
    while bit < count:
        bits.append(bit)
        bit *= 2
    return (bits[::-1] + [1], bits + [1])


def slots_of(order):
    slots = [0]
    for bit in order:
        slots = slots + [s ^ bit for s in slots]
    return slots


def swap(value, bit, count):
    return lax.ppermute(value, "ctx", [(i, i ^ bit) for i in range(count)])


class Gather:
    def __init__(self, first, second, count):
        self.count = count
        self.orders = lane_orders(count)
        self.have = [first[None], second[None]]
        self.at = 0
        self.start()

    def start(self):
        self.got = [
            swap(have, order[self.at], self.count)
            for have, order in zip(self.have, self.orders)
        ]
        self.at += 1

    def step(self):
        self.have = [
            jnp.concatenate([have, got], axis=0) for have, got in zip(self.have, self.got)
        ]
        self.start()

    def run(self):
        while self.at < len(self.orders[0]):
            self.step()
        return [self.have[0], self.got[0], self.have[1], self.got[1]]


def add_up(x, y):
    return (x.astype(f32) + y.astype(f32)).astype(bf16)


def fold_kernel(*refs):
    ins, outs = (refs[:8], refs[8:])
    for lane in range(2):
        near, got, near_far, got_far = ins[4 * lane : 4 * lane + 4]
        outs[2 * lane][...] = add_up(near[...], got[...])
        outs[2 * lane + 1][...] = add_up(near_far[...], got_far[...])


def fold(keep, got):
    size, *rest = keep[0].shape
    half = size // 2
    zeros = (0,) * len(rest)
    near = pl.BlockSpec((1, *rest), lambda i: (i,) + zeros)
    far = pl.BlockSpec((1, *rest), lambda i: (i + half,) + zeros)
    out = [jax.ShapeDtypeStruct((half, *rest), bf16)] * 4
    kept_a, sent_a, kept_b, sent_b = pl.pallas_call(
        fold_kernel,
        grid=(half,),
        in_specs=[near, near, far, far] * 2,
        out_specs=[near] * 4,
        out_shape=out,
        compiler_params=params(16 * 1024 * 1024),
        cost_estimate=pl.CostEstimate(flops=int(3e9), bytes_accessed=int(3e6), transcendentals=0),
        name="fold",
    )(keep[0], got[0], keep[0], got[0], keep[1], got[1], keep[1], got[1])
    return [kept_a, kept_b], [sent_a, sent_b]


class Scatter:
    def __init__(self, pieces, count):
        a, a_far, b, b_far = pieces
        self.count = count
        self.orders = [order[::-1] for order in lane_orders(count)]
        self.keep = [a, b]
        self.got = [swap(a_far, 1, count), swap(b_far, 1, count)]
        self.at = 1

    def step(self):
        self.keep, send = fold(self.keep, self.got)
        self.got = [
            swap(part, order[self.at], self.count) for part, order in zip(send, self.orders)
        ]
        self.at += 1

    def run(self):
        while self.at < len(self.orders[0]):
            self.step()
        return [(keep[0], got[0]) for keep, got in zip(self.keep, self.got)]


def after(values, *others):
    return lax.optimization_barrier((values, others))[0]


def near(slots, lane, step, far):
    return slots[lane, step] < far


def pick(flags, pieces):
    a, a_far, b, b_far = pieces
    return jnp.concatenate(
        [lax.select(flags[0], a[0], a_far[0]), lax.select(flags[1], b[0], b_far[0])], axis=0
    )


def put(flags, outs, rows):
    a, a_far, b, b_far = outs
    half = a.shape[1]
    for flag, near_o, far_o, part in (
        (flags[0], a, a_far, rows[:half]),
        (flags[1], b, b_far, rows[half:]),
    ):

        @pl.when(flag)
        def _():
            near_o[0] = part

        @pl.when(jnp.logical_not(flag))
        def _():
            far_o[0] = part


def prep_kernel(query, key, value, gain_a, gain_f, router, routes, order, out):
    rp = query.shape[0]
    count, _, columns = out.shape
    small = [x[...].astype(f32) for x in (gain_a, gain_f, router)]
    side = jnp.concatenate(small, axis=0).T.astype(bf16)
    tail = jnp.zeros((rp, columns - QKV - side.shape[1]), bf16)
    rows = [x[...].astype(f32) for x in (routes, order)]
    tok = order.shape[1]
    ranks = out.shape[1] - rp
    rows.append(jnp.zeros((ranks - TOP - 1, tok), f32))
    rows = jnp.concatenate(rows, axis=0).astype(bf16)
    rows = jnp.concatenate([rows, jnp.zeros((ranks, columns - tok), bf16)], axis=1)
    for c in range(count):
        g = c * KV // count
        out[c, :rp, :] = jnp.concatenate(
            [
                query[:, g * QW : (g + 1) * QW],
                key[:, g * HD : (g + 1) * HD],
                value[:, g * HD : (g + 1) * HD],
                side,
                tail,
            ],
            axis=1,
        )
        out[c, rp : rp + ranks, :] = rows


def pack_kernel(took, w_out, out):
    count, _, columns = took.shape
    rp, width = w_out.shape
    slab = count * rp
    chunks = width // slab
    for j in range(chunks):
        out[j * rp : (j + 1) * rp, :] = w_out[:, j * slab : (j + 1) * slab]
    rows = took[:, :rp, :].astype(f32).reshape(slab, columns).T
    out[chunks * rp :, :] = rows[: out.shape[0] - chunks * rp].astype(bf16)


def unpack_kernel(shards, rp, where, *refs):
    pieces, (wt_o, gains_o, router_o, rows_o) = (refs[: 2 * shards - 1], refs[2 * shards - 1 :])
    slab = pieces[0].shape[1]
    first = shards * rp
    experts = router_o.shape[0]
    for z in range(shards):

        @pl.when(where[0] == z)
        def _():
            for p in range(shards):
                piece = pieces[p - z + shards - 1]
                columns = slice(p * slab, (p + 1) * slab)
                wt_o[:, columns] = piece[first : first + QKV]
                gains_o[:, columns] = piece[first + QKV : first + QKV + 2].astype(f32)
                router_o[:, columns] = piece[first + QKV + 2 : first + QKV + 2 + experts]
                for j in range(shards):
                    rows_o[p, :, j * slab : (j + 1) * slab] = piece[j * rp : (j + 1) * rp]


def code_kernel(first, table, out, load):
    i = pl.program_id(0)
    tok, experts = out.shape[1:]

    @pl.when(i == 0)
    def _():
        load[...] = jnp.zeros_like(load)

    rows = table[0, first : first + TOP + 1, :tok].astype(f32)
    names = lax.broadcasted_iota(i32, (experts, tok), 0).astype(f32)
    named = jnp.zeros((experts, tok), f32)
    for k in range(TOP):
        named += jnp.where(rows[k : k + 1] == names, 1.0, 0.0)
    ranks = jnp.broadcast_to(rows[TOP : TOP + 1], (tok, tok))
    before = jnp.where(ranks.T < ranks, 1.0, 0.0).astype(bf16)
    slot = dot_nn(named.astype(bf16), before) + load[:, :1]
    out[0] = (named * (1.0 + jnp.where(slot < CAP, 1.0, 0.0))).T
    load[...] += jnp.sum(named, axis=1, keepdims=True)


def qkv_kernel(
    far, slot_ref, xa, xaf, xb, xbf, gain, wt, cos, sin, ain_o, qt_o, k_o, kt_o, v_o, vt_o
):
    i = pl.program_id(0)
    flags = (near(slot_ref, 0, i, far), near(slot_ref, 1, i, far))
    x = pick(flags, (xa, xaf, xb, xbf)).astype(f32)
    inv = lax.rsqrt(jnp.mean(x * x, axis=-1, keepdims=True) + EPS)
    a = (x * inv * gain[...]).astype(bf16)
    ain_o[0] = a
    y = dot_nt(wt[...], a)
    c, s = (cos[0], sin[0])

    def turn(rows):
        lo, hi = (rows[:HALF], rows[HALF:])
        return jnp.concatenate([lo * c - hi * s, hi * c + lo * s], axis=0)

    for h in range(GROUP):
        q = turn(y[h * HD : (h + 1) * HD]).astype(bf16).astype(f32) * SCORE_SCALE
        qt_o[0, h * HD : (h + 1) * HD, :] = q.astype(bf16)
    k = turn(y[QW : QW + HD])
    kt_o[0] = k.astype(bf16)
    k_o[0] = k.T.astype(bf16)
    v = y[QW + HD :]
    vt_o[0] = v.astype(bf16)
    v_o[0] = v.T.astype(bf16)


def heads_wide(rows):
    return jnp.concatenate([rows[h * HD : (h + 1) * HD] for h in range(GROUP)], axis=1)


def causal(shape, width):
    key = lax.broadcasted_iota(i32, shape, 0)
    query = lax.broadcasted_iota(i32, shape, 1)
    for _ in range(GROUP - 1):
        query = jnp.where(query >= width, query - width, query)
    return key <= query


def attn_fwd_kernel(qt, k, vt, of_o, ob_o, lse_o):
    a = pl.program_id(0)
    tok = qt.shape[2]
    q = heads_wide(qt[0])
    s = dot_nn(k[a], q)
    s = jnp.where(causal(s.shape, tok), s, NEG_FILL)
    m = jnp.max(s, axis=0, keepdims=True)
    p = jnp.exp(s - m)
    l = jnp.sum(p, axis=0, keepdims=True)
    o = dot_nn(vt[a], p.astype(bf16))

    def step(b, carry):
        m, l, o = carry
        s = dot_nn(k[b], q)
        new = jnp.maximum(m, jnp.max(s, axis=0, keepdims=True))
        p = jnp.exp(s - new)
        back = jnp.exp(m - new)
        l = l * back + jnp.sum(p, axis=0, keepdims=True)
        o = o * back + dot_nn(vt[b], p.astype(bf16))
        return (new, l, o)

    m, l, o = lax.fori_loop(0, a, step, (m, l, o))
    o = o / l
    lse_o[0] = m + jnp.log(l)
    for h in range(GROUP):
        part = o[:, h * tok : (h + 1) * tok]
        of_o[0, h * HD : (h + 1) * HD, :] = part
        ob_o[0, h * HD : (h + 1) * HD, :] = part.astype(bf16)


def attn_bwd_kernel(qt, dot_, of, lse, k, kt, v, cos, sin, dq_o, dk_o, dv_o, dk_s, dv_s):
    a = pl.program_id(0)
    tok = qt.shape[2]
    count = k.shape[0]
    q = heads_wide(qt[0])
    do = heads_wide(dot_[0])
    delta = jnp.sum(do.astype(f32) * heads_wide(of[0]), axis=0, keepdims=True)
    total = lse[0]

    def pair(b, mask):
        s = dot_nn(k[b], q)
        p = jnp.exp(s - total)
        if mask:
            p = jnp.where(causal(s.shape, tok), p, 0.0)
        dp = dot_nn(v[b], do)
        ds = (p * (dp - delta)).astype(bf16)
        return dot_nt(ds, q), dot_nt(p.astype(bf16), do), dot_nn(kt[b], ds)

    dk, dv, dq = pair(a, True)
    dk_s[a] = dk
    dv_s[a] = dv

    def step(b, dq):
        dk, dv, more = pair(b, False)
        dk_s[b] += dk
        dv_s[b] += dv
        return dq + more

    dq = lax.fori_loop(0, a, step, dq) * SCORE_SCALE

    def back(rows, c, s):
        lo, hi = (rows[:HALF], rows[HALF:])
        return jnp.concatenate([lo * c + hi * s, hi * c - lo * s], axis=0)

    for h in range(GROUP):
        dq_o[0, h * HD : (h + 1) * HD, :] = back(
            dq[:, h * tok : (h + 1) * tok], cos[a], sin[a]
        ).astype(bf16)

    @pl.when(a == count - 1)
    def _():
        @pl.loop(0, count)
        def _(b):
            dk_o[b] = back(dk_s[b].T, cos[b], sin[b]).astype(bf16)
            dv_o[b] = dv_s[b].T.astype(bf16)


def qkv_bwd_kernel(
    share, far, blocks_ref, dqa, dka, dva, dqb, dkb, dvb, aa, ab, xa, xaf, xb, xbf, wt,
    da_o, daf_o, db_o, dbf_o, gw_o, gg_o, acc, gacc,
):
    i = pl.program_id(0)
    flags = (i < far, i < far)
    d = jnp.concatenate(
        [
            jnp.concatenate([dqa[0], dka[0], dva[0]], axis=0),
            jnp.concatenate([dqb[0], dkb[0], dvb[0]], axis=0),
        ],
        axis=1,
    )
    part = dot_tn(d, wt[...]) * share
    x = pick(flags, (xa, xaf, xb, xbf)).astype(f32)
    inv = lax.rsqrt(jnp.mean(x * x, axis=-1, keepdims=True) + EPS)
    put(flags, (da_o, daf_o, db_o, dbf_o), part.astype(bf16))

    @pl.when(i == 0)
    def _():
        acc[...] = jnp.zeros_like(acc)
        gacc[...] = jnp.zeros_like(gacc)

    acc[...] += dot_nn(d, jnp.concatenate([aa[0], ab[0]], axis=0))
    gacc[...] += jnp.sum(part * (x * inv), axis=0, keepdims=True)

    @pl.when(i == pl.num_programs(0) - 1)
    def _():
        width = gw_o.shape[2]
        for z in range(gw_o.shape[0]):
            gw_o[z] = acc[:, z * width : (z + 1) * width].astype(bf16)
        gg_o[...] = gacc[...]


def expert_terms(expert, x, y, router, code, w_gate, w_up, w_down):
    logits = dot_nt(x, router)
    named = code > 0.5
    logits = jnp.where(named, logits, NEG_FILL)
    top = jnp.max(logits, axis=-1, keepdims=True)
    raised = jnp.where(named, jnp.exp(logits - top), 0.0)
    gates = raised / jnp.sum(raised, axis=-1, keepdims=True)
    mine = (lax.broadcasted_iota(i32, gates.shape, 1) == expert) & (code > 1.5)
    weight = RESIDUAL_SCALE * jnp.sum(jnp.where(mine, gates, 0.0), axis=-1, keepdims=True)
    kept = RESIDUAL_SCALE * jnp.sum(jnp.where(mine, 1.0, 0.0), axis=-1, keepdims=True)

    gate_pre = dot_nn(x, w_gate)
    up_pre = dot_nn(x, w_up)
    back = dot_nn(y, w_down)
    sig = jax.nn.sigmoid(gate_pre)
    act = gate_pre * sig
    inner = act * up_pre
    gate_grad = kept * jnp.sum(inner * back, axis=-1, keepdims=True)
    inner_w = (inner * weight).astype(bf16)
    d_inner = back * weight
    d_gate = (d_inner * up_pre * sig * (1.0 + gate_pre * (1.0 - sig))).astype(bf16)
    d_up = (d_inner * act).astype(bf16)
    din = dot_nt(d_gate, w_gate) + dot_nt(d_up, w_up)
    high = gate_grad.astype(bf16).astype(f32)
    low = (gate_grad - high).astype(bf16).astype(f32)
    lane = lax.broadcasted_iota(i32, (x.shape[0], EXTRA), 1)
    side = jnp.where(lane == expert, high, 0.0) + jnp.where(lane == expert + LOW, low, 0.0)
    return inner_w, d_gate, d_up, jnp.concatenate([din, side], axis=1)


def weight_of(weights, which):
    shards, _, depth, ff = weights.shape
    return weights[:, which].reshape(shards * depth, ff)


def clear(accs, i):
    @pl.when(i == 0)
    def _():
        for acc in accs:
            acc[...] = jnp.zeros_like(acc)


def flush(accs, grad_o, i):
    @pl.when(i == pl.num_programs(0) - 1)
    def _():
        shards, _, depth, _ = grad_o.shape
        for which, acc in enumerate(accs):
            for z in range(shards):
                grad_o[z, which] = acc[z * depth : (z + 1) * depth, :].astype(bf16)


def moe_first_kernel(far, which, blocks, *refs):
    xs, ys, (router, code_a, code_b, weights) = (refs[:4], refs[4:8], refs[8:12])
    outs, (b_o, grad_o), accs = (refs[12:16], refs[16:18], refs[18:])
    i = pl.program_id(0)
    flags = (i < far, i < far)
    x, y = (pick(flags, xs), pick(flags, ys))
    code = jnp.concatenate([code_a[0], code_b[0]], axis=0)
    inner_w, d_gate, d_up, din = expert_terms(
        which[0], x, y, router[...], code, *[weight_of(weights, m) for m in range(3)]
    )
    put(flags, outs, din.astype(bf16))
    b_o[0] = inner_w
    clear(accs, i)
    accs[0][...] += dot_tn(x, d_gate)
    accs[1][...] += dot_tn(x, d_up)
    accs[2][...] += dot_tn(y, inner_w)
    flush(accs, grad_o, i)


def moe_second_kernel(far, which, blocks, *refs):
    xs, ys, (router, code_a, code_b, weights) = (refs[:4], refs[4:8], refs[8:12])
    prev, outs, (b_o, dg_o, du_o) = (refs[12:16], refs[16:20], refs[20:])
    i = pl.program_id(0)
    flags = (i < far, i < far)
    x, y = (pick(flags, xs), pick(flags, ys))
    code = jnp.concatenate([code_a[0], code_b[0]], axis=0)
    inner_w, d_gate, d_up, din = expert_terms(
        which[0], x, y, router[...], code, *[weight_of(weights, m) for m in range(3)]
    )
    put(flags, outs, (din + pick(flags, prev).astype(f32)).astype(bf16))
    b_o[0] = inner_w
    dg_o[0] = d_gate
    du_o[0] = d_up


def moe_grads_kernel(far, *refs):
    xs, ys, (b, dg, du), grad_o, accs = (refs[:4], refs[4:8], refs[8:11], refs[11], refs[12:])
    i = pl.program_id(0)
    flags = (i < far, i < far)
    x, y = (pick(flags, xs), pick(flags, ys))
    clear(accs, i)
    accs[0][...] += dot_tn(x, dg[0])
    accs[1][...] += dot_tn(x, du[0])
    accs[2][...] += dot_tn(y, b[0])
    flush(accs, grad_o, i)


def moe_out_kernel(far, b0, b1, w0, w1, *outs):
    i = pl.program_id(0)
    flags = (i < far, i < far)
    out = dot_nt(b0[0], weight_of(w0, 0)) + dot_nt(b1[0], weight_of(w1, 0))
    put(flags, outs, out.astype(bf16))


def place_kernel(far, slot_ref, a, af, b, bf, out):
    i = pl.program_id(0)
    flags = (near(slot_ref, 0, i, far), near(slot_ref, 1, i, far))
    half = a.shape[1]
    for z in range(half):
        out[z, 0] = lax.select(flags[0], a[0, z], af[0, z])
        out[half + z, 0] = lax.select(flags[1], b[0, z], bf[0, z])


def after_attn_kernel(attn, w_out, hidden, gain, resid_o, ma_o, mb_o):
    resid = hidden[...].astype(f32) + RESIDUAL_SCALE * dot_tn(attn[...], w_out[...])
    resid_o[...] = resid
    inv = lax.rsqrt(jnp.mean(resid * resid, axis=-1, keepdims=True) + EPS)
    moe_in = (resid * inv * gain[...]).astype(bf16)
    half = ma_o.shape[1]
    ma_o[0] = moe_in[:half]
    mb_o[0] = moe_in[half:]


def before_attn_kernel(
    a0, a1, b0, b1, resid, ma, mb, grad_out, code, router, gain, w_out,
    d_resid_o, d_branch_o, d_attn_o, d_router_o, d_gain_o,
):
    width = resid.shape[1]
    experts = router.shape[0]
    back = jnp.concatenate(
        [
            a0[...].astype(f32) + a1[...].astype(f32),
            b0[...].astype(f32) + b1[...].astype(f32),
        ],
        axis=0,
    )
    moe_in = jnp.concatenate([ma[0], mb[0]], axis=0)
    chosen = code[...] > 0.5
    logits = jnp.where(chosen, dot_nt(moe_in, router[...]), NEG_FILL)
    raised = jnp.where(chosen, jnp.exp(logits - jnp.max(logits, axis=-1, keepdims=True)), 0.0)
    gates = raised / jnp.sum(raised, axis=-1, keepdims=True)
    gate_grad = (
        back[:, width : width + experts] + back[:, width + LOW : width + LOW + experts]
    )
    logit_grad = gates * (gate_grad - jnp.sum(gates * gate_grad, axis=-1, keepdims=True))
    dlogits = logit_grad.astype(bf16)
    d_router_o[...] = dot_tn(dlogits, moe_in)
    d_moe_in = back[:, :width] + dot_nn(dlogits, router[...])
    r = resid[...]
    inv = lax.rsqrt(jnp.mean(r * r, axis=-1, keepdims=True) + EPS)
    normed = r * inv
    d_gain_o[...] = jnp.sum(d_moe_in * normed, axis=0, keepdims=True)
    d_normed = d_moe_in * gain[...]
    d_resid = grad_out[...].astype(f32) + inv * (
        d_normed - normed * jnp.mean(d_normed * normed, axis=-1, keepdims=True)
    )
    d_resid_o[...] = d_resid
    d_branch = (RESIDUAL_SCALE * d_resid).astype(bf16)
    d_branch_o[...] = d_branch
    d_attn_o[...] = dot_nt(w_out[...], d_branch).astype(bf16)


def wout_grad_kernel(far, slot_ref, attn, d_branch, a, af, b, bf):
    n2, half, rp, width = a.shape
    n = 2 * n2
    d = d_branch[...]
    for z in range(2 * half):
        rows = dot_nn(attn[z * n * rp : (z + 1) * n * rp, :], d).astype(bf16)
        lane = 0 if z < half else 1
        near_o, far_o = ((a, af), (b, bf))[lane]
        for c in range(n):
            part = rows[c * rp : (c + 1) * rp]
            slot = slot_ref[lane, c]

            @pl.when(slot < far)
            def _():
                near_o[slot, z % half] = part

            @pl.when(slot >= far)
            def _():
                far_o[slot - far, z % half] = part


def last_kernel(a0, a1, b0, b1, d_resid, hidden, gain, out):
    d = jnp.concatenate(
        [
            a0[...].astype(f32) + a1[...].astype(f32),
            b0[...].astype(f32) + b1[...].astype(f32),
        ],
        axis=0,
    )
    x = hidden[...].astype(f32)
    inv = lax.rsqrt(jnp.mean(x * x, axis=-1, keepdims=True) + EPS)
    normed = x * inv
    d = d * gain[...]
    out[...] = d_resid[...] + inv * (
        d - normed * jnp.mean(d * normed, axis=-1, keepdims=True)
    )


def whole(shape):
    zeros = (0,) * len(shape)
    return pl.BlockSpec(shape, lambda *at: zeros)


def at_step(shape):
    zeros = (0,) * (len(shape) - 1)
    return pl.BlockSpec(shape, lambda i, *refs: (i,) + zeros)


def lanes_at_step(shape, far):
    zeros = (0,) * (len(shape) - 1)
    first = pl.BlockSpec(shape, lambda i, *refs: (jnp.minimum(i, far - 1),) + zeros)
    second = pl.BlockSpec(shape, lambda i, *refs: (jnp.maximum(i - far, 0),) + zeros)
    return [first, second, first, second]


def lanes_at_slot(shape, far):
    zeros = (0,) * (len(shape) - 1)

    def spec(lane, second):
        def index(i, slots):
            slot = slots[lane, i]
            slot = jnp.maximum(slot - far, 0) if second else jnp.minimum(slot, far - 1)
            return (slot,) + zeros

        return pl.BlockSpec(shape, index)

    return [spec(0, False), spec(0, True), spec(1, False), spec(1, True)]


def shape_of(*dims, dtype=bf16):
    return jax.ShapeDtypeStruct(dims, dtype)


def micros(us):
    return pl.CostEstimate(
        flops=int(us * 1.1e9), bytes_accessed=int(us * 1e6), transcendentals=0
    )


def call(kernel, name, us, out_shape, operands, *, grid=None, specs=None, out_specs=None,
         scratch=(), tables=(), limit=58):
    if grid is None:
        specs = [whole(x.shape) for x in operands]
        out_specs = jax.tree.map(lambda x: whole(x.shape), out_shape)
        grid = 1
    return pl.pallas_call(
        kernel,
        grid_spec=pltpu.PrefetchScalarGridSpec(
            num_scalar_prefetch=len(tables),
            grid=(grid,),
            in_specs=specs,
            out_specs=out_specs,
            scratch_shapes=list(scratch),
        ),
        out_shape=out_shape,
        compiler_params=params(limit * 1024 * 1024),
        cost_estimate=micros(us),
        name=name,
    )(*tables, *operands)


def shards(
    hidden,
    gain_attn,
    w_query,
    w_key,
    w_value,
    w_out,
    gain_ffn,
    router,
    routes,
    slot_order,
    w_gate,
    w_up,
    w_down,
    grad_out,
):
    tok, width = hidden.shape
    n = lax.axis_size("ctx")
    dp = lax.axis_size("dp")
    me = lax.axis_index("ctx")
    copies = n // KV
    far = n // 2
    rp = w_query.shape[0]
    slab = rp * n
    experts = router.shape[1]
    half = tok // 2
    ff = w_gate.shape[2]
    depth = w_gate.shape[1]
    orders = lane_orders(n)
    slots = [slots_of(order) for order in orders]
    blocks = jnp.array(slots, i32) ^ me
    inverse = jnp.array([[lane.index(j) for j in range(n)] for lane in slots], i32)
    slot_at = jnp.take(inverse, jnp.arange(n, dtype=i32) ^ me, axis=1)


    side = QKV + 2 + experts
    pad = -(side + rp * dp) % 16
    send = call(
        prep_kernel,
        "prep",
        2,
        shape_of(n, rp + 16, max(slab, tok, -(-side // 128) * 128)),
        [
            w_query,
            w_key,
            w_value,
            gain_attn[None],
            gain_ffn[None],
            router.T,
            routes.T,
            slot_order,
        ],
        limit=58,
    )
    took = lax.all_to_all(send, "ctx", split_axis=0, concat_axis=0, tiled=True)
    pack = call(
        pack_kernel,
        "pack",
        2,
        shape_of(side + rp * dp, slab),
        [took, w_out],
        limit=58,
    )

    def along(value, by):
        pairs = [(z, z + by) for z in range(dp) if 0 <= z + by < dp]
        return lax.ppermute(value, "dp", pairs)

    below, above = ([], [])
    for _ in range(dp - 1):
        below.append(along(below[-1] if below else pack, 1))
        above.append(along(above[-1] if above else pack, -1))
    wt, gains, router_t, out_rows = call(
        functools.partial(unpack_kernel, dp, rp),
        "unpack",
        2,
        [
            shape_of(QKV, width),
            shape_of(2, width, dtype=f32),
            shape_of(experts, width),
            shape_of(dp, rp, width),
        ],
        [*below[::-1], pack, *above],
        grid=1,
        specs=[whole(pack.shape)] * (2 * dp - 1),
        out_specs=[
            whole((QKV, width)),
            whole((2, width)),
            whole((experts, width)),
            whole((dp, rp, width)),
        ],
        tables=[lax.axis_index("dp").reshape(1).astype(i32)],
        limit=58,
    )
    gain_a, gain_f = (gains[0:1], gains[1:2])

    stacks = [jnp.stack([w_gate[e], w_up[e], w_down[e]]) for e in range(w_gate.shape[0])]
    stacks = after(stacks, below[:-1], above[:-1])
    expert_w = [lax.all_gather(stack, "dp", axis=0) for stack in stacks]

    code = call(
        functools.partial(code_kernel, rp),
        "code",
        6,
        shape_of(n, tok, experts, dtype=f32),
        [took],
        grid=n,
        specs=[at_step((1,) + took.shape[1:])],
        out_specs=at_step((1, tok, experts)),
        scratch=[pltpu.VMEM((experts, 1), f32)],
        limit=58,
    )
    code_mine = lax.dynamic_index_in_dim(code, me, 0, keepdims=False)

    x_rows = after(hidden, took)
    x_rows = Gather(x_rows[:half], x_rows[half:], n)
    xs = x_rows.run()
    y_rows = after(grad_out, x_rows.have)
    y_rows = Gather(y_rows[:half], y_rows[half:], n)

    exponents = jnp.arange(HALF, dtype=f32) * (2.0 / HD)
    inverse_freq = jnp.power(10000.0, -exponents)
    positions = jnp.arange(n * tok, dtype=f32).reshape(n, 1, tok)
    angles = positions * inverse_freq[None, :, None]
    cos, sin = (jnp.cos(angles), jnp.sin(angles))

    o_rows = Gather(out_rows[: dp // 2], out_rows[dp // 2 :], n)
    gain_a, code, y_rows.got = after((gain_a, code, y_rows.got))

    ain, qt, k, kt, v, vt = call(
        functools.partial(qkv_kernel, far),
        "qkv",
        6,
        [
            shape_of(n, tok, width),
            shape_of(n, QW, tok),
            shape_of(n, tok, HD),
            shape_of(n, HD, tok),
            shape_of(n, tok, HD),
            shape_of(n, HD, tok),
        ],
        [*xs, gain_a, wt, cos, sin],
        grid=n,
        specs=lanes_at_slot((1, half, width), far)
        + [whole((1, width)), whole((QKV, width))]
        + [at_step((1, HALF, tok))] * 2,
        out_specs=[
            at_step((1, tok, width)),
            at_step((1, QW, tok)),
            at_step((1, tok, HD)),
            at_step((1, HD, tok)),
            at_step((1, tok, HD)),
            at_step((1, HD, tok)),
        ],
        tables=[slot_at],
        limit=58,
    )

    qt, y_rows.have, y_rows.got, o_rows.have, o_rows.got = after(
        (qt, y_rows.have, y_rows.got, o_rows.have, o_rows.got)
    )
    y_rows.step()
    o_rows.step()
    qt = after(qt, y_rows.have, o_rows.have)
    of, attn_t, lse = call(
        attn_fwd_kernel,
        "attn_fwd",
        19,
        [
            shape_of(n, QW, tok, dtype=f32),
            shape_of(n, QW, tok),
            shape_of(n, 1, GROUP * tok, dtype=f32),
        ],
        [qt, k, vt],
        grid=n,
        specs=[at_step((1, QW, tok)), whole((n, tok, HD)), whole((n, HD, tok))],
        out_specs=[at_step((1, QW, tok))] * 2 + [at_step((1, 1, GROUP * tok))],
        limit=58,
    )

    attn_t, y_rows.got, o_rows.got = after((attn_t, y_rows.got, o_rows.got))
    os = o_rows.run()
    ys = y_rows.run()
    attn_b = lax.all_to_all(attn_t, "ctx", split_axis=0, concat_axis=0, tiled=True)
    attn_b = attn_b[::copies].reshape(KV * QW, tok)

    w_out_all = call(
        functools.partial(place_kernel, far),
        "place",
        4,
        shape_of(dp, n, rp, width),
        os,
        grid=n,
        specs=lanes_at_slot((1, dp // 2, rp, width), far),
        out_specs=pl.BlockSpec((dp, 1, rp, width), lambda i, slots: (0, i, 0, 0)),
        tables=[slot_at],
        limit=58,
    ).reshape(KV * QW, width)

    resid, ma, mb = call(
        after_attn_kernel,
        "after_attn",
        6,
        [shape_of(tok, width, dtype=f32)] + [shape_of(1, half, width)] * 2,
        [attn_b, w_out_all, hidden, gain_f],
        limit=58,
    )
    ms = Gather(ma[0], mb[0], n).run()

    side_w = width + EXTRA
    wide = [shape_of(far, half, side_w)] * 4
    rows_in = lanes_at_step((1, half, width), far) * 2 + [
        whole((experts, width)),
        *[
            pl.BlockSpec((1, half, experts), lambda i, which, blocks, lane=lane: (blocks[lane, i], lane, 0))
            for lane in range(2)
        ],
        whole((dp, 3, depth, ff)),
    ]
    hidden_o = [at_step((1, tok, ff))]
    hidden_s = [shape_of(n, tok, ff)]
    accs = [pltpu.VMEM((width, ff), f32)] * 3
    first = (me * len(expert_w)).reshape(1).astype(i32)
    *din, inner_0, grads_0 = call(
        functools.partial(moe_first_kernel, far),
        "moe_first",
        38,
        wide + hidden_s + [shape_of(dp, 3, depth, ff)],
        [*ms, *ys, router_t, code, code, expert_w[0]],
        grid=n,
        specs=rows_in,
        out_specs=lanes_at_step((1, half, side_w), far) + hidden_o + [whole((dp, 3, depth, ff))],
        scratch=accs,
        tables=[first, blocks],
        limit=58,
    )
    *din, inner_1, d_gate_1, d_up_1 = call(
        functools.partial(moe_second_kernel, far),
        "moe_second",
        25,
        wide + hidden_s * 3,
        [*ms, *ys, router_t, code, code, expert_w[1], *din],
        grid=n,
        specs=rows_in + lanes_at_step((1, half, side_w), far),
        out_specs=lanes_at_step((1, half, side_w), far) + hidden_o * 3,
        tables=[first + 1, blocks],
        limit=58,
    )
    back = Scatter(din, n)
    back.step()
    inner_1 = after(inner_1, back.keep)
    grads_1 = call(
        functools.partial(moe_grads_kernel, far),
        "moe_grads",
        15,
        shape_of(dp, 3, depth, ff),
        [*ms, *ys, inner_1, d_gate_1, d_up_1],
        grid=n,
        specs=lanes_at_step((1, half, width), far) * 2 + hidden_o * 3,
        out_specs=whole((dp, 3, depth, ff)),
        scratch=accs,
        limit=58,
    )
    expert_grads = [
        lax.psum_scatter(grads, "dp", scatter_dimension=0, tiled=True)
        for grads in (grads_0, grads_1)
    ]

    back.got = after(back.got, grads_1)
    (a0, a1), (b0, b1) = back.run()
    inner_1 = after(inner_1, back.keep)
    down = pl.BlockSpec((dp, 1, depth, ff), lambda i: (0, 2, 0, 0))
    outs = call(
        functools.partial(moe_out_kernel, far),
        "moe_out",
        8,
        [shape_of(far, half, width)] * 4,
        [inner_0, inner_1, *expert_w],
        grid=n,
        specs=hidden_o * 2 + [down] * 2,
        out_specs=lanes_at_step((1, half, width), far),
        limit=58,
    )
    mix = Scatter(outs, n)
    resid_in = after(resid, expert_grads[0], outs)
    d_resid, d_branch, d_attn, d_router, d_gain_ffn = call(
        before_attn_kernel,
        "before_attn",
        8,
        [
            shape_of(tok, width, dtype=f32),
            shape_of(tok, width),
            shape_of(KV * QW, tok),
            shape_of(experts, width, dtype=f32),
            shape_of(1, width, dtype=f32),
        ],
        [a0, a1, b0, b1, resid_in, ma, mb, grad_out, code_mine, router_t, gain_f, w_out_all],
        limit=58,
    )
    d_heads = lax.all_to_all(
        jnp.repeat(d_attn.reshape(KV, QW, tok), copies, axis=0),
        "ctx",
        split_axis=0,
        concat_axis=0,
        tiled=True,
    )
    d_wout = call(
        functools.partial(wout_grad_kernel, far),
        "wout_grad",
        6,
        [shape_of(far, dp // 2, rp, width)] * 4,
        [attn_b, d_branch],
        grid=1,
        specs=[whole((KV * QW, tok)), whole((tok, width))],
        out_specs=[whole((far, dp // 2, rp, width))] * 4,
        tables=[slot_at],
        limit=58,
    )

    wout = Scatter(d_wout, n)
    d_heads, wout.got, mix.got = after((d_heads, wout.got, mix.got))
    wout.step()
    mix.step()
    d_heads = after(d_heads, wout.keep, mix.keep)
    dq, dk, dv = call(
        attn_bwd_kernel,
        "attn_bwd",
        24,
        [shape_of(n, QW, tok), shape_of(n, HD, tok), shape_of(n, HD, tok)],
        [qt, d_heads, of, lse, k, kt, v, cos, sin],
        grid=n,
        specs=[
            at_step((1, QW, tok)),
            at_step((1, QW, tok)),
            at_step((1, QW, tok)),
            at_step((1, 1, GROUP * tok)),
            whole((n, tok, HD)),
            whole((n, HD, tok)),
            whole((n, tok, HD)),
            whole((n, HALF, tok)),
            whole((n, HALF, tok)),
        ],
        out_specs=[at_step((1, QW, tok)), whole((n, HD, tok)), whole((n, HD, tok))],
        scratch=[pltpu.VMEM((n, tok, HD), f32), pltpu.VMEM((n, tok, HD), f32)],
        limit=58,
    )

    dq, wout.got, mix.got = after((dq, wout.got, mix.got))
    (p0, p1), (q0, q1) = wout.run()
    (r0, r1), (s0, s1) = mix.run()
    dq = after(dq, wout.keep, mix.keep)

    def columns(rows, lane):
        return pl.BlockSpec((1, rows, half), lambda i, blocks: (blocks[lane, i], 0, lane))

    def tokens(lane):
        return pl.BlockSpec((1, half, width), lambda i, blocks: (blocks[lane, i], lane, 0))

    *d_in, gw, d_gain_attn = call(
        functools.partial(qkv_bwd_kernel, 1.0 / copies, far),
        "qkv_bwd",
        12,
        [shape_of(far, half, width)] * 4
        + [shape_of(dp, QKV, slab), shape_of(1, width, dtype=f32)],
        [dq, dk, dv, dq, dk, dv, ain, ain, *xs, wt],
        grid=n,
        specs=[columns(rows, lane) for lane in range(2) for rows in (QW, HD, HD)]
        + [tokens(0), tokens(1)]
        + lanes_at_step((1, half, width), far)
        + [whole((QKV, width))],
        out_specs=lanes_at_step((1, half, width), far)
        + [whole((dp, QKV, slab)), whole((1, width))],
        scratch=[pltpu.VMEM((QKV, width), f32), pltpu.VMEM((1, width), f32)],
        tables=[blocks],
        limit=58,
    )

    d_wout = jnp.concatenate([add_up(p0, p1), add_up(q0, q1)], axis=0)
    rest = jnp.concatenate([d_gain_attn, d_gain_ffn, d_router], axis=0).astype(bf16)
    grads = jnp.concatenate(
        [
            gw,
            rest.reshape(2 + experts, dp, slab).transpose(1, 0, 2),
            d_wout.reshape(dp, rp * dp, slab),
            jnp.zeros((dp, pad, slab), bf16),
        ],
        axis=1,
    )
    own = lax.psum_scatter(grads, "dp", scatter_dimension=0, tiled=True)[0]
    (c0, c1), (e0, e1) = Scatter(d_in, n).run()
    d_hidden = call(
        last_kernel,
        "last",
        3,
        shape_of(tok, width, dtype=f32),
        [c0, c1, e0, e1, after(d_resid, own), hidden, gain_a],
        limit=58,
    )

    given = lax.all_to_all(
        own[:side].T.reshape(n, rp, side), "ctx", split_axis=0, concat_axis=0, tiled=True
    ).astype(f32)
    heads = given[::copies].transpose(1, 0, 2)
    grad_query = heads[:, :, :QW].reshape(rp, KV * QW)
    grad_key = heads[:, :, QW : QW + HD].reshape(rp, KV * HD)
    grad_value = heads[:, :, QW + HD : QKV].reshape(rp, KV * HD)
    sums = jnp.sum(given[:, :, QKV:], axis=0)
    grad_out_proj = own[side : side + rp * dp].reshape(rp, width).astype(f32)

    mixed = jnp.concatenate(
        [r0.astype(f32) + r1.astype(f32), s0.astype(f32) + s1.astype(f32)], axis=0
    )
    output = (resid + mixed).astype(bf16)

    expert_grads = jnp.concatenate(expert_grads, axis=0).astype(f32)
    return (
        output,
        d_hidden,
        sums[:, 0],
        grad_query,
        grad_key,
        grad_value,
        grad_out_proj,
        sums[:, 1],
        sums[:, 2:],
        expert_grads[:, 0],
        expert_grads[:, 1],
        expert_grads[:, 2],
    )


def solution(mesh):
    rows = P(("dp", "ctx"), None)
    flat = P(("dp", "ctx"))
    expert = P("ctx", "dp", None)
    return jax.shard_map(
        shards,
        mesh=mesh,
        in_specs=(
            rows,
            flat,
            rows,
            rows,
            rows,
            rows,
            flat,
            rows,
            rows,
            rows,
            expert,
            expert,
            expert,
            rows,
        ),
        out_specs=(
            rows,
            rows,
            flat,
            rows,
            rows,
            rows,
            rows,
            flat,
            rows,
            expert,
            expert,
            expert,
        ),
        check_vma=False,
    )
```

```python
import functools

import jax
import jax.numpy as jnp
from jax import lax
from jax.experimental import pallas as pl
from jax.experimental.pallas import tpu as pltpu
from jax.sharding import PartitionSpec as P

H = 24
KV = 8
HD = 64
TOP = 8
CAP = 1024

EPS = 1e-06
NEG_FILL = -1e30
SCORE_SCALE = 0.015625
RESIDUAL_SCALE = 0.22

GROUP = H // KV
HALF = HD // 2
QW = GROUP * HD
QKV = QW + 2 * HD
LOW = 64
EXTRA = 128

f32 = jnp.float32
bf16 = jnp.bfloat16
i32 = jnp.int32
VMEM_LIMIT = 58 * 1024 * 1024


def dot_nn(a, b):
    return lax.dot_general(a, b, (((1,), (0,)), ((), ())), preferred_element_type=f32)


def dot_nt(a, b):
    return lax.dot_general(a, b, (((1,), (1,)), ((), ())), preferred_element_type=f32)


def dot_tn(a, b):
    return lax.dot_general(a, b, (((0,), (0,)), ((), ())), preferred_element_type=f32)


def params(limit=VMEM_LIMIT):
    return pltpu.CompilerParams(dimension_semantics=("arbitrary",), vmem_limit_bytes=limit)


def lane_orders(count):
    bits = []
    bit = 2
    while bit < count:
        bits.append(bit)
        bit *= 2
    return (bits[::-1] + [1], bits + [1])


def slots_of(order):
    slots = [0]
    for bit in order:
        slots = slots + [s ^ bit for s in slots]
    return slots


def swap(value, bit, count):
    return lax.ppermute(value, "ctx", [(i, i ^ bit) for i in range(count)])


class Gather:
    def __init__(self, first, second, count):
        self.count = count
        self.orders = lane_orders(count)
        self.have = [first[None], second[None]]
        self.at = 0
        self.start()

    def start(self):
        self.got = [
            swap(have, order[self.at], self.count)
            for have, order in zip(self.have, self.orders)
        ]
        self.at += 1

    def step(self):
        self.have = [
            jnp.concatenate([have, got], axis=0) for have, got in zip(self.have, self.got)
        ]
        self.start()

    def run(self):
        while self.at < len(self.orders[0]):
            self.step()
        return [self.have[0], self.got[0], self.have[1], self.got[1]]


def add_up(x, y):
    return (x.astype(f32) + y.astype(f32)).astype(bf16)


def fold_kernel(*refs):
    ins, outs = (refs[:8], refs[8:])
    for lane in range(2):
        near, got, near_far, got_far = ins[4 * lane : 4 * lane + 4]
        outs[2 * lane][...] = add_up(near[...], got[...])
        outs[2 * lane + 1][...] = add_up(near_far[...], got_far[...])


def fold(keep, got):
    size, *rest = keep[0].shape
    half = size // 2
    zeros = (0,) * len(rest)
    near = pl.BlockSpec((1, *rest), lambda i: (i,) + zeros)
    far = pl.BlockSpec((1, *rest), lambda i: (i + half,) + zeros)
    out = [jax.ShapeDtypeStruct((half, *rest), bf16)] * 4
    kept_a, sent_a, kept_b, sent_b = pl.pallas_call(
        fold_kernel,
        grid=(half,),
        in_specs=[near, near, far, far] * 2,
        out_specs=[near] * 4,
        out_shape=out,
        compiler_params=params(16 * 1024 * 1024),
        cost_estimate=pl.CostEstimate(flops=int(3e9), bytes_accessed=int(3e6), transcendentals=0),
        name="fold",
    )(keep[0], got[0], keep[0], got[0], keep[1], got[1], keep[1], got[1])
    return [kept_a, kept_b], [sent_a, sent_b]


class Scatter:
    def __init__(self, pieces, count):
        a, a_far, b, b_far = pieces
        self.count = count
        self.orders = [order[::-1] for order in lane_orders(count)]
        self.keep = [a, b]
        self.got = [swap(a_far, 1, count), swap(b_far, 1, count)]
        self.at = 1

    def fold(self):
        self.keep, self.send = fold(self.keep, self.got)

    def start(self):
        self.got = [
            swap(part, order[self.at], self.count)
            for part, order in zip(self.send, self.orders)
        ]
        self.at += 1

    def step(self):
        self.fold()
        self.start()

    def run(self):
        while self.at < len(self.orders[0]):
            self.step()
        return [(keep[0], got[0]) for keep, got in zip(self.keep, self.got)]


def after(values, *others):
    return lax.optimization_barrier((values, others))[0]


def near(slots, lane, step, far):
    return slots[lane, step] < far


def pick(flags, pieces):
    a, a_far, b, b_far = pieces
    return jnp.concatenate(
        [lax.select(flags[0], a[0], a_far[0]), lax.select(flags[1], b[0], b_far[0])], axis=0
    )


def put(flags, outs, rows):
    a, a_far, b, b_far = outs
    half = a.shape[1]
    for flag, near_o, far_o, part in (
        (flags[0], a, a_far, rows[:half]),
        (flags[1], b, b_far, rows[half:]),
    ):

        @pl.when(flag)
        def _():
            near_o[0] = part

        @pl.when(jnp.logical_not(flag))
        def _():
            far_o[0] = part


def prep_kernel(query, key, value, gain_a, gain_f, router, routes, order, out):
    rp = query.shape[0]
    count, _, columns = out.shape
    small = [x[...].astype(f32) for x in (gain_a, gain_f, router)]
    side = jnp.concatenate(small, axis=0).T.astype(bf16)
    tail = jnp.zeros((rp, columns - QKV - side.shape[1]), bf16)
    rows = [x[...].astype(f32) for x in (routes, order)]
    tok = order.shape[1]
    ranks = out.shape[1] - rp
    rows.append(jnp.zeros((ranks - TOP - 1, tok), f32))
    rows = jnp.concatenate(rows, axis=0).astype(bf16)
    rows = jnp.concatenate([rows, jnp.zeros((ranks, columns - tok), bf16)], axis=1)
    for c in range(count):
        g = c * KV // count
        out[c, :rp, :] = jnp.concatenate(
            [
                query[:, g * QW : (g + 1) * QW],
                key[:, g * HD : (g + 1) * HD],
                value[:, g * HD : (g + 1) * HD],
                side,
                tail,
            ],
            axis=1,
        )
        out[c, rp : rp + ranks, :] = rows


def pack_kernel(took, w_out, out):
    count, _, columns = took.shape
    rp, width = w_out.shape
    slab = count * rp
    chunks = width // slab
    for j in range(chunks):
        out[j * rp : (j + 1) * rp, :] = w_out[:, j * slab : (j + 1) * slab]
    rows = took[:, :rp, :].astype(f32).reshape(slab, columns).T
    out[chunks * rp :, :] = rows[: out.shape[0] - chunks * rp].astype(bf16)


def unpack_kernel(shards, rp, where, *refs):
    pieces, (wt_o, gains_o, router_o, rows_o) = (refs[: 2 * shards - 1], refs[2 * shards - 1 :])
    slab = pieces[0].shape[1]
    first = shards * rp
    experts = router_o.shape[0]
    for z in range(shards):

        @pl.when(where[0] == z)
        def _():
            for p in range(shards):
                piece = pieces[p - z + shards - 1]
                columns = slice(p * slab, (p + 1) * slab)
                wt_o[:, columns] = piece[first : first + QKV]
                gains_o[:, columns] = piece[first + QKV : first + QKV + 2].astype(f32)
                router_o[:, columns] = piece[first + QKV + 2 : first + QKV + 2 + experts]
                for j in range(shards):
                    rows_o[p, :, j * slab : (j + 1) * slab] = piece[j * rp : (j + 1) * rp]


def code_kernel(first, table, out, load):
    i = pl.program_id(0)
    tok, experts = out.shape[1:]

    @pl.when(i == 0)
    def _():
        load[...] = jnp.zeros_like(load)

    rows = table[0, first : first + TOP + 1, :tok].astype(f32)
    names = lax.broadcasted_iota(i32, (experts, tok), 0).astype(f32)
    named = jnp.zeros((experts, tok), f32)
    for k in range(TOP):
        named += jnp.where(rows[k : k + 1] == names, 1.0, 0.0)
    ranks = jnp.broadcast_to(rows[TOP : TOP + 1], (tok, tok))
    before = jnp.where(ranks.T < ranks, 1.0, 0.0).astype(bf16)
    slot = dot_nn(named.astype(bf16), before) + load[:, :1]
    out[0] = (named * (1.0 + jnp.where(slot < CAP, 1.0, 0.0))).T
    load[...] += jnp.sum(named, axis=1, keepdims=True)


def qkv_kernel(
    far, slot_ref, xa, xaf, xb, xbf, gain, wt, cos, sin, ain_o, qt_o, k_o, kt_o, v_o, vt_o
):
    i = pl.program_id(0)
    flags = (near(slot_ref, 0, i, far), near(slot_ref, 1, i, far))
    x = pick(flags, (xa, xaf, xb, xbf)).astype(f32)
    inv = lax.rsqrt(jnp.mean(x * x, axis=-1, keepdims=True) + EPS)
    a = (x * inv * gain[...]).astype(bf16)
    ain_o[0] = a
    y = dot_nt(wt[...], a)
    c, s = (cos[0], sin[0])

    def turn(rows):
        lo, hi = (rows[:HALF], rows[HALF:])
        return jnp.concatenate([lo * c - hi * s, hi * c + lo * s], axis=0)

    for h in range(GROUP):
        q = turn(y[h * HD : (h + 1) * HD]).astype(bf16).astype(f32) * SCORE_SCALE
        qt_o[0, h * HD : (h + 1) * HD, :] = q.astype(bf16)
    k = turn(y[QW : QW + HD])
    kt_o[0] = k.astype(bf16)
    k_o[0] = k.T.astype(bf16)
    v = y[QW + HD :]
    vt_o[0] = v.astype(bf16)
    v_o[0] = v.T.astype(bf16)


def heads_wide(rows):
    return jnp.concatenate([rows[h * HD : (h + 1) * HD] for h in range(GROUP)], axis=1)


def causal(shape, width):
    key = lax.broadcasted_iota(i32, shape, 0)
    query = lax.broadcasted_iota(i32, shape, 1)
    for _ in range(GROUP - 1):
        query = jnp.where(query >= width, query - width, query)
    return key <= query


def attn_fwd_kernel(qt, k, vt, of_o, ob_o, lse_o):
    a = pl.program_id(0)
    tok = qt.shape[2]
    q = heads_wide(qt[0])
    s = dot_nn(k[a], q)
    s = jnp.where(causal(s.shape, tok), s, NEG_FILL)
    m = jnp.max(s, axis=0, keepdims=True)
    p = jnp.exp(s - m)
    l = jnp.sum(p, axis=0, keepdims=True)
    o = dot_nn(vt[a], p.astype(bf16))

    def step(b, carry):
        m, l, o = carry
        s = dot_nn(k[b], q)
        new = jnp.maximum(m, jnp.max(s, axis=0, keepdims=True))
        p = jnp.exp(s - new)
        back = jnp.exp(m - new)
        l = l * back + jnp.sum(p, axis=0, keepdims=True)
        o = o * back + dot_nn(vt[b], p.astype(bf16))
        return (new, l, o)

    m, l, o = lax.fori_loop(0, a, step, (m, l, o))
    o = o / l
    lse_o[0] = m + jnp.log(l)
    for h in range(GROUP):
        part = o[:, h * tok : (h + 1) * tok]
        of_o[0, h * HD : (h + 1) * HD, :] = part
        ob_o[0, h * HD : (h + 1) * HD, :] = part.astype(bf16)


def attn_bwd_kernel(qt, dot_, of, lse, k, kt, v, cos, sin, dq_o, dk_o, dv_o, dk_s, dv_s):
    a = pl.program_id(0)
    tok = qt.shape[2]
    count = k.shape[0]
    q = heads_wide(qt[0])
    do = heads_wide(dot_[0])
    delta = jnp.sum(do.astype(f32) * heads_wide(of[0]), axis=0, keepdims=True)
    total = lse[0]

    def pair(b, mask):
        s = dot_nn(k[b], q)
        p = jnp.exp(s - total)
        if mask:
            p = jnp.where(causal(s.shape, tok), p, 0.0)
        dp = dot_nn(v[b], do)
        ds = (p * (dp - delta)).astype(bf16)
        return dot_nt(ds, q), dot_nt(p.astype(bf16), do), dot_nn(kt[b], ds)

    dk, dv, dq = pair(a, True)
    dk_s[a] = dk
    dv_s[a] = dv

    def step(b, dq):
        dk, dv, more = pair(b, False)
        dk_s[b] += dk
        dv_s[b] += dv
        return dq + more

    dq = lax.fori_loop(0, a, step, dq) * SCORE_SCALE

    def back(rows, c, s):
        lo, hi = (rows[:HALF], rows[HALF:])
        return jnp.concatenate([lo * c + hi * s, hi * c - lo * s], axis=0)

    for h in range(GROUP):
        dq_o[0, h * HD : (h + 1) * HD, :] = back(
            dq[:, h * tok : (h + 1) * tok], cos[a], sin[a]
        ).astype(bf16)

    @pl.when(a == count - 1)
    def _():
        @pl.loop(0, count)
        def _(b):
            dk_o[b] = back(dk_s[b].T, cos[b], sin[b]).astype(bf16)
            dv_o[b] = dv_s[b].T.astype(bf16)


def qkv_grads_kernel(share, dq, dk, dv, ain, wt, gain, gw_o, gg_o, acc):
    i = pl.program_id(0)
    d = jnp.concatenate([dq[0], dk[0], dv[0]], axis=0)

    @pl.when(i == 0)
    def _():
        acc[...] = jnp.zeros_like(acc)

    acc[...] += dot_nn(d, ain[0])

    @pl.when(i == pl.num_programs(0) - 1)
    def _():
        width = gw_o.shape[2]
        for z in range(gw_o.shape[0]):
            gw_o[z] = acc[:, z * width : (z + 1) * width].astype(bf16)
        total = jnp.sum(acc[...] * wt[...].astype(f32), axis=0, keepdims=True)
        gg_o[...] = total * share / gain[...]


def qkv_back_kernel(share, far, blocks_ref, dqa, dka, dva, dqb, dkb, dvb, wt, *outs):
    i = pl.program_id(0)
    flags = (i < far, i < far)
    d = jnp.concatenate(
        [
            jnp.concatenate([dqa[0], dka[0], dva[0]], axis=0),
            jnp.concatenate([dqb[0], dkb[0], dvb[0]], axis=0),
        ],
        axis=1,
    )
    put(flags, outs, (dot_tn(d, wt[...]) * share).astype(bf16))


def bundle_kernel(gw, gain_a, gain_f, router, p0, p1, q0, q1, out):
    shards, rows, slab = out.shape
    half, rp, _ = p0.shape
    first = shards * rp
    small = jnp.concatenate([gain_a[...], gain_f[...], router[...]], axis=0).astype(bf16)
    count = small.shape[0]
    for z in range(shards):
        near, got = (p0, p1) if z < half else (q0, q1)
        w_out = add_up(near[z % half], got[z % half])
        for j in range(shards):
            out[z, j * rp : (j + 1) * rp, :] = w_out[:, j * slab : (j + 1) * slab]
        out[z, first : first + QKV, :] = gw[z]
        out[z, first + QKV : first + QKV + count, :] = small[:, z * slab : (z + 1) * slab]
        rest = first + QKV + count
        if rest < rows:
            out[z, rest:, :] = jnp.zeros((rows - rest, slab), bf16)


def share_kernel(own, send, w_out_o):
    count, rp, columns = send.shape
    shards = w_out_o.shape[1] // own.shape[1]
    slab = own.shape[1]
    first = shards * rp
    for j in range(shards):
        w_out_o[:, j * slab : (j + 1) * slab] = own[j * rp : (j + 1) * rp, :].astype(f32)
    rows = own[first:, :].astype(f32)
    rows = jnp.concatenate([rows, jnp.zeros((columns - rows.shape[0], slab), f32)], axis=0)
    send[...] = rows.T.reshape(count, rp, columns).astype(bf16)


def finish_kernel(copies, given, query, key, value, sums):
    count = given.shape[0]
    parts = [given[c].astype(f32) for c in range(count)]
    for c in range(0, count, copies):
        g = c // copies
        query[:, g * QW : (g + 1) * QW] = parts[c][:, :QW]
        key[:, g * HD : (g + 1) * HD] = parts[c][:, QW : QW + HD]
        value[:, g * HD : (g + 1) * HD] = parts[c][:, QW + HD : QKV]
    total = parts[0][:, QKV:]
    for part in parts[1:]:
        total = total + part[:, QKV:]
    sums[...] = total[:, : sums.shape[1]]


def expert_terms(expert, x, y, router, code, w_gate, w_up, w_down):
    logits = dot_nt(x, router)
    named = code > 0.5
    logits = jnp.where(named, logits, NEG_FILL)
    top = jnp.max(logits, axis=-1, keepdims=True)
    raised = jnp.where(named, jnp.exp(logits - top), 0.0)
    gates = raised / jnp.sum(raised, axis=-1, keepdims=True)
    mine = (lax.broadcasted_iota(i32, gates.shape, 1) == expert) & (code > 1.5)
    weight = RESIDUAL_SCALE * jnp.sum(jnp.where(mine, gates, 0.0), axis=-1, keepdims=True)
    kept = RESIDUAL_SCALE * jnp.sum(jnp.where(mine, 1.0, 0.0), axis=-1, keepdims=True)

    gate_pre = dot_nn(x, w_gate)
    up_pre = dot_nn(x, w_up)
    back = dot_nn(y, w_down)
    sig = jax.nn.sigmoid(gate_pre)
    act = gate_pre * sig
    inner = act * up_pre
    gate_grad = kept * jnp.sum(inner * back, axis=-1, keepdims=True)
    inner_w = (inner * weight).astype(bf16)
    d_inner = back * weight
    d_gate = (d_inner * up_pre * sig * (1.0 + gate_pre * (1.0 - sig))).astype(bf16)
    d_up = (d_inner * act).astype(bf16)
    din = dot_nt(d_gate, w_gate) + dot_nt(d_up, w_up)
    high = gate_grad.astype(bf16).astype(f32)
    low = (gate_grad - high).astype(bf16).astype(f32)
    lane = lax.broadcasted_iota(i32, (x.shape[0], EXTRA), 1)
    side = jnp.where(lane == expert, high, 0.0) + jnp.where(lane == expert + LOW, low, 0.0)
    return inner_w, d_gate, d_up, jnp.concatenate([din, side], axis=1)


def weight_of(weights, which):
    shards, _, depth, ff = weights.shape
    return weights[:, which].reshape(shards * depth, ff)


def clear(accs, i):
    @pl.when(i == 0)
    def _():
        for acc in accs:
            acc[...] = jnp.zeros_like(acc)


def flush(accs, grad_o, i):
    @pl.when(i == pl.num_programs(0) - 1)
    def _():
        shards, _, depth, _ = grad_o.shape
        for which, acc in enumerate(accs):
            for z in range(shards):
                grad_o[z, which] = acc[z * depth : (z + 1) * depth, :].astype(bf16)


def moe_first_kernel(far, which, blocks, *refs):
    xs, ys, (router, code_a, code_b, weights) = (refs[:4], refs[4:8], refs[8:12])
    outs, (b_o, grad_o), accs = (refs[12:16], refs[16:18], refs[18:])
    i = pl.program_id(0)
    flags = (i < far, i < far)
    x, y = (pick(flags, xs), pick(flags, ys))
    code = jnp.concatenate([code_a[0], code_b[0]], axis=0)
    inner_w, d_gate, d_up, din = expert_terms(
        which[0], x, y, router[...], code, *[weight_of(weights, m) for m in range(3)]
    )
    put(flags, outs, din.astype(bf16))
    b_o[0] = inner_w
    clear(accs, i)
    accs[0][...] += dot_tn(x, d_gate)
    accs[1][...] += dot_tn(x, d_up)
    accs[2][...] += dot_tn(y, inner_w)
    flush(accs, grad_o, i)


def moe_second_kernel(far, which, blocks, *refs):
    xs, ys, (router, code_a, code_b, weights) = (refs[:4], refs[4:8], refs[8:12])
    prev, outs, (b_o, dg_o, du_o) = (refs[12:16], refs[16:20], refs[20:])
    i = pl.program_id(0)
    flags = (i < far, i < far)
    x, y = (pick(flags, xs), pick(flags, ys))
    code = jnp.concatenate([code_a[0], code_b[0]], axis=0)
    inner_w, d_gate, d_up, din = expert_terms(
        which[0], x, y, router[...], code, *[weight_of(weights, m) for m in range(3)]
    )
    put(flags, outs, (din + pick(flags, prev).astype(f32)).astype(bf16))
    b_o[0] = inner_w
    dg_o[0] = d_gate
    du_o[0] = d_up


def moe_grads_kernel(far, *refs):
    xs, ys, (b, dg, du), grad_o, accs = (refs[:4], refs[4:8], refs[8:11], refs[11], refs[12:])
    i = pl.program_id(0)
    flags = (i < far, i < far)
    x, y = (pick(flags, xs), pick(flags, ys))
    clear(accs, i)
    accs[0][...] += dot_tn(x, dg[0])
    accs[1][...] += dot_tn(x, du[0])
    accs[2][...] += dot_tn(y, b[0])
    flush(accs, grad_o, i)


def moe_out_kernel(far, b0, b1, w0, w1, *outs):
    i = pl.program_id(0)
    flags = (i < far, i < far)
    out = dot_nt(b0[0], weight_of(w0, 0)) + dot_nt(b1[0], weight_of(w1, 0))
    put(flags, outs, out.astype(bf16))


def place_kernel(far, slot_ref, a, af, b, bf, out):
    i = pl.program_id(0)
    flags = (near(slot_ref, 0, i, far), near(slot_ref, 1, i, far))
    half = a.shape[1]
    for z in range(half):
        out[z, 0] = lax.select(flags[0], a[0, z], af[0, z])
        out[half + z, 0] = lax.select(flags[1], b[0, z], bf[0, z])


def after_attn_kernel(attn, w_out, hidden, gain, resid_o, ma_o, mb_o):
    resid = hidden[...].astype(f32) + RESIDUAL_SCALE * dot_tn(attn[...], w_out[...])
    resid_o[...] = resid
    inv = lax.rsqrt(jnp.mean(resid * resid, axis=-1, keepdims=True) + EPS)
    moe_in = (resid * inv * gain[...]).astype(bf16)
    half = ma_o.shape[1]
    ma_o[0] = moe_in[:half]
    mb_o[0] = moe_in[half:]


def before_attn_kernel(
    a0, a1, b0, b1, resid, ma, mb, grad_out, code, router, gain, w_out,
    d_resid_o, d_branch_o, d_attn_o, d_router_o, d_gain_o,
):
    width = resid.shape[1]
    experts = router.shape[0]
    back = jnp.concatenate(
        [
            a0[...].astype(f32) + a1[...].astype(f32),
            b0[...].astype(f32) + b1[...].astype(f32),
        ],
        axis=0,
    )
    moe_in = jnp.concatenate([ma[0], mb[0]], axis=0)
    chosen = code[...] > 0.5
    logits = jnp.where(chosen, dot_nt(moe_in, router[...]), NEG_FILL)
    raised = jnp.where(chosen, jnp.exp(logits - jnp.max(logits, axis=-1, keepdims=True)), 0.0)
    gates = raised / jnp.sum(raised, axis=-1, keepdims=True)
    gate_grad = (
        back[:, width : width + experts] + back[:, width + LOW : width + LOW + experts]
    )
    logit_grad = gates * (gate_grad - jnp.sum(gates * gate_grad, axis=-1, keepdims=True))
    dlogits = logit_grad.astype(bf16)
    d_router_o[...] = dot_tn(dlogits, moe_in)
    d_moe_in = back[:, :width] + dot_nn(dlogits, router[...])
    r = resid[...]
    inv = lax.rsqrt(jnp.mean(r * r, axis=-1, keepdims=True) + EPS)
    normed = r * inv
    d_gain_o[...] = jnp.sum(d_moe_in * normed, axis=0, keepdims=True)
    d_normed = d_moe_in * gain[...]
    d_resid = grad_out[...].astype(f32) + inv * (
        d_normed - normed * jnp.mean(d_normed * normed, axis=-1, keepdims=True)
    )
    d_resid_o[...] = d_resid
    d_branch = (RESIDUAL_SCALE * d_resid).astype(bf16)
    d_branch_o[...] = d_branch
    d_attn_o[...] = dot_nt(w_out[...], d_branch).astype(bf16)


def wout_grad_kernel(far, slot_ref, attn, d_branch, a, af, b, bf):
    n2, half, rp, width = a.shape
    n = 2 * n2
    d = d_branch[...]
    for z in range(2 * half):
        rows = dot_nn(attn[z * n * rp : (z + 1) * n * rp, :], d).astype(bf16)
        lane = 0 if z < half else 1
        near_o, far_o = ((a, af), (b, bf))[lane]
        for c in range(n):
            part = rows[c * rp : (c + 1) * rp]
            slot = slot_ref[lane, c]

            @pl.when(slot < far)
            def _():
                near_o[slot, z % half] = part

            @pl.when(slot >= far)
            def _():
                far_o[slot - far, z % half] = part


def last_kernel(a0, a1, b0, b1, d_resid, hidden, gain, out):
    d = jnp.concatenate(
        [
            a0[...].astype(f32) + a1[...].astype(f32),
            b0[...].astype(f32) + b1[...].astype(f32),
        ],
        axis=0,
    )
    x = hidden[...].astype(f32)
    inv = lax.rsqrt(jnp.mean(x * x, axis=-1, keepdims=True) + EPS)
    normed = x * inv
    d = d * gain[...]
    out[...] = d_resid[...] + inv * (
        d - normed * jnp.mean(d * normed, axis=-1, keepdims=True)
    )


def whole(shape):
    zeros = (0,) * len(shape)
    return pl.BlockSpec(shape, lambda *at: zeros)


def at_step(shape):
    zeros = (0,) * (len(shape) - 1)
    return pl.BlockSpec(shape, lambda i, *refs: (i,) + zeros)


def lanes_at_step(shape, far):
    zeros = (0,) * (len(shape) - 1)
    first = pl.BlockSpec(shape, lambda i, *refs: (jnp.minimum(i, far - 1),) + zeros)
    second = pl.BlockSpec(shape, lambda i, *refs: (jnp.maximum(i - far, 0),) + zeros)
    return [first, second, first, second]


def lanes_at_slot(shape, far):
    zeros = (0,) * (len(shape) - 1)

    def spec(lane, second):
        def index(i, slots):
            slot = slots[lane, i]
            slot = jnp.maximum(slot - far, 0) if second else jnp.minimum(slot, far - 1)
            return (slot,) + zeros

        return pl.BlockSpec(shape, index)

    return [spec(0, False), spec(0, True), spec(1, False), spec(1, True)]


def shape_of(*dims, dtype=bf16):
    return jax.ShapeDtypeStruct(dims, dtype)


def micros(us):
    return pl.CostEstimate(
        flops=int(us * 1.1e9), bytes_accessed=int(us * 1e6), transcendentals=0
    )


def call(kernel, name, us, out_shape, operands, *, grid=None, specs=None, out_specs=None,
         scratch=(), tables=(), limit=58):
    if grid is None:
        specs = [whole(x.shape) for x in operands]
        out_specs = jax.tree.map(lambda x: whole(x.shape), out_shape)
        grid = 1
    return pl.pallas_call(
        kernel,
        grid_spec=pltpu.PrefetchScalarGridSpec(
            num_scalar_prefetch=len(tables),
            grid=(grid,),
            in_specs=specs,
            out_specs=out_specs,
            scratch_shapes=list(scratch),
        ),
        out_shape=out_shape,
        compiler_params=params(limit * 1024 * 1024),
        cost_estimate=micros(us),
        name=name,
    )(*tables, *operands)


def shards(
    hidden,
    gain_attn,
    w_query,
    w_key,
    w_value,
    w_out,
    gain_ffn,
    router,
    routes,
    slot_order,
    w_gate,
    w_up,
    w_down,
    grad_out,
):
    tok, width = hidden.shape
    n = lax.axis_size("ctx")
    dp = lax.axis_size("dp")
    me = lax.axis_index("ctx")
    copies = n // KV
    far = n // 2
    rp = w_query.shape[0]
    slab = rp * n
    experts = router.shape[1]
    half = tok // 2
    ff = w_gate.shape[2]
    depth = w_gate.shape[1]
    orders = lane_orders(n)
    slots = [slots_of(order) for order in orders]
    blocks = jnp.array(slots, i32) ^ me
    inverse = jnp.array([[lane.index(j) for j in range(n)] for lane in slots], i32)
    slot_at = jnp.take(inverse, jnp.arange(n, dtype=i32) ^ me, axis=1)


    side = QKV + 2 + experts
    pad = -(side + rp * dp) % 16
    send = call(
        prep_kernel,
        "prep",
        2,
        shape_of(n, rp + 16, max(slab, tok, -(-side // 128) * 128)),
        [
            w_query,
            w_key,
            w_value,
            gain_attn[None],
            gain_ffn[None],
            router.T,
            routes.T,
            slot_order,
        ],
        limit=58,
    )
    took = lax.all_to_all(send, "ctx", split_axis=0, concat_axis=0, tiled=True)
    pack = call(
        pack_kernel,
        "pack",
        2,
        shape_of(side + rp * dp, slab),
        [took, w_out],
        limit=58,
    )

    def along(value, by):
        pairs = [(z, z + by) for z in range(dp) if 0 <= z + by < dp]
        return lax.ppermute(value, "dp", pairs)

    below, above = ([], [])
    for _ in range(dp - 1):
        below.append(along(below[-1] if below else pack, 1))
        above.append(along(above[-1] if above else pack, -1))
    wt, gains, router_t, out_rows = call(
        functools.partial(unpack_kernel, dp, rp),
        "unpack",
        2,
        [
            shape_of(QKV, width),
            shape_of(2, width, dtype=f32),
            shape_of(experts, width),
            shape_of(dp, rp, width),
        ],
        [*below[::-1], pack, *above],
        grid=1,
        specs=[whole(pack.shape)] * (2 * dp - 1),
        out_specs=[
            whole((QKV, width)),
            whole((2, width)),
            whole((experts, width)),
            whole((dp, rp, width)),
        ],
        tables=[lax.axis_index("dp").reshape(1).astype(i32)],
        limit=30,
    )
    gain_a, gain_f = (gains[0:1], gains[1:2])

    stacks = [jnp.stack([w_gate[e], w_up[e], w_down[e]]) for e in range(w_gate.shape[0])]
    stacks = after(stacks, below[:-1], above[:-1])
    expert_w = [lax.all_gather(stack, "dp", axis=0) for stack in stacks]

    code = call(
        functools.partial(code_kernel, rp),
        "code",
        6,
        shape_of(n, tok, experts, dtype=f32),
        [took],
        grid=n,
        specs=[at_step((1,) + took.shape[1:])],
        out_specs=at_step((1, tok, experts)),
        scratch=[pltpu.VMEM((experts, 1), f32)],
        limit=58,
    )
    code_mine = lax.dynamic_index_in_dim(code, me, 0, keepdims=False)

    x_rows = after(hidden, took)
    x_rows = Gather(x_rows[:half], x_rows[half:], n)
    xs = x_rows.run()
    y_rows = after(grad_out, x_rows.have)
    y_rows = Gather(y_rows[:half], y_rows[half:], n)

    exponents = jnp.arange(HALF, dtype=f32) * (2.0 / HD)
    inverse_freq = jnp.power(10000.0, -exponents)
    positions = jnp.arange(n * tok, dtype=f32).reshape(n, 1, tok)
    angles = positions * inverse_freq[None, :, None]
    cos, sin = (jnp.cos(angles), jnp.sin(angles))

    o_rows = Gather(out_rows[: dp // 2], out_rows[dp // 2 :], n)
    gain_a, code, y_rows.got = after((gain_a, code, y_rows.got))

    ain, qt, k, kt, v, vt = call(
        functools.partial(qkv_kernel, far),
        "qkv",
        6,
        [
            shape_of(n, tok, width),
            shape_of(n, QW, tok),
            shape_of(n, tok, HD),
            shape_of(n, HD, tok),
            shape_of(n, tok, HD),
            shape_of(n, HD, tok),
        ],
        [*xs, gain_a, wt, cos, sin],
        grid=n,
        specs=lanes_at_slot((1, half, width), far)
        + [whole((1, width)), whole((QKV, width))]
        + [at_step((1, HALF, tok))] * 2,
        out_specs=[
            at_step((1, tok, width)),
            at_step((1, QW, tok)),
            at_step((1, tok, HD)),
            at_step((1, HD, tok)),
            at_step((1, tok, HD)),
            at_step((1, HD, tok)),
        ],
        tables=[slot_at],
        limit=30,
    )

    qt, code_mine, y_rows.have, y_rows.got, o_rows.have, o_rows.got = after(
        (qt, code_mine, y_rows.have, y_rows.got, o_rows.have, o_rows.got)
    )
    y_rows.step()
    o_rows.step()
    qt = after(qt, code_mine, y_rows.have, o_rows.have)
    of, attn_t, lse = call(
        attn_fwd_kernel,
        "attn_fwd",
        19,
        [
            shape_of(n, QW, tok, dtype=f32),
            shape_of(n, QW, tok),
            shape_of(n, 1, GROUP * tok, dtype=f32),
        ],
        [qt, k, vt],
        grid=n,
        specs=[at_step((1, QW, tok)), whole((n, tok, HD)), whole((n, HD, tok))],
        out_specs=[at_step((1, QW, tok))] * 2 + [at_step((1, 1, GROUP * tok))],
        limit=30,
    )

    attn_t, y_rows.got, o_rows.got = after((attn_t, y_rows.got, o_rows.got))
    os = o_rows.run()
    ys = y_rows.run()
    attn_b = lax.all_to_all(attn_t, "ctx", split_axis=0, concat_axis=0, tiled=True)
    attn_b = attn_b[::copies].reshape(KV * QW, tok)

    w_out_all = call(
        functools.partial(place_kernel, far),
        "place",
        4,
        shape_of(dp, n, rp, width),
        os,
        grid=n,
        specs=lanes_at_slot((1, dp // 2, rp, width), far),
        out_specs=pl.BlockSpec((dp, 1, rp, width), lambda i, slots: (0, i, 0, 0)),
        tables=[slot_at],
        limit=58,
    ).reshape(KV * QW, width)

    resid, ma, mb = call(
        after_attn_kernel,
        "after_attn",
        6,
        [shape_of(tok, width, dtype=f32)] + [shape_of(1, half, width)] * 2,
        [attn_b, w_out_all, hidden, gain_f],
        limit=30,
    )
    ms = Gather(ma[0], mb[0], n).run()

    side_w = width + EXTRA
    wide = [shape_of(far, half, side_w)] * 4
    rows_in = lanes_at_step((1, half, width), far) * 2 + [
        whole((experts, width)),
        *[
            pl.BlockSpec((1, half, experts), lambda i, which, blocks, lane=lane: (blocks[lane, i], lane, 0))
            for lane in range(2)
        ],
        whole((dp, 3, depth, ff)),
    ]
    hidden_o = [at_step((1, tok, ff))]
    hidden_s = [shape_of(n, tok, ff)]
    accs = [pltpu.VMEM((width, ff), f32)] * 3
    first = (me * len(expert_w)).reshape(1).astype(i32)
    *din, inner_0, grads_0 = call(
        functools.partial(moe_first_kernel, far),
        "moe_first",
        38,
        wide + hidden_s + [shape_of(dp, 3, depth, ff)],
        [*ms, *ys, router_t, code, code, expert_w[0]],
        grid=n,
        specs=rows_in,
        out_specs=lanes_at_step((1, half, side_w), far) + hidden_o + [whole((dp, 3, depth, ff))],
        scratch=accs,
        tables=[first, blocks],
        limit=58,
    )
    *din, inner_1, d_gate_1, d_up_1 = call(
        functools.partial(moe_second_kernel, far),
        "moe_second",
        25,
        wide + hidden_s * 3,
        [*ms, *ys, router_t, code, code, expert_w[1], *din],
        grid=n,
        specs=rows_in + lanes_at_step((1, half, side_w), far),
        out_specs=lanes_at_step((1, half, side_w), far) + hidden_o * 3,
        tables=[first + 1, blocks],
        limit=58,
    )
    back = Scatter(din, n)
    back.step()
    inner_1 = after(inner_1, back.keep)
    grads_1 = call(
        functools.partial(moe_grads_kernel, far),
        "moe_grads",
        15,
        shape_of(dp, 3, depth, ff),
        [*ms, *ys, inner_1, d_gate_1, d_up_1],
        grid=n,
        specs=lanes_at_step((1, half, width), far) * 2 + hidden_o * 3,
        out_specs=whole((dp, 3, depth, ff)),
        scratch=accs,
        limit=58,
    )
    expert_grads = [
        lax.psum_scatter(grads, "dp", scatter_dimension=0, tiled=True)
        for grads in (grads_0, grads_1)
    ]

    back.got = after(back.got, grads_1)
    (a0, a1), (b0, b1) = back.run()
    inner_1 = after(inner_1, back.keep)
    down = pl.BlockSpec((dp, 1, depth, ff), lambda i: (0, 2, 0, 0))
    outs = call(
        functools.partial(moe_out_kernel, far),
        "moe_out",
        8,
        [shape_of(far, half, width)] * 4,
        [inner_0, inner_1, *expert_w],
        grid=n,
        specs=hidden_o * 2 + [down] * 2,
        out_specs=lanes_at_step((1, half, width), far),
        limit=58,
    )
    mix = Scatter(outs, n)
    resid_in = after(resid, outs)
    d_resid, d_branch, d_attn, d_router, d_gain_ffn = call(
        before_attn_kernel,
        "before_attn",
        14,
        [
            shape_of(tok, width, dtype=f32),
            shape_of(tok, width),
            shape_of(KV * QW, tok),
            shape_of(experts, width, dtype=f32),
            shape_of(1, width, dtype=f32),
        ],
        [a0, a1, b0, b1, resid_in, ma, mb, grad_out, code_mine, router_t, gain_f, w_out_all],
        limit=30,
    )
    d_heads = lax.all_to_all(
        jnp.repeat(d_attn.reshape(KV, QW, tok), copies, axis=0),
        "ctx",
        split_axis=0,
        concat_axis=0,
        tiled=True,
    )
    d_wout = call(
        functools.partial(wout_grad_kernel, far),
        "wout_grad",
        6,
        [shape_of(far, dp // 2, rp, width)] * 4,
        [attn_b, d_branch],
        grid=1,
        specs=[whole((KV * QW, tok)), whole((tok, width))],
        out_specs=[whole((far, dp // 2, rp, width))] * 4,
        tables=[slot_at],
        limit=30,
    )

    mix.fold()
    mix.send, mix.keep, d_heads, expert_grads[0] = after(
        (mix.send, mix.keep, d_heads, expert_grads[0])
    )
    mix.start()
    wout = Scatter(after(d_wout, d_heads), n)
    dq, dk, dv = call(
        attn_bwd_kernel,
        "attn_bwd",
        40,
        [shape_of(n, QW, tok), shape_of(n, HD, tok), shape_of(n, HD, tok)],
        [qt, d_heads, of, lse, k, kt, v, cos, sin],
        grid=n,
        specs=[
            at_step((1, QW, tok)),
            at_step((1, QW, tok)),
            at_step((1, QW, tok)),
            at_step((1, 1, GROUP * tok)),
            whole((n, tok, HD)),
            whole((n, HD, tok)),
            whole((n, tok, HD)),
            whole((n, HALF, tok)),
            whole((n, HALF, tok)),
        ],
        out_specs=[at_step((1, QW, tok)), whole((n, HD, tok)), whole((n, HD, tok))],
        scratch=[pltpu.VMEM((n, tok, HD), f32), pltpu.VMEM((n, tok, HD), f32)],
        limit=30,
    )

    dq, wout.keep, wout.got = after((dq, wout.keep, wout.got))
    wout.step()
    dq = after(dq, wout.keep)

    gw, d_gain_attn = call(
        functools.partial(qkv_grads_kernel, 1.0 / copies),
        "qkv_grads",
        20,
        [shape_of(dp, QKV, slab), shape_of(1, width, dtype=f32)],
        [dq, dk, dv, ain, wt, gain_a],
        grid=n,
        specs=[
            at_step((1, QW, tok)),
            at_step((1, HD, tok)),
            at_step((1, HD, tok)),
            at_step((1, tok, width)),
            whole((QKV, width)),
            whole((1, width)),
        ],
        out_specs=[whole((dp, QKV, slab)), whole((1, width))],
        scratch=[pltpu.VMEM((QKV, width), f32)],
        limit=30,
    )

    def columns(rows, lane):
        return pl.BlockSpec((1, rows, half), lambda i, blocks: (blocks[lane, i], 0, lane))

    dq, wout.keep, wout.got, mix.keep, mix.got = after(
        (dq, wout.keep, wout.got, mix.keep, mix.got), gw
    )
    wout.step()
    mix.step()
    dq = after(dq, wout.keep, mix.keep)
    d_in = call(
        functools.partial(qkv_back_kernel, 1.0 / copies, far),
        "qkv_back",
        20,
        [shape_of(far, half, width)] * 4,
        [dq, dk, dv, dq, dk, dv, wt],
        grid=n,
        specs=[columns(rows, lane) for lane in range(2) for rows in (QW, HD, HD)]
        + [whole((QKV, width))],
        out_specs=lanes_at_step((1, half, width), far),
        tables=[blocks],
        limit=30,
    )

    wout.got = after(wout.got, d_in)
    (p0, p1), (q0, q1) = wout.run()
    bundle = call(
        bundle_kernel,
        "bundle",
        2,
        shape_of(dp, side + rp * dp + pad, slab),
        [gw, d_gain_attn, d_gain_ffn, d_router, p0, p1, q0, q1],
        limit=30,
    )
    own = lax.psum_scatter(bundle, "dp", scatter_dimension=0, tiled=True)[0]
    send, grad_out_proj = call(
        share_kernel,
        "share",
        2,
        [shape_of(n, rp, -(-(side + pad) // 128) * 128), shape_of(rp, width, dtype=f32)],
        [own],
        limit=30,
    )
    given = lax.all_to_all(send, "ctx", split_axis=0, concat_axis=0, tiled=True)
    grad_query, grad_key, grad_value, sums = call(
        functools.partial(finish_kernel, copies),
        "finish",
        2,
        [
            shape_of(rp, KV * QW, dtype=f32),
            shape_of(rp, KV * HD, dtype=f32),
            shape_of(rp, KV * HD, dtype=f32),
            shape_of(rp, 2 + experts, dtype=f32),
        ],
        [given],
        limit=30,
    )

    back_in = Scatter(d_in, n)
    (c0, c1), (e0, e1) = back_in.run()
    d_hidden = call(
        last_kernel,
        "last",
        3,
        shape_of(tok, width, dtype=f32),
        [c0, c1, e0, e1, after(d_resid, send), hidden, gain_a],
        limit=30,
    )

    (r0, r1), (s0, s1) = mix.run()
    mixed = jnp.concatenate(
        [r0.astype(f32) + r1.astype(f32), s0.astype(f32) + s1.astype(f32)], axis=0
    )
    output = (resid + mixed).astype(bf16)

    expert_grads = jnp.concatenate(expert_grads, axis=0).astype(f32)
    return (
        output,
        d_hidden,
        sums[:, 0],
        grad_query,
        grad_key,
        grad_value,
        grad_out_proj,
        sums[:, 1],
        sums[:, 2:],
        expert_grads[:, 0],
        expert_grads[:, 1],
        expert_grads[:, 2],
    )


def solution(mesh):
    rows = P(("dp", "ctx"), None)
    flat = P(("dp", "ctx"))
    expert = P("ctx", "dp", None)
    return jax.shard_map(
        shards,
        mesh=mesh,
        in_specs=(
            rows,
            flat,
            rows,
            rows,
            rows,
            rows,
            flat,
            rows,
            rows,
            rows,
            expert,
            expert,
            expert,
            rows,
        ),
        out_specs=(
            rows,
            rows,
            flat,
            rows,
            rows,
            rows,
            rows,
            flat,
            rows,
            expert,
            expert,
            expert,
        ),
        check_vma=False,
    )
```

```python
import functools

import jax
import jax.numpy as jnp
from jax import lax
from jax.experimental import pallas as pl
from jax.experimental.pallas import tpu as pltpu
from jax.sharding import PartitionSpec as P

H = 24
KV = 8
HD = 64
TOP = 8
CAP = 1024

EPS = 1e-06
NEG_FILL = -1e30
SCORE_SCALE = 0.015625
RESIDUAL_SCALE = 0.22

GROUP = H // KV
HALF = HD // 2
QW = GROUP * HD
QKV = QW + 2 * HD
LOW = 64
EXTRA = 128

f32 = jnp.float32
bf16 = jnp.bfloat16
i32 = jnp.int32
VMEM_LIMIT = 58 * 1024 * 1024


def dot_nn(a, b):
    return lax.dot_general(a, b, (((1,), (0,)), ((), ())), preferred_element_type=f32)


def dot_nt(a, b):
    return lax.dot_general(a, b, (((1,), (1,)), ((), ())), preferred_element_type=f32)


def dot_tn(a, b):
    return lax.dot_general(a, b, (((0,), (0,)), ((), ())), preferred_element_type=f32)


def params(limit=VMEM_LIMIT):
    return pltpu.CompilerParams(dimension_semantics=("arbitrary",), vmem_limit_bytes=limit)


def lane_orders(count):
    bits = []
    bit = 2
    while bit < count:
        bits.append(bit)
        bit *= 2
    return (bits[::-1] + [1], bits + [1])


def slots_of(order):
    slots = [0]
    for bit in order:
        slots = slots + [s ^ bit for s in slots]
    return slots


def swap(value, bit, count):
    return lax.ppermute(value, "ctx", [(i, i ^ bit) for i in range(count)])


class Gather:
    def __init__(self, first, second, count):
        self.count = count
        self.orders = lane_orders(count)
        self.have = [first[None], second[None]]
        self.at = 0
        self.start()

    def start(self):
        self.got = [
            swap(have, order[self.at], self.count)
            for have, order in zip(self.have, self.orders)
        ]
        self.at += 1

    def step(self):
        self.have = [
            jnp.concatenate([have, got], axis=0) for have, got in zip(self.have, self.got)
        ]
        self.start()

    def run(self):
        while self.at < len(self.orders[0]):
            self.step()
        return [self.have[0], self.got[0], self.have[1], self.got[1]]


def add_up(x, y):
    return (x.astype(f32) + y.astype(f32)).astype(bf16)


def fold_kernel(*refs):
    ins, outs = (refs[:8], refs[8:])
    for lane in range(2):
        near, got, near_far, got_far = ins[4 * lane : 4 * lane + 4]
        outs[2 * lane][...] = add_up(near[...], got[...])
        outs[2 * lane + 1][...] = add_up(near_far[...], got_far[...])


def fold(keep, got):
    size, *rest = keep[0].shape
    half = size // 2
    zeros = (0,) * len(rest)
    near = pl.BlockSpec((1, *rest), lambda i: (i,) + zeros)
    far = pl.BlockSpec((1, *rest), lambda i: (i + half,) + zeros)
    out = [jax.ShapeDtypeStruct((half, *rest), bf16)] * 4
    kept_a, sent_a, kept_b, sent_b = pl.pallas_call(
        fold_kernel,
        grid=(half,),
        in_specs=[near, near, far, far] * 2,
        out_specs=[near] * 4,
        out_shape=out,
        compiler_params=params(16 * 1024 * 1024),
        cost_estimate=pl.CostEstimate(flops=int(3e9), bytes_accessed=int(3e6), transcendentals=0),
        name="fold",
    )(keep[0], got[0], keep[0], got[0], keep[1], got[1], keep[1], got[1])
    return [kept_a, kept_b], [sent_a, sent_b]


class Scatter:
    def __init__(self, pieces, count):
        a, a_far, b, b_far = pieces
        self.count = count
        self.orders = [order[::-1] for order in lane_orders(count)]
        self.keep = [a, b]
        self.got = [swap(a_far, 1, count), swap(b_far, 1, count)]
        self.at = 1

    def fold(self):
        self.keep, self.send = fold(self.keep, self.got)

    def start(self):
        self.got = [
            swap(part, order[self.at], self.count)
            for part, order in zip(self.send, self.orders)
        ]
        self.at += 1

    def step(self):
        self.fold()
        self.start()

    def run(self):
        while self.at < len(self.orders[0]):
            self.step()
        return [(keep[0], got[0]) for keep, got in zip(self.keep, self.got)]


def after(values, *others):
    return lax.optimization_barrier((values, others))[0]


def near(slots, lane, step, far):
    return slots[lane, step] < far


def pick(flags, pieces):
    a, a_far, b, b_far = pieces
    return jnp.concatenate(
        [lax.select(flags[0], a[0], a_far[0]), lax.select(flags[1], b[0], b_far[0])], axis=0
    )


def put(flags, outs, rows):
    a, a_far, b, b_far = outs
    half = a.shape[1]
    for flag, near_o, far_o, part in (
        (flags[0], a, a_far, rows[:half]),
        (flags[1], b, b_far, rows[half:]),
    ):

        @pl.when(flag)
        def _():
            near_o[0] = part

        @pl.when(jnp.logical_not(flag))
        def _():
            far_o[0] = part


def prep_kernel(query, key, value, gain_a, gain_f, router, routes, order, out):
    rp = query.shape[0]
    count, _, columns = out.shape
    small = [x[...].astype(f32) for x in (gain_a, gain_f, router)]
    side = jnp.concatenate(small, axis=0).T.astype(bf16)
    tail = jnp.zeros((rp, columns - QKV - side.shape[1]), bf16)
    rows = [x[...].astype(f32) for x in (routes, order)]
    tok = order.shape[1]
    ranks = out.shape[1] - rp
    rows.append(jnp.zeros((ranks - TOP - 1, tok), f32))
    rows = jnp.concatenate(rows, axis=0).astype(bf16)
    rows = jnp.concatenate([rows, jnp.zeros((ranks, columns - tok), bf16)], axis=1)
    for c in range(count):
        g = c * KV // count
        out[c, :rp, :] = jnp.concatenate(
            [
                query[:, g * QW : (g + 1) * QW],
                key[:, g * HD : (g + 1) * HD],
                value[:, g * HD : (g + 1) * HD],
                side,
                tail,
            ],
            axis=1,
        )
        out[c, rp : rp + ranks, :] = rows


def pack_kernel(took, w_out, out):
    count, _, columns = took.shape
    rp, width = w_out.shape
    slab = count * rp
    chunks = width // slab
    for j in range(chunks):
        out[j * rp : (j + 1) * rp, :] = w_out[:, j * slab : (j + 1) * slab]
    rows = took[:, :rp, :].astype(f32).reshape(slab, columns).T
    out[chunks * rp :, :] = rows[: out.shape[0] - chunks * rp].astype(bf16)


def unpack_kernel(shards, rp, where, *refs):
    pieces, (wt_o, gains_o, router_o, rows_o) = (refs[: 2 * shards - 1], refs[2 * shards - 1 :])
    slab = pieces[0].shape[1]
    first = shards * rp
    experts = router_o.shape[0]
    for z in range(shards):

        @pl.when(where[0] == z)
        def _():
            for p in range(shards):
                piece = pieces[p - z + shards - 1]
                columns = slice(p * slab, (p + 1) * slab)
                wt_o[:, columns] = piece[first : first + QKV]
                gains_o[:, columns] = piece[first + QKV : first + QKV + 2].astype(f32)
                router_o[:, columns] = piece[first + QKV + 2 : first + QKV + 2 + experts]
                for j in range(shards):
                    rows_o[p, :, j * slab : (j + 1) * slab] = piece[j * rp : (j + 1) * rp]


def code_kernel(first, table, out, load):
    i = pl.program_id(0)
    tok, experts = out.shape[1:]

    @pl.when(i == 0)
    def _():
        load[...] = jnp.zeros_like(load)

    rows = table[0, first : first + TOP + 1, :tok].astype(f32)
    names = lax.broadcasted_iota(i32, (experts, tok), 0).astype(f32)
    named = jnp.zeros((experts, tok), f32)
    for k in range(TOP):
        named += jnp.where(rows[k : k + 1] == names, 1.0, 0.0)
    ranks = jnp.broadcast_to(rows[TOP : TOP + 1], (tok, tok))
    before = jnp.where(ranks.T < ranks, 1.0, 0.0).astype(bf16)
    slot = dot_nn(named.astype(bf16), before) + load[:, :1]
    out[0] = (named * (1.0 + jnp.where(slot < CAP, 1.0, 0.0))).T
    load[...] += jnp.sum(named, axis=1, keepdims=True)


def qkv_kernel(
    far, slot_ref, xa, xaf, xb, xbf, gain, wt, cos, sin, ain_o, qt_o, k_o, kt_o, v_o, vt_o
):
    i = pl.program_id(0)
    flags = (near(slot_ref, 0, i, far), near(slot_ref, 1, i, far))
    x = pick(flags, (xa, xaf, xb, xbf)).astype(f32)
    inv = lax.rsqrt(jnp.mean(x * x, axis=-1, keepdims=True) + EPS)
    a = (x * inv * gain[...]).astype(bf16)
    ain_o[0] = a
    y = dot_nt(wt[...], a)
    c, s = (cos[0], sin[0])

    def turn(rows):
        lo, hi = (rows[:HALF], rows[HALF:])
        return jnp.concatenate([lo * c - hi * s, hi * c + lo * s], axis=0)

    for h in range(GROUP):
        q = turn(y[h * HD : (h + 1) * HD]).astype(bf16).astype(f32) * SCORE_SCALE
        qt_o[0, h * HD : (h + 1) * HD, :] = q.astype(bf16)
    k = turn(y[QW : QW + HD])
    kt_o[0] = k.astype(bf16)
    k_o[0] = k.T.astype(bf16)
    v = y[QW + HD :]
    vt_o[0] = v.astype(bf16)
    v_o[0] = v.T.astype(bf16)


def heads_wide(rows):
    return jnp.concatenate([rows[h * HD : (h + 1) * HD] for h in range(GROUP)], axis=1)


def causal(shape, width):
    key = lax.broadcasted_iota(i32, shape, 0)
    query = lax.broadcasted_iota(i32, shape, 1)
    for _ in range(GROUP - 1):
        query = jnp.where(query >= width, query - width, query)
    return key <= query


def attn_fwd_kernel(qt, k, vt, of_o, ob_o, lse_o):
    a = pl.program_id(0)
    tok = qt.shape[2]
    q = heads_wide(qt[0])
    s = dot_nn(k[a], q)
    s = jnp.where(causal(s.shape, tok), s, NEG_FILL)
    m = jnp.max(s, axis=0, keepdims=True)
    p = jnp.exp(s - m)
    l = jnp.sum(p, axis=0, keepdims=True)
    o = dot_nn(vt[a], p.astype(bf16))

    def step(b, carry):
        m, l, o = carry
        s = dot_nn(k[b], q)
        new = jnp.maximum(m, jnp.max(s, axis=0, keepdims=True))
        p = jnp.exp(s - new)
        back = jnp.exp(m - new)
        l = l * back + jnp.sum(p, axis=0, keepdims=True)
        o = o * back + dot_nn(vt[b], p.astype(bf16))
        return (new, l, o)

    m, l, o = lax.fori_loop(0, a, step, (m, l, o))
    o = o / l
    lse_o[0] = m + jnp.log(l)
    for h in range(GROUP):
        part = o[:, h * tok : (h + 1) * tok]
        of_o[0, h * HD : (h + 1) * HD, :] = part
        ob_o[0, h * HD : (h + 1) * HD, :] = part.astype(bf16)


def attn_bwd_kernel(qt, dot_, of, lse, k, kt, v, cos, sin, dq_o, dk_o, dv_o, dk_s, dv_s):
    a = pl.program_id(0)
    tok = qt.shape[2]
    count = k.shape[0]
    q = heads_wide(qt[0])
    do = heads_wide(dot_[0])
    delta = jnp.sum(do.astype(f32) * heads_wide(of[0]), axis=0, keepdims=True)
    total = lse[0]

    def pair(b, mask):
        s = dot_nn(k[b], q)
        p = jnp.exp(s - total)
        if mask:
            p = jnp.where(causal(s.shape, tok), p, 0.0)
        dp = dot_nn(v[b], do)
        ds = (p * (dp - delta)).astype(bf16)
        return dot_nt(ds, q), dot_nt(p.astype(bf16), do), dot_nn(kt[b], ds)

    dk, dv, dq = pair(a, True)
    dk_s[a] = dk
    dv_s[a] = dv

    def step(b, dq):
        dk, dv, more = pair(b, False)
        dk_s[b] += dk
        dv_s[b] += dv
        return dq + more

    dq = lax.fori_loop(0, a, step, dq) * SCORE_SCALE

    def back(rows, c, s):
        lo, hi = (rows[:HALF], rows[HALF:])
        return jnp.concatenate([lo * c + hi * s, hi * c - lo * s], axis=0)

    for h in range(GROUP):
        dq_o[0, h * HD : (h + 1) * HD, :] = back(
            dq[:, h * tok : (h + 1) * tok], cos[a], sin[a]
        ).astype(bf16)

    @pl.when(a == count - 1)
    def _():
        @pl.loop(0, count)
        def _(b):
            dk_o[b] = back(dk_s[b].T, cos[b], sin[b]).astype(bf16)
            dv_o[b] = dv_s[b].T.astype(bf16)


def qkv_grads_kernel(share, dq, dk, dv, ain, wt, gain, gw_o, gg_o, acc):
    i = pl.program_id(0)
    d = jnp.concatenate([dq[0], dk[0], dv[0]], axis=0)

    @pl.when(i == 0)
    def _():
        acc[...] = jnp.zeros_like(acc)

    acc[...] += dot_nn(d, ain[0])

    @pl.when(i == pl.num_programs(0) - 1)
    def _():
        width = gw_o.shape[2]
        for z in range(gw_o.shape[0]):
            gw_o[z] = acc[:, z * width : (z + 1) * width].astype(bf16)
        total = jnp.sum(acc[...] * wt[...].astype(f32), axis=0, keepdims=True)
        gg_o[...] = total * share / gain[...]


def qkv_back_kernel(share, far, blocks_ref, dqa, dka, dva, dqb, dkb, dvb, wt, *outs):
    i = pl.program_id(0)
    flags = (i < far, i < far)
    d = jnp.concatenate(
        [
            jnp.concatenate([dqa[0], dka[0], dva[0]], axis=0),
            jnp.concatenate([dqb[0], dkb[0], dvb[0]], axis=0),
        ],
        axis=1,
    )
    put(flags, outs, (dot_tn(d, wt[...]) * share).astype(bf16))


def bundle_kernel(gw, gain_a, gain_f, router, p0, p1, q0, q1, out):
    shards, rows, slab = out.shape
    half, rp, _ = p0.shape
    first = shards * rp
    small = jnp.concatenate([gain_a[...], gain_f[...], router[...]], axis=0).astype(bf16)
    count = small.shape[0]
    for z in range(shards):
        near, got = (p0, p1) if z < half else (q0, q1)
        w_out = add_up(near[z % half], got[z % half])
        for j in range(shards):
            out[z, j * rp : (j + 1) * rp, :] = w_out[:, j * slab : (j + 1) * slab]
        out[z, first : first + QKV, :] = gw[z]
        out[z, first + QKV : first + QKV + count, :] = small[:, z * slab : (z + 1) * slab]
        rest = first + QKV + count
        if rest < rows:
            out[z, rest:, :] = jnp.zeros((rows - rest, slab), bf16)


def share_kernel(own, send, w_out_o):
    count, rp, columns = send.shape
    shards = w_out_o.shape[1] // own.shape[1]
    slab = own.shape[1]
    first = shards * rp
    for j in range(shards):
        w_out_o[:, j * slab : (j + 1) * slab] = own[j * rp : (j + 1) * rp, :].astype(f32)
    rows = own[first:, :].astype(f32)
    rows = jnp.concatenate([rows, jnp.zeros((columns - rows.shape[0], slab), f32)], axis=0)
    send[...] = rows.T.reshape(count, rp, columns).astype(bf16)


def finish_kernel(copies, given, query, key, value, sums):
    count = given.shape[0]
    parts = [given[c].astype(f32) for c in range(count)]
    for c in range(0, count, copies):
        g = c // copies
        query[:, g * QW : (g + 1) * QW] = parts[c][:, :QW]
        key[:, g * HD : (g + 1) * HD] = parts[c][:, QW : QW + HD]
        value[:, g * HD : (g + 1) * HD] = parts[c][:, QW + HD : QKV]
    total = parts[0][:, QKV:]
    for part in parts[1:]:
        total = total + part[:, QKV:]
    sums[...] = total[:, : sums.shape[1]]


def expert_terms(expert, x, y, router, code, w_gate, w_up, w_down):
    logits = dot_nt(x, router)
    named = code > 0.5
    logits = jnp.where(named, logits, NEG_FILL)
    top = jnp.max(logits, axis=-1, keepdims=True)
    raised = jnp.where(named, jnp.exp(logits - top), 0.0)
    gates = raised / jnp.sum(raised, axis=-1, keepdims=True)
    mine = (lax.broadcasted_iota(i32, gates.shape, 1) == expert) & (code > 1.5)
    weight = RESIDUAL_SCALE * jnp.sum(jnp.where(mine, gates, 0.0), axis=-1, keepdims=True)
    kept = RESIDUAL_SCALE * jnp.sum(jnp.where(mine, 1.0, 0.0), axis=-1, keepdims=True)

    gate_pre = dot_nn(x, w_gate)
    up_pre = dot_nn(x, w_up)
    back = dot_nn(y, w_down)
    sig = jax.nn.sigmoid(gate_pre)
    act = gate_pre * sig
    inner = act * up_pre
    gate_grad = kept * jnp.sum(inner * back, axis=-1, keepdims=True)
    inner_w = (inner * weight).astype(bf16)
    d_inner = back * weight
    d_gate = (d_inner * up_pre * sig * (1.0 + gate_pre * (1.0 - sig))).astype(bf16)
    d_up = (d_inner * act).astype(bf16)
    din = dot_nt(d_gate, w_gate) + dot_nt(d_up, w_up)
    high = gate_grad.astype(bf16).astype(f32)
    low = (gate_grad - high).astype(bf16).astype(f32)
    lane = lax.broadcasted_iota(i32, (x.shape[0], EXTRA), 1)
    side = jnp.where(lane == expert, high, 0.0) + jnp.where(lane == expert + LOW, low, 0.0)
    return inner_w, d_gate, d_up, jnp.concatenate([din, side], axis=1)


def weight_of(weights, which):
    shards, _, depth, ff = weights.shape
    return weights[:, which].reshape(shards * depth, ff)


def clear(accs, i):
    @pl.when(i == 0)
    def _():
        for acc in accs:
            acc[...] = jnp.zeros_like(acc)


def flush(accs, grad_o, i):
    @pl.when(i == pl.num_programs(0) - 1)
    def _():
        shards, _, depth, _ = grad_o.shape
        for which, acc in enumerate(accs):
            for z in range(shards):
                grad_o[z, which] = acc[z * depth : (z + 1) * depth, :].astype(bf16)


def moe_first_kernel(far, which, blocks, *refs):
    xs, ys, (router, code_a, code_b, weights) = (refs[:4], refs[4:8], refs[8:12])
    outs, (b_o, grad_o), accs = (refs[12:16], refs[16:18], refs[18:])
    i = pl.program_id(0)
    flags = (i < far, i < far)
    x, y = (pick(flags, xs), pick(flags, ys))
    code = jnp.concatenate([code_a[0], code_b[0]], axis=0)
    inner_w, d_gate, d_up, din = expert_terms(
        which[0], x, y, router[...], code, *[weight_of(weights, m) for m in range(3)]
    )
    put(flags, outs, din.astype(bf16))
    b_o[0] = inner_w
    clear(accs, i)
    accs[0][...] += dot_tn(x, d_gate)
    accs[1][...] += dot_tn(x, d_up)
    accs[2][...] += dot_tn(y, inner_w)
    flush(accs, grad_o, i)


def moe_second_kernel(far, which, blocks, *refs):
    xs, ys, (router, code_a, code_b, weights) = (refs[:4], refs[4:8], refs[8:12])
    prev, outs, (b_o, dg_o, du_o) = (refs[12:16], refs[16:20], refs[20:])
    i = pl.program_id(0)
    flags = (i < far, i < far)
    x, y = (pick(flags, xs), pick(flags, ys))
    code = jnp.concatenate([code_a[0], code_b[0]], axis=0)
    inner_w, d_gate, d_up, din = expert_terms(
        which[0], x, y, router[...], code, *[weight_of(weights, m) for m in range(3)]
    )
    put(flags, outs, (din + pick(flags, prev).astype(f32)).astype(bf16))
    b_o[0] = inner_w
    dg_o[0] = d_gate
    du_o[0] = d_up


def moe_grads_kernel(far, *refs):
    xs, ys, (b, dg, du), grad_o, accs = (refs[:4], refs[4:8], refs[8:11], refs[11], refs[12:])
    i = pl.program_id(0)
    flags = (i < far, i < far)
    x, y = (pick(flags, xs), pick(flags, ys))
    clear(accs, i)
    accs[0][...] += dot_tn(x, dg[0])
    accs[1][...] += dot_tn(x, du[0])
    accs[2][...] += dot_tn(y, b[0])
    flush(accs, grad_o, i)


def moe_out_kernel(far, b0, b1, w0, w1, *outs):
    i = pl.program_id(0)
    flags = (i < far, i < far)
    out = dot_nt(b0[0], weight_of(w0, 0)) + dot_nt(b1[0], weight_of(w1, 0))
    put(flags, outs, out.astype(bf16))


def place_kernel(far, slot_ref, a, af, b, bf, out):
    i = pl.program_id(0)
    flags = (near(slot_ref, 0, i, far), near(slot_ref, 1, i, far))
    half = a.shape[1]
    for z in range(half):
        out[z, 0] = lax.select(flags[0], a[0, z], af[0, z])
        out[half + z, 0] = lax.select(flags[1], b[0, z], bf[0, z])


def after_attn_kernel(attn, w_out, hidden, gain, resid_o, ma_o, mb_o):
    resid = hidden[...].astype(f32) + RESIDUAL_SCALE * dot_tn(attn[...], w_out[...])
    resid_o[...] = resid
    inv = lax.rsqrt(jnp.mean(resid * resid, axis=-1, keepdims=True) + EPS)
    moe_in = (resid * inv * gain[...]).astype(bf16)
    half = ma_o.shape[1]
    ma_o[0] = moe_in[:half]
    mb_o[0] = moe_in[half:]


def before_attn_kernel(
    a0, a1, b0, b1, resid, ma, mb, grad_out, code, router, gain, w_out,
    d_resid_o, d_branch_o, d_attn_o, d_router_o, d_gain_o,
):
    width = resid.shape[1]
    experts = router.shape[0]
    back = jnp.concatenate(
        [
            a0[...].astype(f32) + a1[...].astype(f32),
            b0[...].astype(f32) + b1[...].astype(f32),
        ],
        axis=0,
    )
    moe_in = jnp.concatenate([ma[0], mb[0]], axis=0)
    chosen = code[...] > 0.5
    logits = jnp.where(chosen, dot_nt(moe_in, router[...]), NEG_FILL)
    raised = jnp.where(chosen, jnp.exp(logits - jnp.max(logits, axis=-1, keepdims=True)), 0.0)
    gates = raised / jnp.sum(raised, axis=-1, keepdims=True)
    gate_grad = (
        back[:, width : width + experts] + back[:, width + LOW : width + LOW + experts]
    )
    logit_grad = gates * (gate_grad - jnp.sum(gates * gate_grad, axis=-1, keepdims=True))
    dlogits = logit_grad.astype(bf16)
    d_router_o[...] = dot_tn(dlogits, moe_in)
    d_moe_in = back[:, :width] + dot_nn(dlogits, router[...])
    r = resid[...]
    inv = lax.rsqrt(jnp.mean(r * r, axis=-1, keepdims=True) + EPS)
    normed = r * inv
    d_gain_o[...] = jnp.sum(d_moe_in * normed, axis=0, keepdims=True)
    d_normed = d_moe_in * gain[...]
    d_resid = grad_out[...].astype(f32) + inv * (
        d_normed - normed * jnp.mean(d_normed * normed, axis=-1, keepdims=True)
    )
    d_resid_o[...] = d_resid
    d_branch = (RESIDUAL_SCALE * d_resid).astype(bf16)
    d_branch_o[...] = d_branch
    d_attn_o[...] = dot_nt(w_out[...], d_branch).astype(bf16)


def wout_grad_kernel(far, slot_ref, attn, d_branch, a, af, b, bf):
    n2, half, rp, width = a.shape
    n = 2 * n2
    d = d_branch[...]
    for z in range(2 * half):
        rows = dot_nn(attn[z * n * rp : (z + 1) * n * rp, :], d).astype(bf16)
        lane = 0 if z < half else 1
        near_o, far_o = ((a, af), (b, bf))[lane]
        for c in range(n):
            part = rows[c * rp : (c + 1) * rp]
            slot = slot_ref[lane, c]

            @pl.when(slot < far)
            def _():
                near_o[slot, z % half] = part

            @pl.when(slot >= far)
            def _():
                far_o[slot - far, z % half] = part


def last_kernel(a0, a1, b0, b1, d_resid, hidden, gain, out):
    d = jnp.concatenate(
        [
            a0[...].astype(f32) + a1[...].astype(f32),
            b0[...].astype(f32) + b1[...].astype(f32),
        ],
        axis=0,
    )
    x = hidden[...].astype(f32)
    inv = lax.rsqrt(jnp.mean(x * x, axis=-1, keepdims=True) + EPS)
    normed = x * inv
    d = d * gain[...]
    out[...] = d_resid[...] + inv * (
        d - normed * jnp.mean(d * normed, axis=-1, keepdims=True)
    )


def whole(shape):
    zeros = (0,) * len(shape)
    return pl.BlockSpec(shape, lambda *at: zeros)


def at_step(shape):
    zeros = (0,) * (len(shape) - 1)
    return pl.BlockSpec(shape, lambda i, *refs: (i,) + zeros)


def lanes_at_step(shape, far):
    zeros = (0,) * (len(shape) - 1)
    first = pl.BlockSpec(shape, lambda i, *refs: (jnp.minimum(i, far - 1),) + zeros)
    second = pl.BlockSpec(shape, lambda i, *refs: (jnp.maximum(i - far, 0),) + zeros)
    return [first, second, first, second]


def lanes_at_slot(shape, far):
    zeros = (0,) * (len(shape) - 1)

    def spec(lane, second):
        def index(i, slots):
            slot = slots[lane, i]
            slot = jnp.maximum(slot - far, 0) if second else jnp.minimum(slot, far - 1)
            return (slot,) + zeros

        return pl.BlockSpec(shape, index)

    return [spec(0, False), spec(0, True), spec(1, False), spec(1, True)]


def shape_of(*dims, dtype=bf16):
    return jax.ShapeDtypeStruct(dims, dtype)


def micros(us):
    return pl.CostEstimate(
        flops=int(us * 1.1e9), bytes_accessed=int(us * 1e6), transcendentals=0
    )


def call(kernel, name, us, out_shape, operands, *, grid=None, specs=None, out_specs=None,
         scratch=(), tables=(), limit=58):
    if grid is None:
        specs = [whole(x.shape) for x in operands]
        out_specs = jax.tree.map(lambda x: whole(x.shape), out_shape)
        grid = 1
    return pl.pallas_call(
        kernel,
        grid_spec=pltpu.PrefetchScalarGridSpec(
            num_scalar_prefetch=len(tables),
            grid=(grid,),
            in_specs=specs,
            out_specs=out_specs,
            scratch_shapes=list(scratch),
        ),
        out_shape=out_shape,
        compiler_params=params(limit * 1024 * 1024),
        cost_estimate=micros(us),
        name=name,
    )(*tables, *operands)


def shards(
    hidden,
    gain_attn,
    w_query,
    w_key,
    w_value,
    w_out,
    gain_ffn,
    router,
    routes,
    slot_order,
    w_gate,
    w_up,
    w_down,
    grad_out,
):
    tok, width = hidden.shape
    n = lax.axis_size("ctx")
    dp = lax.axis_size("dp")
    me = lax.axis_index("ctx")
    copies = n // KV
    far = n // 2
    rp = w_query.shape[0]
    slab = rp * n
    experts = router.shape[1]
    half = tok // 2
    ff = w_gate.shape[2]
    depth = w_gate.shape[1]
    orders = lane_orders(n)
    slots = [slots_of(order) for order in orders]
    blocks = jnp.array(slots, i32) ^ me
    inverse = jnp.array([[lane.index(j) for j in range(n)] for lane in slots], i32)
    slot_at = jnp.take(inverse, jnp.arange(n, dtype=i32) ^ me, axis=1)


    side = QKV + 2 + experts
    pad = -(side + rp * dp) % 16
    send = call(
        prep_kernel,
        "prep",
        2,
        shape_of(n, rp + 16, max(slab, tok, -(-side // 128) * 128)),
        [
            w_query,
            w_key,
            w_value,
            gain_attn[None],
            gain_ffn[None],
            router.T,
            routes.T,
            slot_order,
        ],
        limit=58,
    )
    took = lax.all_to_all(send, "ctx", split_axis=0, concat_axis=0, tiled=True)
    pack = call(
        pack_kernel,
        "pack",
        2,
        shape_of(side + rp * dp, slab),
        [took, w_out],
        limit=58,
    )

    def along(value, by):
        pairs = [(z, z + by) for z in range(dp) if 0 <= z + by < dp]
        return lax.ppermute(value, "dp", pairs)

    below, above = ([], [])
    for _ in range(dp - 1):
        below.append(along(below[-1] if below else pack, 1))
        above.append(along(above[-1] if above else pack, -1))
    wt, gains, router_t, out_rows = call(
        functools.partial(unpack_kernel, dp, rp),
        "unpack",
        2,
        [
            shape_of(QKV, width),
            shape_of(2, width, dtype=f32),
            shape_of(experts, width),
            shape_of(dp, rp, width),
        ],
        [*below[::-1], pack, *above],
        grid=1,
        specs=[whole(pack.shape)] * (2 * dp - 1),
        out_specs=[
            whole((QKV, width)),
            whole((2, width)),
            whole((experts, width)),
            whole((dp, rp, width)),
        ],
        tables=[lax.axis_index("dp").reshape(1).astype(i32)],
        limit=58,
    )
    gain_a, gain_f = (gains[0:1], gains[1:2])

    stacks = [jnp.stack([w_gate[e], w_up[e], w_down[e]]) for e in range(w_gate.shape[0])]
    stacks = after(stacks, below[:-1], above[:-1])
    expert_w = [lax.all_gather(stack, "dp", axis=0) for stack in stacks]

    x_rows = after(hidden, took)
    x_rows = Gather(x_rows[:half], x_rows[half:], n)
    xs = x_rows.run()
    y_rows = after(grad_out, x_rows.have)
    y_rows = Gather(y_rows[:half], y_rows[half:], n)

    exponents = jnp.arange(HALF, dtype=f32) * (2.0 / HD)
    inverse_freq = jnp.power(10000.0, -exponents)
    positions = jnp.arange(n * tok, dtype=f32).reshape(n, 1, tok)
    angles = positions * inverse_freq[None, :, None]
    cos, sin = (jnp.cos(angles), jnp.sin(angles))

    o_rows = Gather(out_rows[: dp // 2], out_rows[dp // 2 :], n)
    gain_a, y_rows.got = after((gain_a, y_rows.got))

    ain, qt, k, kt, v, vt = call(
        functools.partial(qkv_kernel, far),
        "qkv",
        6,
        [
            shape_of(n, tok, width),
            shape_of(n, QW, tok),
            shape_of(n, tok, HD),
            shape_of(n, HD, tok),
            shape_of(n, tok, HD),
            shape_of(n, HD, tok),
        ],
        [*xs, gain_a, wt, cos, sin],
        grid=n,
        specs=lanes_at_slot((1, half, width), far)
        + [whole((1, width)), whole((QKV, width))]
        + [at_step((1, HALF, tok))] * 2,
        out_specs=[
            at_step((1, tok, width)),
            at_step((1, QW, tok)),
            at_step((1, tok, HD)),
            at_step((1, HD, tok)),
            at_step((1, tok, HD)),
            at_step((1, HD, tok)),
        ],
        tables=[slot_at],
        limit=58,
    )

    qt, y_rows.have, y_rows.got, o_rows.have, o_rows.got = after(
        (qt, y_rows.have, y_rows.got, o_rows.have, o_rows.got)
    )
    y_rows.step()
    o_rows.step()
    qt = after(qt, y_rows.have, o_rows.have)
    of, attn_t, lse = call(
        attn_fwd_kernel,
        "attn_fwd",
        19,
        [
            shape_of(n, QW, tok, dtype=f32),
            shape_of(n, QW, tok),
            shape_of(n, 1, GROUP * tok, dtype=f32),
        ],
        [qt, k, vt],
        grid=n,
        specs=[at_step((1, QW, tok)), whole((n, tok, HD)), whole((n, HD, tok))],
        out_specs=[at_step((1, QW, tok))] * 2 + [at_step((1, 1, GROUP * tok))],
        limit=58,
    )

    attn_t, y_rows.got, o_rows.got = after((attn_t, y_rows.got, o_rows.got))
    os = o_rows.run()
    ys = y_rows.run()
    attn_b = lax.all_to_all(attn_t, "ctx", split_axis=0, concat_axis=0, tiled=True)
    attn_b = attn_b[::copies].reshape(KV * QW, tok)

    w_out_all = call(
        functools.partial(place_kernel, far),
        "place",
        4,
        shape_of(dp, n, rp, width),
        os,
        grid=n,
        specs=lanes_at_slot((1, dp // 2, rp, width), far),
        out_specs=pl.BlockSpec((dp, 1, rp, width), lambda i, slots: (0, i, 0, 0)),
        tables=[slot_at],
        limit=58,
    ).reshape(KV * QW, width)

    resid, ma, mb = call(
        after_attn_kernel,
        "after_attn",
        6,
        [shape_of(tok, width, dtype=f32)] + [shape_of(1, half, width)] * 2,
        [attn_b, w_out_all, hidden, gain_f],
        limit=58,
    )
    m_rows = Gather(ma[0], mb[0], n)
    took = after(took, ma)

    code = call(
        functools.partial(code_kernel, rp),
        "code",
        6,
        shape_of(n, tok, experts, dtype=f32),
        [took],
        grid=n,
        specs=[at_step((1,) + took.shape[1:])],
        out_specs=at_step((1, tok, experts)),
        scratch=[pltpu.VMEM((experts, 1), f32)],
        limit=58,
    )
    code_mine = lax.dynamic_index_in_dim(code, me, 0, keepdims=False)

    m_rows.got, code, code_mine = after((m_rows.got, code, code_mine))
    ms = m_rows.run()

    side_w = width + EXTRA
    wide = [shape_of(far, half, side_w)] * 4
    rows_in = lanes_at_step((1, half, width), far) * 2 + [
        whole((experts, width)),
        *[
            pl.BlockSpec((1, half, experts), lambda i, which, blocks, lane=lane: (blocks[lane, i], lane, 0))
            for lane in range(2)
        ],
        whole((dp, 3, depth, ff)),
    ]
    hidden_o = [at_step((1, tok, ff))]
    hidden_s = [shape_of(n, tok, ff)]
    accs = [pltpu.VMEM((width, ff), f32)] * 3
    first = (me * len(expert_w)).reshape(1).astype(i32)
    *din, inner_0, grads_0 = call(
        functools.partial(moe_first_kernel, far),
        "moe_first",
        38,
        wide + hidden_s + [shape_of(dp, 3, depth, ff)],
        [*ms, *ys, router_t, code, code, expert_w[0]],
        grid=n,
        specs=rows_in,
        out_specs=lanes_at_step((1, half, side_w), far) + hidden_o + [whole((dp, 3, depth, ff))],
        scratch=accs,
        tables=[first, blocks],
        limit=58,
    )
    *din, inner_1, d_gate_1, d_up_1 = call(
        functools.partial(moe_second_kernel, far),
        "moe_second",
        25,
        wide + hidden_s * 3,
        [*ms, *ys, router_t, code, code, expert_w[1], *din],
        grid=n,
        specs=rows_in + lanes_at_step((1, half, side_w), far),
        out_specs=lanes_at_step((1, half, side_w), far) + hidden_o * 3,
        tables=[first + 1, blocks],
        limit=58,
    )
    back = Scatter(din, n)
    back.step()
    inner_1 = after(inner_1, back.keep)
    grads_1 = call(
        functools.partial(moe_grads_kernel, far),
        "moe_grads",
        15,
        shape_of(dp, 3, depth, ff),
        [*ms, *ys, inner_1, d_gate_1, d_up_1],
        grid=n,
        specs=lanes_at_step((1, half, width), far) * 2 + hidden_o * 3,
        out_specs=whole((dp, 3, depth, ff)),
        scratch=accs,
        limit=58,
    )
    expert_grads = [
        lax.psum_scatter(grads, "dp", scatter_dimension=0, tiled=True)
        for grads in (grads_0, grads_1)
    ]

    back.got = after(back.got, grads_1)
    (a0, a1), (b0, b1) = back.run()
    inner_1 = after(inner_1, back.keep)
    down = pl.BlockSpec((dp, 1, depth, ff), lambda i: (0, 2, 0, 0))
    outs = call(
        functools.partial(moe_out_kernel, far),
        "moe_out",
        8,
        [shape_of(far, half, width)] * 4,
        [inner_0, inner_1, *expert_w],
        grid=n,
        specs=hidden_o * 2 + [down] * 2,
        out_specs=lanes_at_step((1, half, width), far),
        limit=58,
    )
    mix = Scatter(outs, n)
    resid_in = after(resid, outs)
    d_resid, d_branch, d_attn, d_router, d_gain_ffn = call(
        before_attn_kernel,
        "before_attn",
        14,
        [
            shape_of(tok, width, dtype=f32),
            shape_of(tok, width),
            shape_of(KV * QW, tok),
            shape_of(experts, width, dtype=f32),
            shape_of(1, width, dtype=f32),
        ],
        [a0, a1, b0, b1, resid_in, ma, mb, grad_out, code_mine, router_t, gain_f, w_out_all],
        limit=58,
    )
    d_heads = lax.all_to_all(
        jnp.repeat(d_attn.reshape(KV, QW, tok), copies, axis=0),
        "ctx",
        split_axis=0,
        concat_axis=0,
        tiled=True,
    )
    d_wout = call(
        functools.partial(wout_grad_kernel, far),
        "wout_grad",
        6,
        [shape_of(far, dp // 2, rp, width)] * 4,
        [attn_b, d_branch],
        grid=1,
        specs=[whole((KV * QW, tok)), whole((tok, width))],
        out_specs=[whole((far, dp // 2, rp, width))] * 4,
        tables=[slot_at],
        limit=58,
    )

    mix.fold()
    mix.send, mix.keep, d_heads, expert_grads[0] = after(
        (mix.send, mix.keep, d_heads, expert_grads[0])
    )
    mix.start()
    wout = Scatter(after(d_wout, d_heads), n)
    dq, dk, dv = call(
        attn_bwd_kernel,
        "attn_bwd",
        40,
        [shape_of(n, QW, tok), shape_of(n, HD, tok), shape_of(n, HD, tok)],
        [qt, d_heads, of, lse, k, kt, v, cos, sin],
        grid=n,
        specs=[
            at_step((1, QW, tok)),
            at_step((1, QW, tok)),
            at_step((1, QW, tok)),
            at_step((1, 1, GROUP * tok)),
            whole((n, tok, HD)),
            whole((n, HD, tok)),
            whole((n, tok, HD)),
            whole((n, HALF, tok)),
            whole((n, HALF, tok)),
        ],
        out_specs=[at_step((1, QW, tok)), whole((n, HD, tok)), whole((n, HD, tok))],
        scratch=[pltpu.VMEM((n, tok, HD), f32), pltpu.VMEM((n, tok, HD), f32)],
        limit=58,
    )

    dq, wout.keep, wout.got = after((dq, wout.keep, wout.got))
    wout.step()
    dq = after(dq, wout.keep)

    gw, d_gain_attn = call(
        functools.partial(qkv_grads_kernel, 1.0 / copies),
        "qkv_grads",
        20,
        [shape_of(dp, QKV, slab), shape_of(1, width, dtype=f32)],
        [dq, dk, dv, ain, wt, gain_a],
        grid=n,
        specs=[
            at_step((1, QW, tok)),
            at_step((1, HD, tok)),
            at_step((1, HD, tok)),
            at_step((1, tok, width)),
            whole((QKV, width)),
            whole((1, width)),
        ],
        out_specs=[whole((dp, QKV, slab)), whole((1, width))],
        scratch=[pltpu.VMEM((QKV, width), f32)],
        limit=30,
    )

    def columns(rows, lane):
        return pl.BlockSpec((1, rows, half), lambda i, blocks: (blocks[lane, i], 0, lane))

    dq, wout.keep, wout.got, mix.keep, mix.got = after(
        (dq, wout.keep, wout.got, mix.keep, mix.got), gw
    )
    wout.step()
    mix.step()
    dq = after(dq, wout.keep, mix.keep)
    d_in = call(
        functools.partial(qkv_back_kernel, 1.0 / copies, far),
        "qkv_back",
        20,
        [shape_of(far, half, width)] * 4,
        [dq, dk, dv, dq, dk, dv, wt],
        grid=n,
        specs=[columns(rows, lane) for lane in range(2) for rows in (QW, HD, HD)]
        + [whole((QKV, width))],
        out_specs=lanes_at_step((1, half, width), far),
        tables=[blocks],
        limit=30,
    )

    wout.got = after(wout.got, d_in)
    (p0, p1), (q0, q1) = wout.run()
    bundle = call(
        bundle_kernel,
        "bundle",
        2,
        shape_of(dp, side + rp * dp + pad, slab),
        [gw, d_gain_attn, d_gain_ffn, d_router, p0, p1, q0, q1],
        limit=30,
    )
    own = lax.psum_scatter(bundle, "dp", scatter_dimension=0, tiled=True)[0]
    send, grad_out_proj = call(
        share_kernel,
        "share",
        2,
        [shape_of(n, rp, -(-(side + pad) // 128) * 128), shape_of(rp, width, dtype=f32)],
        [own],
        limit=30,
    )
    given = lax.all_to_all(send, "ctx", split_axis=0, concat_axis=0, tiled=True)
    grad_query, grad_key, grad_value, sums = call(
        functools.partial(finish_kernel, copies),
        "finish",
        2,
        [
            shape_of(rp, KV * QW, dtype=f32),
            shape_of(rp, KV * HD, dtype=f32),
            shape_of(rp, KV * HD, dtype=f32),
            shape_of(rp, 2 + experts, dtype=f32),
        ],
        [given],
        limit=30,
    )

    back_in = Scatter(d_in, n)
    back_in.got = after(back_in.got, bundle)
    back_in.step()
    expert_grads, mix.got = after((expert_grads, mix.got), back_in.keep)
    (c0, c1), (e0, e1) = back_in.run()
    d_hidden = call(
        last_kernel,
        "last",
        3,
        shape_of(tok, width, dtype=f32),
        [c0, c1, e0, e1, after(d_resid, send), hidden, gain_a],
        limit=30,
    )

    (r0, r1), (s0, s1) = mix.run()
    mixed = jnp.concatenate(
        [r0.astype(f32) + r1.astype(f32), s0.astype(f32) + s1.astype(f32)], axis=0
    )
    output = (resid + mixed).astype(bf16)

    expert_grads = jnp.concatenate(expert_grads, axis=0).astype(f32)
    return (
        output,
        d_hidden,
        sums[:, 0],
        grad_query,
        grad_key,
        grad_value,
        grad_out_proj,
        sums[:, 1],
        sums[:, 2:],
        expert_grads[:, 0],
        expert_grads[:, 1],
        expert_grads[:, 2],
    )


def solution(mesh):
    rows = P(("dp", "ctx"), None)
    flat = P(("dp", "ctx"))
    expert = P("ctx", "dp", None)
    return jax.shard_map(
        shards,
        mesh=mesh,
        in_specs=(
            rows,
            flat,
            rows,
            rows,
            rows,
            rows,
            flat,
            rows,
            rows,
            rows,
            expert,
            expert,
            expert,
            rows,
        ),
        out_specs=(
            rows,
            rows,
            flat,
            rows,
            rows,
            rows,
            rows,
            flat,
            rows,
            expert,
            expert,
            expert,
        ),
        check_vma=False,
    )
```

```python
import functools

import jax
import jax.numpy as jnp
from jax import lax
from jax.experimental import pallas as pl
from jax.experimental.pallas import tpu as pltpu
from jax.sharding import PartitionSpec as P

H = 24
KV = 8
HD = 64
TOP = 8
CAP = 1024

EPS = 1e-06
NEG_FILL = -1e30
SCORE_SCALE = 0.015625
RESIDUAL_SCALE = 0.22

GROUP = H // KV
HALF = HD // 2
QW = GROUP * HD
QKV = QW + 2 * HD
LOW = 64
EXTRA = 128

f32 = jnp.float32
bf16 = jnp.bfloat16
i32 = jnp.int32
VMEM_LIMIT = 58 * 1024 * 1024


def dot_nn(a, b):
    return lax.dot_general(a, b, (((1,), (0,)), ((), ())), preferred_element_type=f32)


def dot_nt(a, b):
    return lax.dot_general(a, b, (((1,), (1,)), ((), ())), preferred_element_type=f32)


def dot_tn(a, b):
    return lax.dot_general(a, b, (((0,), (0,)), ((), ())), preferred_element_type=f32)


def params(limit=VMEM_LIMIT):
    return pltpu.CompilerParams(dimension_semantics=("arbitrary",), vmem_limit_bytes=limit)


def lane_orders(count):
    bits = []
    bit = 2
    while bit < count:
        bits.append(bit)
        bit *= 2
    return (bits[::-1] + [1], bits + [1])


def slots_of(order):
    slots = [0]
    for bit in order:
        slots = slots + [s ^ bit for s in slots]
    return slots


def swap(value, bit, count):
    return lax.ppermute(value, "ctx", [(i, i ^ bit) for i in range(count)])


class Gather:
    def __init__(self, first, second, count):
        self.count = count
        self.orders = lane_orders(count)
        self.have = [first[None], second[None]]
        self.at = 0
        self.start()

    def start(self):
        self.got = [
            swap(have, order[self.at], self.count)
            for have, order in zip(self.have, self.orders)
        ]
        self.at += 1

    def step(self):
        self.have = [
            jnp.concatenate([have, got], axis=0) for have, got in zip(self.have, self.got)
        ]
        self.start()

    def run(self):
        while self.at < len(self.orders[0]):
            self.step()
        return [self.have[0], self.got[0], self.have[1], self.got[1]]


def add_up(x, y):
    return (x.astype(f32) + y.astype(f32)).astype(bf16)


def fold_kernel(*refs):
    ins, outs = (refs[:8], refs[8:])
    for lane in range(2):
        near, got, near_far, got_far = ins[4 * lane : 4 * lane + 4]
        outs[2 * lane][...] = add_up(near[...], got[...])
        outs[2 * lane + 1][...] = add_up(near_far[...], got_far[...])


def fold(keep, got):
    size, *rest = keep[0].shape
    half = size // 2
    zeros = (0,) * len(rest)
    near = pl.BlockSpec((1, *rest), lambda i: (i,) + zeros)
    far = pl.BlockSpec((1, *rest), lambda i: (i + half,) + zeros)
    out = [jax.ShapeDtypeStruct((half, *rest), bf16)] * 4
    kept_a, sent_a, kept_b, sent_b = pl.pallas_call(
        fold_kernel,
        grid=(half,),
        in_specs=[near, near, far, far] * 2,
        out_specs=[near] * 4,
        out_shape=out,
        compiler_params=params(16 * 1024 * 1024),
        cost_estimate=pl.CostEstimate(flops=int(3e9), bytes_accessed=int(3e6), transcendentals=0),
        name="fold",
    )(keep[0], got[0], keep[0], got[0], keep[1], got[1], keep[1], got[1])
    return [kept_a, kept_b], [sent_a, sent_b]


class Scatter:
    def __init__(self, pieces, count):
        a, a_far, b, b_far = pieces
        self.count = count
        self.orders = [order[::-1] for order in lane_orders(count)]
        self.keep = [a, b]
        self.got = [swap(a_far, 1, count), swap(b_far, 1, count)]
        self.at = 1

    def fold(self):
        self.keep, self.send = fold(self.keep, self.got)

    def start(self):
        self.got = [
            swap(part, order[self.at], self.count)
            for part, order in zip(self.send, self.orders)
        ]
        self.at += 1

    def step(self):
        self.fold()
        self.start()

    def run(self):
        while self.at < len(self.orders[0]):
            self.step()
        return [(keep[0], got[0]) for keep, got in zip(self.keep, self.got)]


def after(values, *others):
    return lax.optimization_barrier((values, others))[0]


def near(slots, lane, step, far):
    return slots[lane, step] < far


def pick(flags, pieces):
    a, a_far, b, b_far = pieces
    return jnp.concatenate(
        [lax.select(flags[0], a[0], a_far[0]), lax.select(flags[1], b[0], b_far[0])], axis=0
    )


def put(flags, outs, rows):
    a, a_far, b, b_far = outs
    half = a.shape[1]
    for flag, near_o, far_o, part in (
        (flags[0], a, a_far, rows[:half]),
        (flags[1], b, b_far, rows[half:]),
    ):

        @pl.when(flag)
        def _():
            near_o[0] = part

        @pl.when(jnp.logical_not(flag))
        def _():
            far_o[0] = part


def prep_kernel(query, key, value, gain_a, gain_f, router, routes, order, out):
    rp = query.shape[0]
    count, _, columns = out.shape
    small = [x[...].astype(f32) for x in (gain_a, gain_f, router)]
    side = jnp.concatenate(small, axis=0).T.astype(bf16)
    tail = jnp.zeros((rp, columns - QKV - side.shape[1]), bf16)
    rows = [x[...].astype(f32) for x in (routes, order)]
    tok = order.shape[1]
    ranks = out.shape[1] - rp
    rows.append(jnp.zeros((ranks - TOP - 1, tok), f32))
    rows = jnp.concatenate(rows, axis=0).astype(bf16)
    rows = jnp.concatenate([rows, jnp.zeros((ranks, columns - tok), bf16)], axis=1)
    for c in range(count):
        g = c * KV // count
        out[c, :rp, :] = jnp.concatenate(
            [
                query[:, g * QW : (g + 1) * QW],
                key[:, g * HD : (g + 1) * HD],
                value[:, g * HD : (g + 1) * HD],
                side,
                tail,
            ],
            axis=1,
        )
        out[c, rp : rp + ranks, :] = rows


def pack_kernel(took, w_out, out):
    count, _, columns = took.shape
    rp, width = w_out.shape
    slab = count * rp
    chunks = width // slab
    for j in range(chunks):
        out[j * rp : (j + 1) * rp, :] = w_out[:, j * slab : (j + 1) * slab]
    rows = took[:, :rp, :].astype(f32).reshape(slab, columns).T
    out[chunks * rp :, :] = rows[: out.shape[0] - chunks * rp].astype(bf16)


def unpack_kernel(shards, rp, where, *refs):
    pieces, (wt_o, gains_o, router_o, rows_o) = (refs[: 2 * shards - 1], refs[2 * shards - 1 :])
    slab = pieces[0].shape[1]
    first = shards * rp
    experts = router_o.shape[0]
    for z in range(shards):

        @pl.when(where[0] == z)
        def _():
            for p in range(shards):
                piece = pieces[p - z + shards - 1]
                columns = slice(p * slab, (p + 1) * slab)
                wt_o[:, columns] = piece[first : first + QKV]
                gains_o[:, columns] = piece[first + QKV : first + QKV + 2].astype(f32)
                router_o[:, columns] = piece[first + QKV + 2 : first + QKV + 2 + experts]
                for j in range(shards):
                    rows_o[p, :, j * slab : (j + 1) * slab] = piece[j * rp : (j + 1) * rp]


def code_kernel(first, table, out, load):
    i = pl.program_id(0)
    tok, experts = out.shape[1:]

    @pl.when(i == 0)
    def _():
        load[...] = jnp.zeros_like(load)

    rows = table[0, first : first + TOP + 1, :tok].astype(f32)
    names = lax.broadcasted_iota(i32, (experts, tok), 0).astype(f32)
    named = jnp.zeros((experts, tok), f32)
    for k in range(TOP):
        named += jnp.where(rows[k : k + 1] == names, 1.0, 0.0)
    ranks = jnp.broadcast_to(rows[TOP : TOP + 1], (tok, tok))
    before = jnp.where(ranks.T < ranks, 1.0, 0.0).astype(bf16)
    slot = dot_nn(named.astype(bf16), before) + load[:, :1]
    out[0] = (named * (1.0 + jnp.where(slot < CAP, 1.0, 0.0))).T
    load[...] += jnp.sum(named, axis=1, keepdims=True)


def qkv_kernel(
    far, slot_ref, xa, xaf, xb, xbf, gain, wt, cos, sin, ain_o, qt_o, k_o, kt_o, v_o, vt_o
):
    i = pl.program_id(0)
    flags = (near(slot_ref, 0, i, far), near(slot_ref, 1, i, far))
    x = pick(flags, (xa, xaf, xb, xbf)).astype(f32)
    inv = lax.rsqrt(jnp.mean(x * x, axis=-1, keepdims=True) + EPS)
    a = (x * inv * gain[...]).astype(bf16)
    ain_o[0] = a
    y = dot_nt(wt[...], a)
    c, s = (cos[0], sin[0])

    def turn(rows):
        lo, hi = (rows[:HALF], rows[HALF:])
        return jnp.concatenate([lo * c - hi * s, hi * c + lo * s], axis=0)

    for h in range(GROUP):
        q = turn(y[h * HD : (h + 1) * HD]).astype(bf16).astype(f32) * SCORE_SCALE
        qt_o[0, h * HD : (h + 1) * HD, :] = q.astype(bf16)
    k = turn(y[QW : QW + HD])
    kt_o[0] = k.astype(bf16)
    k_o[0] = k.T.astype(bf16)
    v = y[QW + HD :]
    vt_o[0] = v.astype(bf16)
    v_o[0] = v.T.astype(bf16)


def heads_wide(rows):
    return jnp.concatenate([rows[h * HD : (h + 1) * HD] for h in range(GROUP)], axis=1)


def causal(shape, width):
    key = lax.broadcasted_iota(i32, shape, 0)
    query = lax.broadcasted_iota(i32, shape, 1)
    for _ in range(GROUP - 1):
        query = jnp.where(query >= width, query - width, query)
    return key <= query


def attn_fwd_kernel(qt, k, vt, of_o, ob_o, lse_o):
    a = pl.program_id(0)
    tok = qt.shape[2]
    q = heads_wide(qt[0])
    s = dot_nn(k[a], q)
    s = jnp.where(causal(s.shape, tok), s, NEG_FILL)
    m = jnp.max(s, axis=0, keepdims=True)
    p = jnp.exp(s - m)
    l = jnp.sum(p, axis=0, keepdims=True)
    o = dot_nn(vt[a], p.astype(bf16))

    def step(b, carry):
        m, l, o = carry
        s = dot_nn(k[b], q)
        new = jnp.maximum(m, jnp.max(s, axis=0, keepdims=True))
        p = jnp.exp(s - new)
        back = jnp.exp(m - new)
        l = l * back + jnp.sum(p, axis=0, keepdims=True)
        o = o * back + dot_nn(vt[b], p.astype(bf16))
        return (new, l, o)

    m, l, o = lax.fori_loop(0, a, step, (m, l, o))
    o = o / l
    lse_o[0] = m + jnp.log(l)
    for h in range(GROUP):
        part = o[:, h * tok : (h + 1) * tok]
        of_o[0, h * HD : (h + 1) * HD, :] = part
        ob_o[0, h * HD : (h + 1) * HD, :] = part.astype(bf16)


def attn_bwd_kernel(qt, dot_, of, lse, k, kt, v, cos, sin, dq_o, dk_o, dv_o, dk_s, dv_s):
    a = pl.program_id(0)
    tok = qt.shape[2]
    count = k.shape[0]
    q = heads_wide(qt[0])
    do = heads_wide(dot_[0])
    delta = jnp.sum(do.astype(f32) * heads_wide(of[0]), axis=0, keepdims=True)
    total = lse[0]

    def pair(b, mask):
        s = dot_nn(k[b], q)
        p = jnp.exp(s - total)
        if mask:
            p = jnp.where(causal(s.shape, tok), p, 0.0)
        dp = dot_nn(v[b], do)
        ds = (p * (dp - delta)).astype(bf16)
        return dot_nt(ds, q), dot_nt(p.astype(bf16), do), dot_nn(kt[b], ds)

    dk, dv, dq = pair(a, True)
    dk_s[a] = dk
    dv_s[a] = dv

    def step(b, dq):
        dk, dv, more = pair(b, False)
        dk_s[b] += dk
        dv_s[b] += dv
        return dq + more

    dq = lax.fori_loop(0, a, step, dq) * SCORE_SCALE

    def back(rows, c, s):
        lo, hi = (rows[:HALF], rows[HALF:])
        return jnp.concatenate([lo * c + hi * s, hi * c - lo * s], axis=0)

    for h in range(GROUP):
        dq_o[0, h * HD : (h + 1) * HD, :] = back(
            dq[:, h * tok : (h + 1) * tok], cos[a], sin[a]
        ).astype(bf16)

    @pl.when(a == count - 1)
    def _():
        @pl.loop(0, count)
        def _(b):
            dk_o[b] = back(dk_s[b].T, cos[b], sin[b]).astype(bf16)
            dv_o[b] = dv_s[b].T.astype(bf16)


def qkv_grads_kernel(share, dq, dk, dv, ain, wt, gain, gw_o, gg_o, acc):
    i = pl.program_id(0)
    d = jnp.concatenate([dq[0], dk[0], dv[0]], axis=0)

    @pl.when(i == 0)
    def _():
        acc[...] = jnp.zeros_like(acc)

    acc[...] += dot_nn(d, ain[0])

    @pl.when(i == pl.num_programs(0) - 1)
    def _():
        width = gw_o.shape[2]
        for z in range(gw_o.shape[0]):
            gw_o[z] = acc[:, z * width : (z + 1) * width].astype(bf16)
        total = jnp.sum(acc[...] * wt[...].astype(f32), axis=0, keepdims=True)
        gg_o[...] = total * share / gain[...]


def qkv_back_kernel(share, far, blocks_ref, dqa, dka, dva, dqb, dkb, dvb, wt, *outs):
    i = pl.program_id(0)
    flags = (i < far, i < far)
    d = jnp.concatenate(
        [
            jnp.concatenate([dqa[0], dka[0], dva[0]], axis=0),
            jnp.concatenate([dqb[0], dkb[0], dvb[0]], axis=0),
        ],
        axis=1,
    )
    put(flags, outs, (dot_tn(d, wt[...]) * share).astype(bf16))


def bundle_kernel(gw, gain_a, gain_f, router, p0, p1, q0, q1, out):
    shards, rows, slab = out.shape
    half, rp, _ = p0.shape
    first = shards * rp
    small = jnp.concatenate([gain_a[...], gain_f[...], router[...]], axis=0).astype(bf16)
    count = small.shape[0]
    for z in range(shards):
        near, got = (p0, p1) if z < half else (q0, q1)
        w_out = add_up(near[z % half], got[z % half])
        for j in range(shards):
            out[z, j * rp : (j + 1) * rp, :] = w_out[:, j * slab : (j + 1) * slab]
        out[z, first : first + QKV, :] = gw[z]
        out[z, first + QKV : first + QKV + count, :] = small[:, z * slab : (z + 1) * slab]
        rest = first + QKV + count
        if rest < rows:
            out[z, rest:, :] = jnp.zeros((rows - rest, slab), bf16)


def share_kernel(own, send, w_out_o):
    count, rp, columns = send.shape
    shards = w_out_o.shape[1] // own.shape[1]
    slab = own.shape[1]
    first = shards * rp
    for j in range(shards):
        w_out_o[:, j * slab : (j + 1) * slab] = own[j * rp : (j + 1) * rp, :].astype(f32)
    rows = own[first:, :].astype(f32)
    rows = jnp.concatenate([rows, jnp.zeros((columns - rows.shape[0], slab), f32)], axis=0)
    send[...] = rows.T.reshape(count, rp, columns).astype(bf16)


def finish_kernel(copies, given, query, key, value, sums):
    count = given.shape[0]
    parts = [given[c].astype(f32) for c in range(count)]
    for c in range(0, count, copies):
        g = c // copies
        query[:, g * QW : (g + 1) * QW] = parts[c][:, :QW]
        key[:, g * HD : (g + 1) * HD] = parts[c][:, QW : QW + HD]
        value[:, g * HD : (g + 1) * HD] = parts[c][:, QW + HD : QKV]
    total = parts[0][:, QKV:]
    for part in parts[1:]:
        total = total + part[:, QKV:]
    sums[...] = total.T[: sums.shape[0]]


def expert_terms(expert, x, y, router, code, w_gate, w_up, w_down):
    logits = dot_nt(x, router)
    named = code > 0.5
    logits = jnp.where(named, logits, NEG_FILL)
    top = jnp.max(logits, axis=-1, keepdims=True)
    raised = jnp.where(named, jnp.exp(logits - top), 0.0)
    gates = raised / jnp.sum(raised, axis=-1, keepdims=True)
    mine = (lax.broadcasted_iota(i32, gates.shape, 1) == expert) & (code > 1.5)
    weight = RESIDUAL_SCALE * jnp.sum(jnp.where(mine, gates, 0.0), axis=-1, keepdims=True)
    kept = RESIDUAL_SCALE * jnp.sum(jnp.where(mine, 1.0, 0.0), axis=-1, keepdims=True)

    gate_pre = dot_nn(x, w_gate)
    up_pre = dot_nn(x, w_up)
    back = dot_nn(y, w_down)
    sig = jax.nn.sigmoid(gate_pre)
    act = gate_pre * sig
    inner = act * up_pre
    gate_grad = kept * jnp.sum(inner * back, axis=-1, keepdims=True)
    inner_w = (inner * weight).astype(bf16)
    d_inner = back * weight
    d_gate = (d_inner * up_pre * sig * (1.0 + gate_pre * (1.0 - sig))).astype(bf16)
    d_up = (d_inner * act).astype(bf16)
    din = dot_nt(d_gate, w_gate) + dot_nt(d_up, w_up)
    high = gate_grad.astype(bf16).astype(f32)
    low = (gate_grad - high).astype(bf16).astype(f32)
    lane = lax.broadcasted_iota(i32, (x.shape[0], EXTRA), 1)
    side = jnp.where(lane == expert, high, 0.0) + jnp.where(lane == expert + LOW, low, 0.0)
    return inner_w, d_gate, d_up, jnp.concatenate([din, side], axis=1)


def weight_of(weights, which):
    shards, _, depth, ff = weights.shape
    return weights[:, which].reshape(shards * depth, ff)


def clear(accs, i):
    @pl.when(i == 0)
    def _():
        for acc in accs:
            acc[...] = jnp.zeros_like(acc)


def flush(accs, grad_o, i):
    @pl.when(i == pl.num_programs(0) - 1)
    def _():
        shards, _, depth, _ = grad_o.shape
        for which, acc in enumerate(accs):
            for z in range(shards):
                grad_o[z, which] = acc[z * depth : (z + 1) * depth, :].astype(bf16)


def moe_first_kernel(far, which, blocks, *refs):
    xs, ys, (router, code_a, code_b, weights) = (refs[:4], refs[4:8], refs[8:12])
    outs, (b_o, grad_o), accs = (refs[12:16], refs[16:18], refs[18:])
    i = pl.program_id(0)
    flags = (i < far, i < far)
    x, y = (pick(flags, xs), pick(flags, ys))
    code = jnp.concatenate([code_a[0], code_b[0]], axis=0)
    inner_w, d_gate, d_up, din = expert_terms(
        which[0], x, y, router[...], code, *[weight_of(weights, m) for m in range(3)]
    )
    put(flags, outs, din.astype(bf16))
    b_o[0] = inner_w
    clear(accs, i)
    accs[0][...] += dot_tn(x, d_gate)
    accs[1][...] += dot_tn(x, d_up)
    accs[2][...] += dot_tn(y, inner_w)
    flush(accs, grad_o, i)


def moe_second_kernel(far, which, blocks, *refs):
    xs, ys, (router, code_a, code_b, weights) = (refs[:4], refs[4:8], refs[8:12])
    prev, outs, (b_o, dg_o, du_o) = (refs[12:16], refs[16:20], refs[20:])
    i = pl.program_id(0)
    flags = (i < far, i < far)
    x, y = (pick(flags, xs), pick(flags, ys))
    code = jnp.concatenate([code_a[0], code_b[0]], axis=0)
    inner_w, d_gate, d_up, din = expert_terms(
        which[0], x, y, router[...], code, *[weight_of(weights, m) for m in range(3)]
    )
    put(flags, outs, (din + pick(flags, prev).astype(f32)).astype(bf16))
    b_o[0] = inner_w
    dg_o[0] = d_gate
    du_o[0] = d_up


def moe_grads_kernel(far, *refs):
    xs, ys, (b, dg, du), grad_o, accs = (refs[:4], refs[4:8], refs[8:11], refs[11], refs[12:])
    i = pl.program_id(0)
    flags = (i < far, i < far)
    x, y = (pick(flags, xs), pick(flags, ys))
    clear(accs, i)
    accs[0][...] += dot_tn(x, dg[0])
    accs[1][...] += dot_tn(x, du[0])
    accs[2][...] += dot_tn(y, b[0])
    flush(accs, grad_o, i)


def moe_out_kernel(far, b0, b1, w0, w1, *outs):
    i = pl.program_id(0)
    flags = (i < far, i < far)
    out = dot_nt(b0[0], weight_of(w0, 0)) + dot_nt(b1[0], weight_of(w1, 0))
    put(flags, outs, out.astype(bf16))


def place_kernel(far, slot_ref, a, af, b, bf, out):
    i = pl.program_id(0)
    flags = (near(slot_ref, 0, i, far), near(slot_ref, 1, i, far))
    half = a.shape[1]
    for z in range(half):
        out[z, 0] = lax.select(flags[0], a[0, z], af[0, z])
        out[half + z, 0] = lax.select(flags[1], b[0, z], bf[0, z])


def after_attn_kernel(attn, w_out, hidden, gain, resid_o, ma_o, mb_o):
    resid = hidden[...].astype(f32) + RESIDUAL_SCALE * dot_tn(attn[...], w_out[...])
    resid_o[...] = resid
    inv = lax.rsqrt(jnp.mean(resid * resid, axis=-1, keepdims=True) + EPS)
    moe_in = (resid * inv * gain[...]).astype(bf16)
    half = ma_o.shape[1]
    ma_o[0] = moe_in[:half]
    mb_o[0] = moe_in[half:]


def before_attn_kernel(
    a0, a1, b0, b1, resid, ma, mb, grad_out, code, router, gain, w_out,
    d_resid_o, d_branch_o, d_attn_o, d_router_o, d_gain_o,
):
    width = resid.shape[1]
    experts = router.shape[0]
    back = jnp.concatenate(
        [
            a0[...].astype(f32) + a1[...].astype(f32),
            b0[...].astype(f32) + b1[...].astype(f32),
        ],
        axis=0,
    )
    moe_in = jnp.concatenate([ma[0], mb[0]], axis=0)
    chosen = code[...] > 0.5
    logits = jnp.where(chosen, dot_nt(moe_in, router[...]), NEG_FILL)
    raised = jnp.where(chosen, jnp.exp(logits - jnp.max(logits, axis=-1, keepdims=True)), 0.0)
    gates = raised / jnp.sum(raised, axis=-1, keepdims=True)
    gate_grad = (
        back[:, width : width + experts] + back[:, width + LOW : width + LOW + experts]
    )
    logit_grad = gates * (gate_grad - jnp.sum(gates * gate_grad, axis=-1, keepdims=True))
    dlogits = logit_grad.astype(bf16)
    d_router_o[...] = dot_tn(dlogits, moe_in)
    d_moe_in = back[:, :width] + dot_nn(dlogits, router[...])
    r = resid[...]
    inv = lax.rsqrt(jnp.mean(r * r, axis=-1, keepdims=True) + EPS)
    normed = r * inv
    d_gain_o[...] = jnp.sum(d_moe_in * normed, axis=0, keepdims=True)
    d_normed = d_moe_in * gain[...]
    d_resid = grad_out[...].astype(f32) + inv * (
        d_normed - normed * jnp.mean(d_normed * normed, axis=-1, keepdims=True)
    )
    d_resid_o[...] = d_resid
    d_branch = (RESIDUAL_SCALE * d_resid).astype(bf16)
    d_branch_o[...] = d_branch
    d_attn_o[...] = dot_nt(w_out[...], d_branch).astype(bf16)


def wout_grad_kernel(far, slot_ref, attn, d_branch, a, af, b, bf):
    n2, half, rp, width = a.shape
    n = 2 * n2
    d = d_branch[...]
    for z in range(2 * half):
        rows = dot_nn(attn[z * n * rp : (z + 1) * n * rp, :], d).astype(bf16)
        lane = 0 if z < half else 1
        near_o, far_o = ((a, af), (b, bf))[lane]
        for c in range(n):
            part = rows[c * rp : (c + 1) * rp]
            slot = slot_ref[lane, c]

            @pl.when(slot < far)
            def _():
                near_o[slot, z % half] = part

            @pl.when(slot >= far)
            def _():
                far_o[slot - far, z % half] = part


def last_kernel(a0, a1, b0, b1, d_resid, hidden, gain, out):
    d = jnp.concatenate(
        [
            a0[...].astype(f32) + a1[...].astype(f32),
            b0[...].astype(f32) + b1[...].astype(f32),
        ],
        axis=0,
    )
    x = hidden[...].astype(f32)
    inv = lax.rsqrt(jnp.mean(x * x, axis=-1, keepdims=True) + EPS)
    normed = x * inv
    d = d * gain[...]
    out[...] = d_resid[...] + inv * (
        d - normed * jnp.mean(d * normed, axis=-1, keepdims=True)
    )


def whole(shape):
    zeros = (0,) * len(shape)
    return pl.BlockSpec(shape, lambda *at: zeros)


def at_step(shape):
    zeros = (0,) * (len(shape) - 1)
    return pl.BlockSpec(shape, lambda i, *refs: (i,) + zeros)


def lanes_at_step(shape, far):
    zeros = (0,) * (len(shape) - 1)
    first = pl.BlockSpec(shape, lambda i, *refs: (jnp.minimum(i, far - 1),) + zeros)
    second = pl.BlockSpec(shape, lambda i, *refs: (jnp.maximum(i - far, 0),) + zeros)
    return [first, second, first, second]


def lanes_at_slot(shape, far):
    zeros = (0,) * (len(shape) - 1)

    def spec(lane, second):
        def index(i, slots):
            slot = slots[lane, i]
            slot = jnp.maximum(slot - far, 0) if second else jnp.minimum(slot, far - 1)
            return (slot,) + zeros

        return pl.BlockSpec(shape, index)

    return [spec(0, False), spec(0, True), spec(1, False), spec(1, True)]


def shape_of(*dims, dtype=bf16):
    return jax.ShapeDtypeStruct(dims, dtype)


def micros(us):
    return pl.CostEstimate(
        flops=int(us * 1.1e9), bytes_accessed=int(us * 1e6), transcendentals=0
    )


def call(kernel, name, us, out_shape, operands, *, grid=None, specs=None, out_specs=None,
         scratch=(), tables=(), limit=58):
    if grid is None:
        specs = [whole(x.shape) for x in operands]
        out_specs = jax.tree.map(lambda x: whole(x.shape), out_shape)
        grid = 1
    return pl.pallas_call(
        kernel,
        grid_spec=pltpu.PrefetchScalarGridSpec(
            num_scalar_prefetch=len(tables),
            grid=(grid,),
            in_specs=specs,
            out_specs=out_specs,
            scratch_shapes=list(scratch),
        ),
        out_shape=out_shape,
        compiler_params=params(limit * 1024 * 1024),
        cost_estimate=micros(us),
        name=name,
    )(*tables, *operands)


def shards(
    hidden,
    gain_attn,
    w_query,
    w_key,
    w_value,
    w_out,
    gain_ffn,
    router,
    routes,
    slot_order,
    w_gate,
    w_up,
    w_down,
    grad_out,
):
    tok, width = hidden.shape
    n = lax.axis_size("ctx")
    dp = lax.axis_size("dp")
    me = lax.axis_index("ctx")
    copies = n // KV
    far = n // 2
    rp = w_query.shape[0]
    slab = rp * n
    experts = router.shape[1]
    half = tok // 2
    ff = w_gate.shape[2]
    depth = w_gate.shape[1]
    orders = lane_orders(n)
    slots = [slots_of(order) for order in orders]
    blocks = jnp.array(slots, i32) ^ me
    inverse = jnp.array([[lane.index(j) for j in range(n)] for lane in slots], i32)
    slot_at = jnp.take(inverse, jnp.arange(n, dtype=i32) ^ me, axis=1)


    side = QKV + 2 + experts
    pad = -(side + rp * dp) % 16
    send = call(
        prep_kernel,
        "prep",
        2,
        shape_of(n, rp + 16, max(slab, tok, -(-side // 128) * 128)),
        [
            w_query,
            w_key,
            w_value,
            gain_attn[None],
            gain_ffn[None],
            router.T,
            routes.T,
            slot_order,
        ],
        limit=58,
    )
    took = lax.all_to_all(send, "ctx", split_axis=0, concat_axis=0, tiled=True)
    pack = call(
        pack_kernel,
        "pack",
        2,
        shape_of(side + rp * dp, slab),
        [took, w_out],
        limit=58,
    )

    def along(value, by):
        pairs = [(z, z + by) for z in range(dp) if 0 <= z + by < dp]
        return lax.ppermute(value, "dp", pairs)

    below, above = ([], [])
    for _ in range(dp - 1):
        below.append(along(below[-1] if below else pack, 1))
        above.append(along(above[-1] if above else pack, -1))
    wt, gains, router_t, out_rows = call(
        functools.partial(unpack_kernel, dp, rp),
        "unpack",
        2,
        [
            shape_of(QKV, width),
            shape_of(2, width, dtype=f32),
            shape_of(experts, width),
            shape_of(dp, rp, width),
        ],
        [*below[::-1], pack, *above],
        grid=1,
        specs=[whole(pack.shape)] * (2 * dp - 1),
        out_specs=[
            whole((QKV, width)),
            whole((2, width)),
            whole((experts, width)),
            whole((dp, rp, width)),
        ],
        tables=[lax.axis_index("dp").reshape(1).astype(i32)],
        limit=58,
    )
    gain_a, gain_f = (gains[0:1], gains[1:2])

    stacks = [jnp.stack([w_gate[e], w_up[e], w_down[e]]) for e in range(w_gate.shape[0])]
    stacks = after(stacks, below[:-1], above[:-1])
    expert_w = [lax.all_gather(stack, "dp", axis=0) for stack in stacks]

    x_rows = after(hidden, took)
    x_rows = Gather(x_rows[:half], x_rows[half:], n)
    xs = x_rows.run()
    y_rows = after(grad_out, x_rows.have)
    y_rows = Gather(y_rows[:half], y_rows[half:], n)

    exponents = jnp.arange(HALF, dtype=f32) * (2.0 / HD)
    inverse_freq = jnp.power(10000.0, -exponents)
    positions = jnp.arange(n * tok, dtype=f32).reshape(n, 1, tok)
    angles = positions * inverse_freq[None, :, None]
    cos, sin = (jnp.cos(angles), jnp.sin(angles))

    o_rows = Gather(out_rows[: dp // 2], out_rows[dp // 2 :], n)
    gain_a, y_rows.got = after((gain_a, y_rows.got))

    ain, qt, k, kt, v, vt = call(
        functools.partial(qkv_kernel, far),
        "qkv",
        6,
        [
            shape_of(n, tok, width),
            shape_of(n, QW, tok),
            shape_of(n, tok, HD),
            shape_of(n, HD, tok),
            shape_of(n, tok, HD),
            shape_of(n, HD, tok),
        ],
        [*xs, gain_a, wt, cos, sin],
        grid=n,
        specs=lanes_at_slot((1, half, width), far)
        + [whole((1, width)), whole((QKV, width))]
        + [at_step((1, HALF, tok))] * 2,
        out_specs=[
            at_step((1, tok, width)),
            at_step((1, QW, tok)),
            at_step((1, tok, HD)),
            at_step((1, HD, tok)),
            at_step((1, tok, HD)),
            at_step((1, HD, tok)),
        ],
        tables=[slot_at],
        limit=58,
    )

    qt, y_rows.have, y_rows.got, o_rows.have, o_rows.got = after(
        (qt, y_rows.have, y_rows.got, o_rows.have, o_rows.got)
    )
    y_rows.step()
    o_rows.step()
    qt = after(qt, y_rows.have, o_rows.have)
    of, attn_t, lse = call(
        attn_fwd_kernel,
        "attn_fwd",
        19,
        [
            shape_of(n, QW, tok, dtype=f32),
            shape_of(n, QW, tok),
            shape_of(n, 1, GROUP * tok, dtype=f32),
        ],
        [qt, k, vt],
        grid=n,
        specs=[at_step((1, QW, tok)), whole((n, tok, HD)), whole((n, HD, tok))],
        out_specs=[at_step((1, QW, tok))] * 2 + [at_step((1, 1, GROUP * tok))],
        limit=58,
    )

    attn_t, y_rows.got, o_rows.got = after((attn_t, y_rows.got, o_rows.got))
    os = o_rows.run()
    ys = y_rows.run()
    attn_b = lax.all_to_all(attn_t, "ctx", split_axis=0, concat_axis=0, tiled=True)
    attn_b = attn_b[::copies].reshape(KV * QW, tok)

    w_out_all = call(
        functools.partial(place_kernel, far),
        "place",
        4,
        shape_of(dp, n, rp, width),
        os,
        grid=n,
        specs=lanes_at_slot((1, dp // 2, rp, width), far),
        out_specs=pl.BlockSpec((dp, 1, rp, width), lambda i, slots: (0, i, 0, 0)),
        tables=[slot_at],
        limit=58,
    ).reshape(KV * QW, width)

    resid, ma, mb = call(
        after_attn_kernel,
        "after_attn",
        6,
        [shape_of(tok, width, dtype=f32)] + [shape_of(1, half, width)] * 2,
        [attn_b, w_out_all, hidden, gain_f],
        limit=58,
    )
    m_rows = Gather(ma[0], mb[0], n)
    took = after(took, ma)

    code = call(
        functools.partial(code_kernel, rp),
        "code",
        6,
        shape_of(n, tok, experts, dtype=f32),
        [took],
        grid=n,
        specs=[at_step((1,) + took.shape[1:])],
        out_specs=at_step((1, tok, experts)),
        scratch=[pltpu.VMEM((experts, 1), f32)],
        limit=58,
    )
    code_mine = lax.dynamic_index_in_dim(code, me, 0, keepdims=False)

    m_rows.got, code, code_mine = after((m_rows.got, code, code_mine))
    ms = m_rows.run()

    side_w = width + EXTRA
    wide = [shape_of(far, half, side_w)] * 4
    rows_in = lanes_at_step((1, half, width), far) * 2 + [
        whole((experts, width)),
        *[
            pl.BlockSpec((1, half, experts), lambda i, which, blocks, lane=lane: (blocks[lane, i], lane, 0))
            for lane in range(2)
        ],
        whole((dp, 3, depth, ff)),
    ]
    hidden_o = [at_step((1, tok, ff))]
    hidden_s = [shape_of(n, tok, ff)]
    accs = [pltpu.VMEM((width, ff), f32)] * 3
    first = (me * len(expert_w)).reshape(1).astype(i32)
    *din, inner_0, grads_0 = call(
        functools.partial(moe_first_kernel, far),
        "moe_first",
        38,
        wide + hidden_s + [shape_of(dp, 3, depth, ff)],
        [*ms, *ys, router_t, code, code, expert_w[0]],
        grid=n,
        specs=rows_in,
        out_specs=lanes_at_step((1, half, side_w), far) + hidden_o + [whole((dp, 3, depth, ff))],
        scratch=accs,
        tables=[first, blocks],
        limit=58,
    )
    *din, inner_1, d_gate_1, d_up_1 = call(
        functools.partial(moe_second_kernel, far),
        "moe_second",
        25,
        wide + hidden_s * 3,
        [*ms, *ys, router_t, code, code, expert_w[1], *din],
        grid=n,
        specs=rows_in + lanes_at_step((1, half, side_w), far),
        out_specs=lanes_at_step((1, half, side_w), far) + hidden_o * 3,
        tables=[first + 1, blocks],
        limit=58,
    )
    back = Scatter(din, n)
    back.step()
    inner_1 = after(inner_1, back.keep)
    grads_1 = call(
        functools.partial(moe_grads_kernel, far),
        "moe_grads",
        15,
        shape_of(dp, 3, depth, ff),
        [*ms, *ys, inner_1, d_gate_1, d_up_1],
        grid=n,
        specs=lanes_at_step((1, half, width), far) * 2 + hidden_o * 3,
        out_specs=whole((dp, 3, depth, ff)),
        scratch=accs,
        limit=58,
    )
    expert_grads = [
        lax.psum_scatter(grads, "dp", scatter_dimension=0, tiled=True)
        for grads in (grads_0, grads_1)
    ]

    back.got = after(back.got, grads_1)
    (a0, a1), (b0, b1) = back.run()
    inner_1 = after(inner_1, back.keep)
    down = pl.BlockSpec((dp, 1, depth, ff), lambda i: (0, 2, 0, 0))
    outs = call(
        functools.partial(moe_out_kernel, far),
        "moe_out",
        8,
        [shape_of(far, half, width)] * 4,
        [inner_0, inner_1, *expert_w],
        grid=n,
        specs=hidden_o * 2 + [down] * 2,
        out_specs=lanes_at_step((1, half, width), far),
        limit=40,
    )
    mix = Scatter(outs, n)
    resid_in = after(resid, outs)
    d_resid, d_branch, d_attn, d_router, d_gain_ffn = call(
        before_attn_kernel,
        "before_attn",
        14,
        [
            shape_of(tok, width, dtype=f32),
            shape_of(tok, width),
            shape_of(KV * QW, tok),
            shape_of(experts, width, dtype=f32),
            shape_of(1, width, dtype=f32),
        ],
        [a0, a1, b0, b1, resid_in, ma, mb, grad_out, code_mine, router_t, gain_f, w_out_all],
        limit=58,
    )
    d_heads = lax.all_to_all(
        jnp.repeat(d_attn.reshape(KV, QW, tok), copies, axis=0),
        "ctx",
        split_axis=0,
        concat_axis=0,
        tiled=True,
    )
    d_wout = call(
        functools.partial(wout_grad_kernel, far),
        "wout_grad",
        6,
        [shape_of(far, dp // 2, rp, width)] * 4,
        [attn_b, d_branch],
        grid=1,
        specs=[whole((KV * QW, tok)), whole((tok, width))],
        out_specs=[whole((far, dp // 2, rp, width))] * 4,
        tables=[slot_at],
        limit=58,
    )

    mix.fold()
    mix.send, mix.keep, d_heads, expert_grads[0] = after(
        (mix.send, mix.keep, d_heads, expert_grads[0])
    )
    mix.start()
    wout = Scatter(after(d_wout, d_heads), n)
    dq, dk, dv = call(
        attn_bwd_kernel,
        "attn_bwd",
        40,
        [shape_of(n, QW, tok), shape_of(n, HD, tok), shape_of(n, HD, tok)],
        [qt, d_heads, of, lse, k, kt, v, cos, sin],
        grid=n,
        specs=[
            at_step((1, QW, tok)),
            at_step((1, QW, tok)),
            at_step((1, QW, tok)),
            at_step((1, 1, GROUP * tok)),
            whole((n, tok, HD)),
            whole((n, HD, tok)),
            whole((n, tok, HD)),
            whole((n, HALF, tok)),
            whole((n, HALF, tok)),
        ],
        out_specs=[at_step((1, QW, tok)), whole((n, HD, tok)), whole((n, HD, tok))],
        scratch=[pltpu.VMEM((n, tok, HD), f32), pltpu.VMEM((n, tok, HD), f32)],
        limit=40,
    )

    dq, wout.keep, wout.got = after((dq, wout.keep, wout.got))
    wout.step()
    dq = after(dq, wout.keep)

    gw, d_gain_attn = call(
        functools.partial(qkv_grads_kernel, 1.0 / copies),
        "qkv_grads",
        20,
        [shape_of(dp, QKV, slab), shape_of(1, width, dtype=f32)],
        [dq, dk, dv, ain, wt, gain_a],
        grid=n,
        specs=[
            at_step((1, QW, tok)),
            at_step((1, HD, tok)),
            at_step((1, HD, tok)),
            at_step((1, tok, width)),
            whole((QKV, width)),
            whole((1, width)),
        ],
        out_specs=[whole((dp, QKV, slab)), whole((1, width))],
        scratch=[pltpu.VMEM((QKV, width), f32)],
        limit=30,
    )

    def columns(rows, lane):
        return pl.BlockSpec((1, rows, half), lambda i, blocks: (blocks[lane, i], 0, lane))

    dq, wout.keep, wout.got, mix.keep, mix.got = after(
        (dq, wout.keep, wout.got, mix.keep, mix.got), gw
    )
    wout.step()
    mix.step()
    dq = after(dq, wout.keep, mix.keep)
    d_in = call(
        functools.partial(qkv_back_kernel, 1.0 / copies, far),
        "qkv_back",
        20,
        [shape_of(far, half, width)] * 4,
        [dq, dk, dv, dq, dk, dv, wt],
        grid=n,
        specs=[columns(rows, lane) for lane in range(2) for rows in (QW, HD, HD)]
        + [whole((QKV, width))],
        out_specs=lanes_at_step((1, half, width), far),
        tables=[blocks],
        limit=30,
    )

    wout.got = after(wout.got, d_in)
    (p0, p1), (q0, q1) = wout.run()
    bundle = call(
        bundle_kernel,
        "bundle",
        2,
        shape_of(dp, side + rp * dp + pad, slab),
        [gw, d_gain_attn, d_gain_ffn, d_router, p0, p1, q0, q1],
        limit=30,
    )
    own = lax.psum_scatter(bundle, "dp", scatter_dimension=0, tiled=True)[0]
    send, grad_out_proj = call(
        share_kernel,
        "share",
        2,
        [shape_of(n, rp, -(-(side + pad) // 128) * 128), shape_of(rp, width, dtype=f32)],
        [own],
        limit=30,
    )
    given = lax.all_to_all(send, "ctx", split_axis=0, concat_axis=0, tiled=True)
    grad_query, grad_key, grad_value, sums = call(
        functools.partial(finish_kernel, copies),
        "finish",
        2,
        [
            shape_of(rp, KV * QW, dtype=f32),
            shape_of(rp, KV * HD, dtype=f32),
            shape_of(rp, KV * HD, dtype=f32),
            shape_of(2 + experts, rp, dtype=f32),
        ],
        [given],
        limit=30,
    )

    back_in = Scatter(after(d_in, bundle), n)
    back_in.step()
    expert_grads, mix.got = after((expert_grads, mix.got), back_in.keep)
    (c0, c1), (e0, e1) = back_in.run()
    d_hidden = call(
        last_kernel,
        "last",
        3,
        shape_of(tok, width, dtype=f32),
        [c0, c1, e0, e1, after(d_resid, send), hidden, gain_a],
        limit=30,
    )

    (r0, r1), (s0, s1) = mix.run()
    mixed = jnp.concatenate(
        [r0.astype(f32) + r1.astype(f32), s0.astype(f32) + s1.astype(f32)], axis=0
    )
    output = (resid + mixed).astype(bf16)

    expert_grads = jnp.concatenate(expert_grads, axis=0).astype(f32)
    return (
        output,
        d_hidden,
        sums[0],
        grad_query,
        grad_key,
        grad_value,
        grad_out_proj,
        sums[1],
        sums[2:].T,
        expert_grads[:, 0],
        expert_grads[:, 1],
        expert_grads[:, 2],
    )


def solution(mesh):
    rows = P(("dp", "ctx"), None)
    flat = P(("dp", "ctx"))
    expert = P("ctx", "dp", None)
    return jax.shard_map(
        shards,
        mesh=mesh,
        in_specs=(
            rows,
            flat,
            rows,
            rows,
            rows,
            rows,
            flat,
            rows,
            rows,
            rows,
            expert,
            expert,
            expert,
            rows,
        ),
        out_specs=(
            rows,
            rows,
            flat,
            rows,
            rows,
            rows,
            rows,
            flat,
            rows,
            expert,
            expert,
            expert,
        ),
        check_vma=False,
    )
```

```python
import functools

import jax
import jax.numpy as jnp
from jax import lax
from jax.experimental import pallas as pl
from jax.experimental.pallas import tpu as pltpu
from jax.sharding import PartitionSpec as P

H = 24
KV = 8
HD = 64
TOP = 8
CAP = 1024

EPS = 1e-06
NEG_FILL = -1e30
SCORE_SCALE = 0.015625
RESIDUAL_SCALE = 0.22

GROUP = H // KV
HALF = HD // 2
QW = GROUP * HD
QKV = QW + 2 * HD
LOW = 64
EXTRA = 128

f32 = jnp.float32
bf16 = jnp.bfloat16
i32 = jnp.int32
VMEM_LIMIT = 58 * 1024 * 1024


def dot_nn(a, b):
    return lax.dot_general(a, b, (((1,), (0,)), ((), ())), preferred_element_type=f32)


def dot_nt(a, b):
    return lax.dot_general(a, b, (((1,), (1,)), ((), ())), preferred_element_type=f32)


def dot_tn(a, b):
    return lax.dot_general(a, b, (((0,), (0,)), ((), ())), preferred_element_type=f32)


def params(limit=VMEM_LIMIT):
    return pltpu.CompilerParams(dimension_semantics=("arbitrary",), vmem_limit_bytes=limit)


def lane_orders(count):
    bits = []
    bit = 2
    while bit < count:
        bits.append(bit)
        bit *= 2
    return (bits[::-1] + [1], bits + [1])


def slots_of(order):
    slots = [0]
    for bit in order:
        slots = slots + [s ^ bit for s in slots]
    return slots


def swap(value, bit, count):
    return lax.ppermute(value, "ctx", [(i, i ^ bit) for i in range(count)])


class Gather:
    def __init__(self, first, second, count):
        self.count = count
        self.orders = lane_orders(count)
        self.have = [first[None], second[None]]
        self.at = 0
        self.start()

    def start(self):
        self.got = [
            swap(have, order[self.at], self.count)
            for have, order in zip(self.have, self.orders)
        ]
        self.at += 1

    def step(self):
        self.have = [
            jnp.concatenate([have, got], axis=0) for have, got in zip(self.have, self.got)
        ]
        self.start()

    def run(self):
        while self.at < len(self.orders[0]):
            self.step()
        return [self.have[0], self.got[0], self.have[1], self.got[1]]


def add_up(x, y):
    return (x.astype(f32) + y.astype(f32)).astype(bf16)


def fold_kernel(*refs):
    ins, outs = (refs[:8], refs[8:])
    for lane in range(2):
        near, got, near_far, got_far = ins[4 * lane : 4 * lane + 4]
        outs[2 * lane][...] = add_up(near[...], got[...])
        outs[2 * lane + 1][...] = add_up(near_far[...], got_far[...])


def fold(keep, got):
    size, *rest = keep[0].shape
    half = size // 2
    zeros = (0,) * len(rest)
    near = pl.BlockSpec((1, *rest), lambda i: (i,) + zeros)
    far = pl.BlockSpec((1, *rest), lambda i: (i + half,) + zeros)
    out = [jax.ShapeDtypeStruct((half, *rest), bf16)] * 4
    kept_a, sent_a, kept_b, sent_b = pl.pallas_call(
        fold_kernel,
        grid=(half,),
        in_specs=[near, near, far, far] * 2,
        out_specs=[near] * 4,
        out_shape=out,
        compiler_params=params(16 * 1024 * 1024),
        cost_estimate=pl.CostEstimate(flops=int(3e9), bytes_accessed=int(3e6), transcendentals=0),
        name="fold",
    )(keep[0], got[0], keep[0], got[0], keep[1], got[1], keep[1], got[1])
    return [kept_a, kept_b], [sent_a, sent_b]


class Scatter:
    def __init__(self, pieces, count):
        a, a_far, b, b_far = pieces
        self.count = count
        self.orders = [order[::-1] for order in lane_orders(count)]
        self.keep = [a, b]
        self.got = [swap(a_far, 1, count), swap(b_far, 1, count)]
        self.at = 1

    def fold(self):
        self.keep, self.send = fold(self.keep, self.got)

    def start(self):
        self.got = [
            swap(part, order[self.at], self.count)
            for part, order in zip(self.send, self.orders)
        ]
        self.at += 1

    def step(self):
        self.fold()
        self.start()

    def run(self):
        while self.at < len(self.orders[0]):
            self.step()
        return [(keep[0], got[0]) for keep, got in zip(self.keep, self.got)]


def after(values, *others):
    return lax.optimization_barrier((values, others))[0]


def near(slots, lane, step, far):
    return slots[lane, step] < far


def pick(flags, pieces):
    a, a_far, b, b_far = pieces
    return jnp.concatenate(
        [lax.select(flags[0], a[0], a_far[0]), lax.select(flags[1], b[0], b_far[0])], axis=0
    )


def put(flags, outs, rows):
    a, a_far, b, b_far = outs
    half = a.shape[1]
    for flag, near_o, far_o, part in (
        (flags[0], a, a_far, rows[:half]),
        (flags[1], b, b_far, rows[half:]),
    ):

        @pl.when(flag)
        def _():
            near_o[0] = part

        @pl.when(jnp.logical_not(flag))
        def _():
            far_o[0] = part


def prep_kernel(query, key, value, gain_a, gain_f, router, routes, order, out):
    rp = query.shape[0]
    count, _, columns = out.shape
    small = [x[...].astype(f32) for x in (gain_a, gain_f, router)]
    side = jnp.concatenate(small, axis=0).T.astype(bf16)
    tail = jnp.zeros((rp, columns - QKV - side.shape[1]), bf16)
    rows = [x[...].astype(f32) for x in (routes, order)]
    tok = order.shape[1]
    ranks = out.shape[1] - rp
    rows.append(jnp.zeros((ranks - TOP - 1, tok), f32))
    rows = jnp.concatenate(rows, axis=0).astype(bf16)
    rows = jnp.concatenate([rows, jnp.zeros((ranks, columns - tok), bf16)], axis=1)
    for c in range(count):
        g = c * KV // count
        out[c, :rp, :] = jnp.concatenate(
            [
                query[:, g * QW : (g + 1) * QW],
                key[:, g * HD : (g + 1) * HD],
                value[:, g * HD : (g + 1) * HD],
                side,
                tail,
            ],
            axis=1,
        )
        out[c, rp : rp + ranks, :] = rows


def pack_kernel(took, w_out, out):
    count, _, columns = took.shape
    rp, width = w_out.shape
    slab = count * rp
    chunks = width // slab
    for j in range(chunks):
        out[j * rp : (j + 1) * rp, :] = w_out[:, j * slab : (j + 1) * slab]
    rows = took[:, :rp, :].astype(f32).reshape(slab, columns).T
    out[chunks * rp :, :] = rows[: out.shape[0] - chunks * rp].astype(bf16)


def unpack_kernel(shards, rp, where, *refs):
    pieces, (wt_o, gains_o, router_o, rows_o) = (refs[: 2 * shards - 1], refs[2 * shards - 1 :])
    slab = pieces[0].shape[1]
    first = shards * rp
    experts = router_o.shape[0]
    for z in range(shards):

        @pl.when(where[0] == z)
        def _():
            for p in range(shards):
                piece = pieces[p - z + shards - 1]
                columns = slice(p * slab, (p + 1) * slab)
                wt_o[:, columns] = piece[first : first + QKV]
                gains_o[:, columns] = piece[first + QKV : first + QKV + 2].astype(f32)
                router_o[:, columns] = piece[first + QKV + 2 : first + QKV + 2 + experts]
                for j in range(shards):
                    rows_o[p, :, j * slab : (j + 1) * slab] = piece[j * rp : (j + 1) * rp]


def code_kernel(first, table, out, load):
    i = pl.program_id(0)
    tok, experts = out.shape[1:]

    @pl.when(i == 0)
    def _():
        load[...] = jnp.zeros_like(load)

    rows = table[0, first : first + TOP + 1, :tok].astype(f32)
    names = lax.broadcasted_iota(i32, (experts, tok), 0).astype(f32)
    named = jnp.zeros((experts, tok), f32)
    for k in range(TOP):
        named += jnp.where(rows[k : k + 1] == names, 1.0, 0.0)
    ranks = jnp.broadcast_to(rows[TOP : TOP + 1], (tok, tok))
    before = jnp.where(ranks.T < ranks, 1.0, 0.0).astype(bf16)
    slot = dot_nn(named.astype(bf16), before) + load[:, :1]
    out[0] = (named * (1.0 + jnp.where(slot < CAP, 1.0, 0.0))).T
    load[...] += jnp.sum(named, axis=1, keepdims=True)


def qkv_kernel(
    far, slot_ref, xa, xaf, xb, xbf, gain, wt, cos, sin, ain_o, qt_o, k_o, kt_o, v_o, vt_o
):
    i = pl.program_id(0)
    flags = (near(slot_ref, 0, i, far), near(slot_ref, 1, i, far))
    x = pick(flags, (xa, xaf, xb, xbf)).astype(f32)
    inv = lax.rsqrt(jnp.mean(x * x, axis=-1, keepdims=True) + EPS)
    a = (x * inv * gain[...]).astype(bf16)
    ain_o[0] = a
    y = dot_nt(wt[...], a)
    c, s = (cos[0], sin[0])

    def turn(rows):
        lo, hi = (rows[:HALF], rows[HALF:])
        return jnp.concatenate([lo * c - hi * s, hi * c + lo * s], axis=0)

    for h in range(GROUP):
        q = turn(y[h * HD : (h + 1) * HD]).astype(bf16).astype(f32) * SCORE_SCALE
        qt_o[0, h * HD : (h + 1) * HD, :] = q.astype(bf16)
    k = turn(y[QW : QW + HD])
    kt_o[0] = k.astype(bf16)
    k_o[0] = k.T.astype(bf16)
    v = y[QW + HD :]
    vt_o[0] = v.astype(bf16)
    v_o[0] = v.T.astype(bf16)


def heads_wide(rows):
    return jnp.concatenate([rows[h * HD : (h + 1) * HD] for h in range(GROUP)], axis=1)


def causal(shape, width):
    key = lax.broadcasted_iota(i32, shape, 0)
    query = lax.broadcasted_iota(i32, shape, 1)
    for _ in range(GROUP - 1):
        query = jnp.where(query >= width, query - width, query)
    return key <= query


def attn_fwd_kernel(qt, k, vt, of_o, ob_o, lse_o):
    a = pl.program_id(0)
    tok = qt.shape[2]
    q = heads_wide(qt[0])
    s = dot_nn(k[a], q)
    s = jnp.where(causal(s.shape, tok), s, NEG_FILL)
    m = jnp.max(s, axis=0, keepdims=True)
    p = jnp.exp(s - m)
    l = jnp.sum(p, axis=0, keepdims=True)
    o = dot_nn(vt[a], p.astype(bf16))

    def step(b, carry):
        m, l, o = carry
        s = dot_nn(k[b], q)
        new = jnp.maximum(m, jnp.max(s, axis=0, keepdims=True))
        p = jnp.exp(s - new)
        back = jnp.exp(m - new)
        l = l * back + jnp.sum(p, axis=0, keepdims=True)
        o = o * back + dot_nn(vt[b], p.astype(bf16))
        return (new, l, o)

    m, l, o = lax.fori_loop(0, a, step, (m, l, o))
    o = o / l
    lse_o[0] = m + jnp.log(l)
    for h in range(GROUP):
        part = o[:, h * tok : (h + 1) * tok]
        of_o[0, h * HD : (h + 1) * HD, :] = part
        ob_o[0, h * HD : (h + 1) * HD, :] = part.astype(bf16)


def attn_bwd_kernel(qt, dot_, of, lse, k, kt, v, cos, sin, dq_o, dk_o, dv_o, dk_s, dv_s):
    a = pl.program_id(0)
    tok = qt.shape[2]
    count = k.shape[0]
    q = heads_wide(qt[0])
    do = heads_wide(dot_[0])
    delta = jnp.sum(do.astype(f32) * heads_wide(of[0]), axis=0, keepdims=True)
    total = lse[0]

    def pair(b, mask):
        s = dot_nn(k[b], q)
        p = jnp.exp(s - total)
        if mask:
            p = jnp.where(causal(s.shape, tok), p, 0.0)
        dp = dot_nn(v[b], do)
        ds = (p * (dp - delta)).astype(bf16)
        return dot_nt(ds, q), dot_nt(p.astype(bf16), do), dot_nn(kt[b], ds)

    dk, dv, dq = pair(a, True)
    dk_s[a] = dk
    dv_s[a] = dv

    def step(b, dq):
        dk, dv, more = pair(b, False)
        dk_s[b] += dk
        dv_s[b] += dv
        return dq + more

    dq = lax.fori_loop(0, a, step, dq) * SCORE_SCALE

    def back(rows, c, s):
        lo, hi = (rows[:HALF], rows[HALF:])
        return jnp.concatenate([lo * c + hi * s, hi * c - lo * s], axis=0)

    for h in range(GROUP):
        dq_o[0, h * HD : (h + 1) * HD, :] = back(
            dq[:, h * tok : (h + 1) * tok], cos[a], sin[a]
        ).astype(bf16)

    @pl.when(a == count - 1)
    def _():
        @pl.loop(0, count)
        def _(b):
            dk_o[b] = back(dk_s[b].T, cos[b], sin[b]).astype(bf16)
            dv_o[b] = dv_s[b].T.astype(bf16)


def qkv_grads_kernel(share, dq, dk, dv, ain, wt, gain, gw_o, gg_o, acc):
    i = pl.program_id(0)
    d = jnp.concatenate([dq[0], dk[0], dv[0]], axis=0)

    @pl.when(i == 0)
    def _():
        acc[...] = jnp.zeros_like(acc)

    acc[...] += dot_nn(d, ain[0])

    @pl.when(i == pl.num_programs(0) - 1)
    def _():
        width = gw_o.shape[2]
        for z in range(gw_o.shape[0]):
            gw_o[z] = acc[:, z * width : (z + 1) * width].astype(bf16)
        total = jnp.sum(acc[...] * wt[...].astype(f32), axis=0, keepdims=True)
        gg_o[...] = total * share / gain[...]


def qkv_back_kernel(share, far, blocks_ref, dqa, dka, dva, dqb, dkb, dvb, wt, *outs):
    i = pl.program_id(0)
    flags = (i < far, i < far)
    d = jnp.concatenate(
        [
            jnp.concatenate([dqa[0], dka[0], dva[0]], axis=0),
            jnp.concatenate([dqb[0], dkb[0], dvb[0]], axis=0),
        ],
        axis=1,
    )
    put(flags, outs, (dot_tn(d, wt[...]) * share).astype(bf16))


def bundle_kernel(gw, gain_a, gain_f, router, p0, p1, q0, q1, out):
    shards, rows, slab = out.shape
    half, rp, _ = p0.shape
    first = shards * rp
    small = jnp.concatenate([gain_a[...], gain_f[...], router[...]], axis=0).astype(bf16)
    count = small.shape[0]
    for z in range(shards):
        near, got = (p0, p1) if z < half else (q0, q1)
        w_out = add_up(near[z % half], got[z % half])
        for j in range(shards):
            out[z, j * rp : (j + 1) * rp, :] = w_out[:, j * slab : (j + 1) * slab]
        out[z, first : first + QKV, :] = gw[z]
        out[z, first + QKV : first + QKV + count, :] = small[:, z * slab : (z + 1) * slab]
        rest = first + QKV + count
        if rest < rows:
            out[z, rest:, :] = jnp.zeros((rows - rest, slab), bf16)


def share_kernel(own, send, w_out_o):
    count, rp, columns = send.shape
    shards = w_out_o.shape[1] // own.shape[1]
    slab = own.shape[1]
    first = shards * rp
    for j in range(shards):
        w_out_o[:, j * slab : (j + 1) * slab] = own[j * rp : (j + 1) * rp, :].astype(f32)
    rows = own[first:, :].astype(f32)
    rows = jnp.concatenate([rows, jnp.zeros((columns - rows.shape[0], slab), f32)], axis=0)
    send[...] = rows.T.reshape(count, rp, columns).astype(bf16)


def finish_kernel(copies, given, query, key, value, sums):
    count = given.shape[0]
    parts = [given[c].astype(f32) for c in range(count)]
    for c in range(0, count, copies):
        g = c // copies
        query[:, g * QW : (g + 1) * QW] = parts[c][:, :QW]
        key[:, g * HD : (g + 1) * HD] = parts[c][:, QW : QW + HD]
        value[:, g * HD : (g + 1) * HD] = parts[c][:, QW + HD : QKV]
    total = parts[0][:, QKV:]
    for part in parts[1:]:
        total = total + part[:, QKV:]
    sums[...] = total.T[: sums.shape[0]]


def expert_terms(expert, x, y, router, code, w_gate, w_up, w_down):
    logits = dot_nt(x, router)
    named = code > 0.5
    logits = jnp.where(named, logits, NEG_FILL)
    top = jnp.max(logits, axis=-1, keepdims=True)
    raised = jnp.where(named, jnp.exp(logits - top), 0.0)
    gates = raised / jnp.sum(raised, axis=-1, keepdims=True)
    mine = (lax.broadcasted_iota(i32, gates.shape, 1) == expert) & (code > 1.5)
    weight = RESIDUAL_SCALE * jnp.sum(jnp.where(mine, gates, 0.0), axis=-1, keepdims=True)
    kept = RESIDUAL_SCALE * jnp.sum(jnp.where(mine, 1.0, 0.0), axis=-1, keepdims=True)

    gate_pre = dot_nn(x, w_gate)
    up_pre = dot_nn(x, w_up)
    back = dot_nn(y, w_down)
    sig = jax.nn.sigmoid(gate_pre)
    act = gate_pre * sig
    inner = act * up_pre
    gate_grad = kept * jnp.sum(inner * back, axis=-1, keepdims=True)
    inner_w = (inner * weight).astype(bf16)
    d_inner = back * weight
    d_gate = (d_inner * up_pre * sig * (1.0 + gate_pre * (1.0 - sig))).astype(bf16)
    d_up = (d_inner * act).astype(bf16)
    din = dot_nt(d_gate, w_gate) + dot_nt(d_up, w_up)
    high = gate_grad.astype(bf16).astype(f32)
    low = (gate_grad - high).astype(bf16).astype(f32)
    lane = lax.broadcasted_iota(i32, (x.shape[0], EXTRA), 1)
    side = jnp.where(lane == expert, high, 0.0) + jnp.where(lane == expert + LOW, low, 0.0)
    return inner_w, d_gate, d_up, jnp.concatenate([din, side], axis=1)


def weight_of(weights, which):
    shards, _, depth, ff = weights.shape
    return weights[:, which].reshape(shards * depth, ff)


def clear(accs, i):
    @pl.when(i == 0)
    def _():
        for acc in accs:
            acc[...] = jnp.zeros_like(acc)


def flush(accs, grad_o, i):
    @pl.when(i == pl.num_programs(0) - 1)
    def _():
        shards, _, depth, _ = grad_o.shape
        for which, acc in enumerate(accs):
            for z in range(shards):
                grad_o[z, which] = acc[z * depth : (z + 1) * depth, :].astype(bf16)


def moe_first_kernel(far, which, blocks, *refs):
    xs, ys, (router, code_a, code_b, weights) = (refs[:4], refs[4:8], refs[8:12])
    outs, (b_o, grad_o), accs = (refs[12:16], refs[16:18], refs[18:])
    i = pl.program_id(0)
    flags = (i < far, i < far)
    x, y = (pick(flags, xs), pick(flags, ys))
    code = jnp.concatenate([code_a[0], code_b[0]], axis=0)
    inner_w, d_gate, d_up, din = expert_terms(
        which[0], x, y, router[...], code, *[weight_of(weights, m) for m in range(3)]
    )
    put(flags, outs, din.astype(bf16))
    b_o[0] = inner_w
    clear(accs, i)
    accs[0][...] += dot_tn(x, d_gate)
    accs[1][...] += dot_tn(x, d_up)
    accs[2][...] += dot_tn(y, inner_w)
    flush(accs, grad_o, i)


def moe_second_kernel(far, which, blocks, *refs):
    xs, ys, (router, code_a, code_b, weights) = (refs[:4], refs[4:8], refs[8:12])
    prev, outs, (b_o, dg_o, du_o) = (refs[12:16], refs[16:20], refs[20:])
    i = pl.program_id(0)
    flags = (i < far, i < far)
    x, y = (pick(flags, xs), pick(flags, ys))
    code = jnp.concatenate([code_a[0], code_b[0]], axis=0)
    inner_w, d_gate, d_up, din = expert_terms(
        which[0], x, y, router[...], code, *[weight_of(weights, m) for m in range(3)]
    )
    put(flags, outs, (din + pick(flags, prev).astype(f32)).astype(bf16))
    b_o[0] = inner_w
    dg_o[0] = d_gate
    du_o[0] = d_up


def moe_grads_kernel(far, *refs):
    xs, ys, (b, dg, du), grad_o, accs = (refs[:4], refs[4:8], refs[8:11], refs[11], refs[12:])
    i = pl.program_id(0)
    flags = (i < far, i < far)
    x, y = (pick(flags, xs), pick(flags, ys))
    clear(accs, i)
    accs[0][...] += dot_tn(x, dg[0])
    accs[1][...] += dot_tn(x, du[0])
    accs[2][...] += dot_tn(y, b[0])
    flush(accs, grad_o, i)


def moe_out_kernel(far, b0, b1, w0, w1, *outs):
    i = pl.program_id(0)
    flags = (i < far, i < far)
    out = dot_nt(b0[0], weight_of(w0, 0)) + dot_nt(b1[0], weight_of(w1, 0))
    put(flags, outs, out.astype(bf16))


def place_kernel(far, slot_ref, a, af, b, bf, out):
    i = pl.program_id(0)
    flags = (near(slot_ref, 0, i, far), near(slot_ref, 1, i, far))
    half = a.shape[1]
    for z in range(half):
        out[z, 0] = lax.select(flags[0], a[0, z], af[0, z])
        out[half + z, 0] = lax.select(flags[1], b[0, z], bf[0, z])


def after_attn_kernel(attn, w_out, hidden, gain, resid_o, ma_o, mb_o):
    resid = hidden[...].astype(f32) + RESIDUAL_SCALE * dot_tn(attn[...], w_out[...])
    resid_o[...] = resid
    inv = lax.rsqrt(jnp.mean(resid * resid, axis=-1, keepdims=True) + EPS)
    moe_in = (resid * inv * gain[...]).astype(bf16)
    half = ma_o.shape[1]
    ma_o[0] = moe_in[:half]
    mb_o[0] = moe_in[half:]


def before_attn_kernel(
    a0, a1, b0, b1, resid, ma, mb, grad_out, code, router, gain, w_out,
    d_resid_o, d_branch_o, d_attn_o, d_router_o, d_gain_o,
):
    width = resid.shape[1]
    experts = router.shape[0]
    back = jnp.concatenate(
        [
            a0[...].astype(f32) + a1[...].astype(f32),
            b0[...].astype(f32) + b1[...].astype(f32),
        ],
        axis=0,
    )
    moe_in = jnp.concatenate([ma[0], mb[0]], axis=0)
    chosen = code[...] > 0.5
    logits = jnp.where(chosen, dot_nt(moe_in, router[...]), NEG_FILL)
    raised = jnp.where(chosen, jnp.exp(logits - jnp.max(logits, axis=-1, keepdims=True)), 0.0)
    gates = raised / jnp.sum(raised, axis=-1, keepdims=True)
    gate_grad = (
        back[:, width : width + experts] + back[:, width + LOW : width + LOW + experts]
    )
    logit_grad = gates * (gate_grad - jnp.sum(gates * gate_grad, axis=-1, keepdims=True))
    dlogits = logit_grad.astype(bf16)
    d_router_o[...] = dot_tn(dlogits, moe_in)
    d_moe_in = back[:, :width] + dot_nn(dlogits, router[...])
    r = resid[...]
    inv = lax.rsqrt(jnp.mean(r * r, axis=-1, keepdims=True) + EPS)
    normed = r * inv
    d_gain_o[...] = jnp.sum(d_moe_in * normed, axis=0, keepdims=True)
    d_normed = d_moe_in * gain[...]
    d_resid = grad_out[...].astype(f32) + inv * (
        d_normed - normed * jnp.mean(d_normed * normed, axis=-1, keepdims=True)
    )
    d_resid_o[...] = d_resid
    d_branch = (RESIDUAL_SCALE * d_resid).astype(bf16)
    d_branch_o[...] = d_branch
    d_attn_o[...] = dot_nt(w_out[...], d_branch).astype(bf16)


def wout_grad_kernel(far, slot_ref, attn, d_branch, a, af, b, bf):
    n2, half, rp, width = a.shape
    n = 2 * n2
    d = d_branch[...]
    for z in range(2 * half):
        rows = dot_nn(attn[z * n * rp : (z + 1) * n * rp, :], d).astype(bf16)
        lane = 0 if z < half else 1
        near_o, far_o = ((a, af), (b, bf))[lane]
        for c in range(n):
            part = rows[c * rp : (c + 1) * rp]
            slot = slot_ref[lane, c]

            @pl.when(slot < far)
            def _():
                near_o[slot, z % half] = part

            @pl.when(slot >= far)
            def _():
                far_o[slot - far, z % half] = part


def last_kernel(a0, a1, b0, b1, d_resid, hidden, gain, out):
    d = jnp.concatenate(
        [
            a0[...].astype(f32) + a1[...].astype(f32),
            b0[...].astype(f32) + b1[...].astype(f32),
        ],
        axis=0,
    )
    x = hidden[...].astype(f32)
    inv = lax.rsqrt(jnp.mean(x * x, axis=-1, keepdims=True) + EPS)
    normed = x * inv
    d = d * gain[...]
    out[...] = d_resid[...] + inv * (
        d - normed * jnp.mean(d * normed, axis=-1, keepdims=True)
    )


def whole(shape):
    zeros = (0,) * len(shape)
    return pl.BlockSpec(shape, lambda *at: zeros)


def at_step(shape):
    zeros = (0,) * (len(shape) - 1)
    return pl.BlockSpec(shape, lambda i, *refs: (i,) + zeros)


def lanes_at_step(shape, far):
    zeros = (0,) * (len(shape) - 1)
    first = pl.BlockSpec(shape, lambda i, *refs: (jnp.minimum(i, far - 1),) + zeros)
    second = pl.BlockSpec(shape, lambda i, *refs: (jnp.maximum(i - far, 0),) + zeros)
    return [first, second, first, second]


def lanes_at_slot(shape, far):
    zeros = (0,) * (len(shape) - 1)

    def spec(lane, second):
        def index(i, slots):
            slot = slots[lane, i]
            slot = jnp.maximum(slot - far, 0) if second else jnp.minimum(slot, far - 1)
            return (slot,) + zeros

        return pl.BlockSpec(shape, index)

    return [spec(0, False), spec(0, True), spec(1, False), spec(1, True)]


def shape_of(*dims, dtype=bf16):
    return jax.ShapeDtypeStruct(dims, dtype)


def micros(us):
    return pl.CostEstimate(
        flops=int(us * 1.1e9), bytes_accessed=int(us * 1e6), transcendentals=0
    )


def call(kernel, name, us, out_shape, operands, *, grid=None, specs=None, out_specs=None,
         scratch=(), tables=(), limit=58):
    if grid is None:
        specs = [whole(x.shape) for x in operands]
        out_specs = jax.tree.map(lambda x: whole(x.shape), out_shape)
        grid = 1
    return pl.pallas_call(
        kernel,
        grid_spec=pltpu.PrefetchScalarGridSpec(
            num_scalar_prefetch=len(tables),
            grid=(grid,),
            in_specs=specs,
            out_specs=out_specs,
            scratch_shapes=list(scratch),
        ),
        out_shape=out_shape,
        compiler_params=params(limit * 1024 * 1024),
        cost_estimate=micros(us),
        name=name,
    )(*tables, *operands)


def shards(
    hidden,
    gain_attn,
    w_query,
    w_key,
    w_value,
    w_out,
    gain_ffn,
    router,
    routes,
    slot_order,
    w_gate,
    w_up,
    w_down,
    grad_out,
):
    tok, width = hidden.shape
    n = lax.axis_size("ctx")
    dp = lax.axis_size("dp")
    me = lax.axis_index("ctx")
    copies = n // KV
    far = n // 2
    rp = w_query.shape[0]
    slab = rp * n
    experts = router.shape[1]
    half = tok // 2
    ff = w_gate.shape[2]
    depth = w_gate.shape[1]
    orders = lane_orders(n)
    slots = [slots_of(order) for order in orders]
    blocks = jnp.array(slots, i32) ^ me
    inverse = jnp.array([[lane.index(j) for j in range(n)] for lane in slots], i32)
    slot_at = jnp.take(inverse, jnp.arange(n, dtype=i32) ^ me, axis=1)


    side = QKV + 2 + experts
    pad = -(side + rp * dp) % 16
    send = call(
        prep_kernel,
        "prep",
        2,
        shape_of(n, rp + 16, max(slab, tok, -(-side // 128) * 128)),
        [
            w_query,
            w_key,
            w_value,
            gain_attn[None],
            gain_ffn[None],
            router.T,
            routes.T,
            slot_order,
        ],
        limit=58,
    )
    took = lax.all_to_all(send, "ctx", split_axis=0, concat_axis=0, tiled=True)
    pack = call(
        pack_kernel,
        "pack",
        2,
        shape_of(side + rp * dp, slab),
        [took, w_out],
        limit=58,
    )

    def along(value, by):
        pairs = [(z, z + by) for z in range(dp) if 0 <= z + by < dp]
        return lax.ppermute(value, "dp", pairs)

    below, above = ([], [])
    for _ in range(dp - 1):
        below.append(along(below[-1] if below else pack, 1))
        above.append(along(above[-1] if above else pack, -1))
    wt, gains, router_t, out_rows = call(
        functools.partial(unpack_kernel, dp, rp),
        "unpack",
        2,
        [
            shape_of(QKV, width),
            shape_of(2, width, dtype=f32),
            shape_of(experts, width),
            shape_of(dp, rp, width),
        ],
        [*below[::-1], pack, *above],
        grid=1,
        specs=[whole(pack.shape)] * (2 * dp - 1),
        out_specs=[
            whole((QKV, width)),
            whole((2, width)),
            whole((experts, width)),
            whole((dp, rp, width)),
        ],
        tables=[lax.axis_index("dp").reshape(1).astype(i32)],
        limit=58,
    )
    gain_a, gain_f = (gains[0:1], gains[1:2])

    stacks = [jnp.stack([w_gate[e], w_up[e], w_down[e]]) for e in range(w_gate.shape[0])]
    stacks = after(stacks, below[:-1], above[:-1])
    expert_w = [lax.all_gather(stack, "dp", axis=0) for stack in stacks]

    x_rows = after(hidden, took)
    x_rows = Gather(x_rows[:half], x_rows[half:], n)
    xs = x_rows.run()
    y_rows = after(grad_out, x_rows.have)
    y_rows = Gather(y_rows[:half], y_rows[half:], n)

    exponents = jnp.arange(HALF, dtype=f32) * (2.0 / HD)
    inverse_freq = jnp.power(10000.0, -exponents)
    positions = jnp.arange(n * tok, dtype=f32).reshape(n, 1, tok)
    angles = positions * inverse_freq[None, :, None]
    cos, sin = (jnp.cos(angles), jnp.sin(angles))

    o_rows = Gather(out_rows[: dp // 2], out_rows[dp // 2 :], n)
    gain_a, y_rows.got = after((gain_a, y_rows.got))

    ain, qt, k, kt, v, vt = call(
        functools.partial(qkv_kernel, far),
        "qkv",
        6,
        [
            shape_of(n, tok, width),
            shape_of(n, QW, tok),
            shape_of(n, tok, HD),
            shape_of(n, HD, tok),
            shape_of(n, tok, HD),
            shape_of(n, HD, tok),
        ],
        [*xs, gain_a, wt, cos, sin],
        grid=n,
        specs=lanes_at_slot((1, half, width), far)
        + [whole((1, width)), whole((QKV, width))]
        + [at_step((1, HALF, tok))] * 2,
        out_specs=[
            at_step((1, tok, width)),
            at_step((1, QW, tok)),
            at_step((1, tok, HD)),
            at_step((1, HD, tok)),
            at_step((1, tok, HD)),
            at_step((1, HD, tok)),
        ],
        tables=[slot_at],
        limit=58,
    )

    qt, y_rows.have, y_rows.got, o_rows.have, o_rows.got = after(
        (qt, y_rows.have, y_rows.got, o_rows.have, o_rows.got)
    )
    y_rows.step()
    o_rows.step()
    qt = after(qt, y_rows.have, o_rows.have)
    of, attn_t, lse = call(
        attn_fwd_kernel,
        "attn_fwd",
        19,
        [
            shape_of(n, QW, tok, dtype=f32),
            shape_of(n, QW, tok),
            shape_of(n, 1, GROUP * tok, dtype=f32),
        ],
        [qt, k, vt],
        grid=n,
        specs=[at_step((1, QW, tok)), whole((n, tok, HD)), whole((n, HD, tok))],
        out_specs=[at_step((1, QW, tok))] * 2 + [at_step((1, 1, GROUP * tok))],
        limit=58,
    )

    attn_t, y_rows.got, o_rows.got = after((attn_t, y_rows.got, o_rows.got))
    os = o_rows.run()
    ys = y_rows.run()
    attn_b = lax.all_to_all(attn_t, "ctx", split_axis=0, concat_axis=0, tiled=True)
    attn_b = attn_b[::copies].reshape(KV * QW, tok)

    w_out_all = call(
        functools.partial(place_kernel, far),
        "place",
        4,
        shape_of(dp, n, rp, width),
        os,
        grid=n,
        specs=lanes_at_slot((1, dp // 2, rp, width), far),
        out_specs=pl.BlockSpec((dp, 1, rp, width), lambda i, slots: (0, i, 0, 0)),
        tables=[slot_at],
        limit=58,
    ).reshape(KV * QW, width)

    resid, ma, mb = call(
        after_attn_kernel,
        "after_attn",
        6,
        [shape_of(tok, width, dtype=f32)] + [shape_of(1, half, width)] * 2,
        [attn_b, w_out_all, hidden, gain_f],
        limit=58,
    )
    m_rows = Gather(ma[0], mb[0], n)
    took = after(took, ma)

    code = call(
        functools.partial(code_kernel, rp),
        "code",
        6,
        shape_of(n, tok, experts, dtype=f32),
        [took],
        grid=n,
        specs=[at_step((1,) + took.shape[1:])],
        out_specs=at_step((1, tok, experts)),
        scratch=[pltpu.VMEM((experts, 1), f32)],
        limit=58,
    )
    code_mine = lax.dynamic_index_in_dim(code, me, 0, keepdims=False)

    m_rows.got, code, code_mine = after((m_rows.got, code, code_mine))
    ms = m_rows.run()

    side_w = width + EXTRA
    wide = [shape_of(far, half, side_w)] * 4
    rows_in = lanes_at_step((1, half, width), far) * 2 + [
        whole((experts, width)),
        *[
            pl.BlockSpec((1, half, experts), lambda i, which, blocks, lane=lane: (blocks[lane, i], lane, 0))
            for lane in range(2)
        ],
        whole((dp, 3, depth, ff)),
    ]
    hidden_o = [at_step((1, tok, ff))]
    hidden_s = [shape_of(n, tok, ff)]
    accs = [pltpu.VMEM((width, ff), f32)] * 3
    first = (me * len(expert_w)).reshape(1).astype(i32)
    *din, inner_0, grads_0 = call(
        functools.partial(moe_first_kernel, far),
        "moe_first",
        38,
        wide + hidden_s + [shape_of(dp, 3, depth, ff)],
        [*ms, *ys, router_t, code, code, expert_w[0]],
        grid=n,
        specs=rows_in,
        out_specs=lanes_at_step((1, half, side_w), far) + hidden_o + [whole((dp, 3, depth, ff))],
        scratch=accs,
        tables=[first, blocks],
        limit=58,
    )
    *din, inner_1, d_gate_1, d_up_1 = call(
        functools.partial(moe_second_kernel, far),
        "moe_second",
        25,
        wide + hidden_s * 3,
        [*ms, *ys, router_t, code, code, expert_w[1], *din],
        grid=n,
        specs=rows_in + lanes_at_step((1, half, side_w), far),
        out_specs=lanes_at_step((1, half, side_w), far) + hidden_o * 3,
        tables=[first + 1, blocks],
        limit=58,
    )
    back = Scatter(din, n)
    back.step()
    inner_1 = after(inner_1, back.keep)
    grads_1 = call(
        functools.partial(moe_grads_kernel, far),
        "moe_grads",
        15,
        shape_of(dp, 3, depth, ff),
        [*ms, *ys, inner_1, d_gate_1, d_up_1],
        grid=n,
        specs=lanes_at_step((1, half, width), far) * 2 + hidden_o * 3,
        out_specs=whole((dp, 3, depth, ff)),
        scratch=accs,
        limit=58,
    )
    expert_grads = [
        lax.psum_scatter(grads, "dp", scatter_dimension=0, tiled=True)
        for grads in (grads_0, grads_1)
    ]

    back.got = after(back.got, grads_1)
    (a0, a1), (b0, b1) = back.run()
    inner_1 = after(inner_1, back.keep)
    down = pl.BlockSpec((dp, 1, depth, ff), lambda i: (0, 2, 0, 0))
    outs = call(
        functools.partial(moe_out_kernel, far),
        "moe_out",
        8,
        [shape_of(far, half, width)] * 4,
        [inner_0, inner_1, *expert_w],
        grid=n,
        specs=hidden_o * 2 + [down] * 2,
        out_specs=lanes_at_step((1, half, width), far),
        limit=40,
    )
    mix = Scatter(outs, n)
    resid_in = after(resid, outs)
    d_resid, d_branch, d_attn, d_router, d_gain_ffn = call(
        before_attn_kernel,
        "before_attn",
        14,
        [
            shape_of(tok, width, dtype=f32),
            shape_of(tok, width),
            shape_of(KV * QW, tok),
            shape_of(experts, width, dtype=f32),
            shape_of(1, width, dtype=f32),
        ],
        [a0, a1, b0, b1, resid_in, ma, mb, grad_out, code_mine, router_t, gain_f, w_out_all],
        limit=58,
    )
    d_heads = lax.all_to_all(
        jnp.repeat(d_attn.reshape(KV, QW, tok), copies, axis=0),
        "ctx",
        split_axis=0,
        concat_axis=0,
        tiled=True,
    )
    d_wout = call(
        functools.partial(wout_grad_kernel, far),
        "wout_grad",
        6,
        [shape_of(far, dp // 2, rp, width)] * 4,
        [attn_b, d_branch],
        grid=1,
        specs=[whole((KV * QW, tok)), whole((tok, width))],
        out_specs=[whole((far, dp // 2, rp, width))] * 4,
        tables=[slot_at],
        limit=58,
    )

    mix.fold()
    mix.send, mix.keep, d_heads, expert_grads[0] = after(
        (mix.send, mix.keep, d_heads, expert_grads[0])
    )
    mix.start()
    wout = Scatter(after(d_wout, d_heads), n)
    dq, dk, dv = call(
        attn_bwd_kernel,
        "attn_bwd",
        40,
        [shape_of(n, QW, tok), shape_of(n, HD, tok), shape_of(n, HD, tok)],
        [qt, d_heads, of, lse, k, kt, v, cos, sin],
        grid=n,
        specs=[
            at_step((1, QW, tok)),
            at_step((1, QW, tok)),
            at_step((1, QW, tok)),
            at_step((1, 1, GROUP * tok)),
            whole((n, tok, HD)),
            whole((n, HD, tok)),
            whole((n, tok, HD)),
            whole((n, HALF, tok)),
            whole((n, HALF, tok)),
        ],
        out_specs=[at_step((1, QW, tok)), whole((n, HD, tok)), whole((n, HD, tok))],
        scratch=[pltpu.VMEM((n, tok, HD), f32), pltpu.VMEM((n, tok, HD), f32)],
        limit=40,
    )

    dq, wout.keep, wout.got = after((dq, wout.keep, wout.got))
    wout.step()
    dq = after(dq, wout.keep)

    gw, d_gain_attn = call(
        functools.partial(qkv_grads_kernel, 1.0 / copies),
        "qkv_grads",
        20,
        [shape_of(dp, QKV, slab), shape_of(1, width, dtype=f32)],
        [dq, dk, dv, ain, wt, gain_a],
        grid=n,
        specs=[
            at_step((1, QW, tok)),
            at_step((1, HD, tok)),
            at_step((1, HD, tok)),
            at_step((1, tok, width)),
            whole((QKV, width)),
            whole((1, width)),
        ],
        out_specs=[whole((dp, QKV, slab)), whole((1, width))],
        scratch=[pltpu.VMEM((QKV, width), f32)],
        limit=30,
    )

    def columns(rows, lane):
        return pl.BlockSpec((1, rows, half), lambda i, blocks: (blocks[lane, i], 0, lane))

    dq, wout.keep, wout.got, mix.keep, mix.got = after(
        (dq, wout.keep, wout.got, mix.keep, mix.got), gw
    )
    wout.step()
    dq = after(dq, wout.keep)
    d_in = call(
        functools.partial(qkv_back_kernel, 1.0 / copies, far),
        "qkv_back",
        20,
        [shape_of(far, half, width)] * 4,
        [dq, dk, dv, dq, dk, dv, wt],
        grid=n,
        specs=[columns(rows, lane) for lane in range(2) for rows in (QW, HD, HD)]
        + [whole((QKV, width))],
        out_specs=lanes_at_step((1, half, width), far),
        tables=[blocks],
        limit=30,
    )

    wout.got = after(wout.got, d_in)
    (p0, p1), (q0, q1) = wout.run()
    bundle = call(
        bundle_kernel,
        "bundle",
        2,
        shape_of(dp, side + rp * dp + pad, slab),
        [gw, d_gain_attn, d_gain_ffn, d_router, p0, p1, q0, q1],
        limit=30,
    )
    own = lax.psum_scatter(bundle, "dp", scatter_dimension=0, tiled=True)[0]
    send, grad_out_proj = call(
        share_kernel,
        "share",
        2,
        [shape_of(n, rp, -(-(side + pad) // 128) * 128), shape_of(rp, width, dtype=f32)],
        [own],
        limit=30,
    )
    given = lax.all_to_all(send, "ctx", split_axis=0, concat_axis=0, tiled=True)
    grad_query, grad_key, grad_value, sums = call(
        functools.partial(finish_kernel, copies),
        "finish",
        2,
        [
            shape_of(rp, KV * QW, dtype=f32),
            shape_of(rp, KV * HD, dtype=f32),
            shape_of(rp, KV * HD, dtype=f32),
            shape_of(2 + experts, rp, dtype=f32),
        ],
        [given],
        limit=30,
    )

    back_in = Scatter(after(d_in, bundle), n)
    mix.keep, mix.got = after((mix.keep, mix.got), bundle)
    mix.step()
    back_in.got = after(back_in.got, mix.keep)
    back_in.step()
    expert_grads, mix.got = after((expert_grads, mix.got), back_in.keep)
    (c0, c1), (e0, e1) = back_in.run()
    d_hidden = call(
        last_kernel,
        "last",
        3,
        shape_of(tok, width, dtype=f32),
        [c0, c1, e0, e1, after(d_resid, send), hidden, gain_a],
        limit=30,
    )

    (r0, r1), (s0, s1) = mix.run()
    mixed = jnp.concatenate(
        [r0.astype(f32) + r1.astype(f32), s0.astype(f32) + s1.astype(f32)], axis=0
    )
    output = (resid + mixed).astype(bf16)

    expert_grads = jnp.concatenate(expert_grads, axis=0).astype(f32)
    return (
        output,
        d_hidden,
        sums[0],
        grad_query,
        grad_key,
        grad_value,
        grad_out_proj,
        sums[1],
        sums[2:].T,
        expert_grads[:, 0],
        expert_grads[:, 1],
        expert_grads[:, 2],
    )


def solution(mesh):
    rows = P(("dp", "ctx"), None)
    flat = P(("dp", "ctx"))
    expert = P("ctx", "dp", None)
    return jax.shard_map(
        shards,
        mesh=mesh,
        in_specs=(
            rows,
            flat,
            rows,
            rows,
            rows,
            rows,
            flat,
            rows,
            rows,
            rows,
            expert,
            expert,
            expert,
            rows,
        ),
        out_specs=(
            rows,
            rows,
            flat,
            rows,
            rows,
            rows,
            rows,
            flat,
            rows,
            expert,
            expert,
            expert,
        ),
        check_vma=False,
    )
```
